32 devices in a mesh: dp: 8 (over y, x, core), seq: 4 (over z).
Axes of the slice: x: 2, y: 2, z: 4, core: 2. Of those that a mesh axis runs over, the one named last changes fastest.
Arguments:
- inputs: bfloat16 [24, 1024, 768], P('dp', 'seq'), may hold values from -6 to 6
- cotangent: bfloat16 [24, 1024, 768], P('dp', 'seq'), may hold values from -6 to 6
- lengths: int32 [24], P('dp'), may hold values from 100 to 1024, as said below
- predicted: int32 [24, 1024], P('dp', 'seq'), may hold values from 0 to 69
- norm1_gain: float32 [768], replicated, may hold values from 0.1 to 1.9
- norm1_shift: float32 [768], replicated, may hold values from -4 to 4
- w_query: bfloat16 [768, 768], replicated, may hold values from -0.3125 to 0.3125
- b_query: float32 [768], replicated, may hold values from -6 to 6
- w_key: bfloat16 [768, 768], replicated, may hold values from -0.3125 to 0.3125
- b_key: float32 [768], replicated, may hold values from -6 to 6
- w_value: bfloat16 [768, 768], replicated, may hold values from -0.21875 to 0.21875
- b_value: float32 [768], replicated, may hold values from -6 to 6
- w_out: bfloat16 [768, 768], replicated, may hold values from -2 to 2
- b_out: float32 [768], replicated, may hold values from -6 to 6
- norm2_gain: float32 [768], replicated, may hold values from 0.1 to 1.9
- norm2_shift: float32 [768], replicated, may hold values from -4 to 4
- w_up: bfloat16 [768, 3072], replicated, may hold values from -0.21875 to 0.21875
- b_up: float32 [3072], replicated, may hold values from -6 to 6
- w_down: bfloat16 [3072, 768], replicated, may hold values from -0.109375 to 0.109375
- b_down: float32 [768], replicated, may hold values from -6 to 6
Outputs:
- result: bfloat16 [24, 1024, 768], P('dp', 'seq')
- grad_inputs: bfloat16 [24, 1024, 768], P('dp', 'seq')
- grad_norm1_gain: float32 [768], replicated
- grad_norm1_shift: float32 [768], replicated
- grad_w_query: float32 [768, 768], replicated
- grad_b_query: float32 [768], replicated
- grad_w_key: float32 [768, 768], replicated
- grad_b_key: float32 [768], replicated
- grad_w_value: float32 [768, 768], replicated
- grad_b_value: float32 [768], replicated
- grad_w_out: float32 [768, 768], replicated
- grad_b_out: float32 [768], replicated
- grad_norm2_gain: float32 [768], replicated
- grad_norm2_shift: float32 [768], replicated
- grad_w_up: float32 [768, 3072], replicated
- grad_b_up: float32 [3072], replicated
- grad_w_down: float32 [3072, 768], replicated
- grad_b_down: float32 [768], replicated
- histogram: int32 [70], replicated
The draws below stay inside these ranges and needn't reach their ends.
Inputs may be any that keep to these rules, and one draw needn't show every extreme that they name: Some sequence has 1024 real codons and some has 100; the codons from position lengths[s] on are padding.
All inputs are finite; a program needn't handle non-finite values.
Results may differ from the reference program's by a relative error of at most 0.014.
The reference program's roundings to bfloat16 on the way count: a program that leaves them out, or rounds other values in their place, can miss the bound.
Values may be sent and summed in bfloat16 or wider, within the bound.
No kernel may reach another device: no remote copies, remote signals or barrier semaphores. Data moves between devices by JAX's collectives and lax.ppermute only.
A program may use at most 192 MiB of HBM per device.

```python
import math
import jax
import jax.numpy as jnp
from jax import lax

D = 768
HEADS = 12
HEAD = 64
FF = 3072
CLASSES = 70
LEN = 1024
MINLEN = 100
SEQS = 24


def draw_lengths(key, part):
    base = jax.random.randint(key, (SEQS,), 0, 1000)
    spread = (LEN - MINLEN) * (base * base // 1000) * base // 1000000
    lengths = MINLEN + spread
    lengths = lengths.at[0].set(LEN).at[1].set(MINLEN)
    return lengths.astype(jnp.int32)


def set_ends(values, rng, low, high):
    index_at = [jax.random.randint(jax.random.fold_in(rng, axis), (), 0, length) for axis, length in enumerate(values.shape)]
    widest = values.shape.index(max(values.shape))
    next_to = index_at[:widest] + [(index_at[widest] + 1) % values.shape[widest]] + index_at[widest + 1:]
    return values.at[tuple(index_at)].set(low).at[tuple(next_to)].set(high)


def level_of(rng, extent, split, low, top_value):
    level, own = 1.0, jax.random.fold_in(rng, 6)
    for axis_at, shards_of in split:
        draws = jnp.exp(jax.random.uniform(jax.random.fold_in(own, axis_at), (shards_of,), jnp.float32, low / len(split), top_value / len(split)))
        level = level * jnp.repeat(draws, extent[axis_at] // shards_of).reshape([-1 if axis == axis_at else 1 for axis in range(len(extent))])
    return level


def noise(own_key, shape, scale, limit, pieces=(), kind=jnp.bfloat16):
    drawn = jax.random.normal(own_key, shape, jnp.float32) * scale
    if len(pieces) > 0:
        drawn = level_of(own_key, shape, pieces, -0.22, 0.18) * drawn
    return jnp.clip(drawn, min=-limit, max=limit).astype(kind)


def setup_inputs(seed: int = 0) -> dict:
    seeds = jax.random.split(jax.random.key(seed), 21)
    return {
        "inputs": noise(seeds[0], (SEQS, LEN, D), 1.0, 6.0, ((0, 8), (1, 4))),
        "cotangent": noise(seeds[1], (SEQS, LEN, D), 1.0, 6.0, ((0, 8), (1, 4))),
        "lengths": draw_lengths(jax.random.fold_in(seeds[20], 71), 0),
        "predicted": set_ends(jax.random.randint(seeds[3], (SEQS, LEN), 0, CLASSES), jax.random.fold_in(seeds[3], 1), 0, CLASSES - 1).astype(jnp.int32),
        "norm1_gain": jnp.clip(1.0 + 0.18 * jax.random.normal(seeds[4], (D,), jnp.float32), 0.1, 1.9),
        "norm1_shift": noise(seeds[5], (D,), 0.3, 4.0, (), jnp.float32),
        "w_query": noise(seeds[6], (D, D), (D // 2) ** -0.5, 0.3125),
        "b_query": noise(seeds[7], (D,), 0.5, 6.0, (), jnp.float32),
        "w_key": noise(seeds[8], (D, D), (D // 2) ** -0.5, 0.3125),
        "b_key": noise(seeds[9], (D,), 0.5, 6.0, (), jnp.float32),
        "w_value": noise(seeds[10], (D, D), D ** -0.5, 0.21875),
        "b_value": noise(seeds[11], (D,), 0.5, 6.0, (), jnp.float32),
        "w_out": noise(seeds[12], (D, D), (max(D // 96, 1)) ** -0.5, 2.0),
        "b_out": noise(seeds[13], (D,), 0.5, 6.0, (), jnp.float32),
        "norm2_gain": jnp.clip(1.0 + 0.18 * jax.random.normal(seeds[14], (D,), jnp.float32), 0.1, 1.9),
        "norm2_shift": noise(seeds[15], (D,), 0.3, 4.0, (), jnp.float32),
        "w_up": noise(seeds[16], (D, FF), D ** -0.5, 0.21875),
        "b_up": noise(seeds[17], (FF,), 0.5, 6.0, (), jnp.float32),
        "w_down": noise(seeds[18], (FF, D), FF ** -0.5, 0.109375),
        "b_down": noise(seeds[19], (D,), 0.5, 6.0, (), jnp.float32),
    }


epsilon = 1e-05
highest = lax.Precision.HIGHEST

@jax.custom_vjp
def low(v):
    return lax.optimization_barrier(v.astype(jnp.bfloat16)).astype(jnp.float32)

@jax.custom_vjp
def low_back(v):
    return v

def low_keep(v):
    return (low(v), None)

def low_pass(kept, grad):
    return (grad,)

def back_keep(v):
    return (v, None)

def back_low(kept, grad):
    return (low(grad),)
low.defvjp(low_keep, low_pass)
low_back.defvjp(back_keep, back_low)

def matmul(left, right):
    return jnp.dot(left, right, precision=highest, preferred_element_type=jnp.float32)

def layer_norm(value, gain, shift):
    centre = value - lax.optimization_barrier(jnp.mean(value, axis=-1, keepdims=True))
    scale = lax.rsqrt(lax.optimization_barrier(jnp.mean(centre * centre, axis=-1, keepdims=True)) + epsilon)
    return centre * scale * gain + shift

def gelu(value):
    return jax.nn.gelu(value, approximate=False)

def rotate(value, direction):
    count = value.shape[-3]
    half = value.shape[-1] // 2
    frequency = 10000.0 ** (-jnp.arange(half, dtype=jnp.float32) / half)
    angle = jnp.arange(count, dtype=jnp.float32)[:, None] * frequency[None, :]
    cosine = jnp.cos(angle)[:, None, :]
    sine = direction * jnp.sin(angle)[:, None, :]
    first = value[..., :half]
    second = value[..., half:]
    return jnp.concatenate([first * cosine - second * sine, second * cosine + first * sine], axis=-1)

def attend_block(query_block, key, value, valid):
    scores = jnp.einsum('qhd,khd->hqk', query_block, key, precision=highest) * HEAD ** (-0.5)
    scores = jnp.where(valid[None, None, :], low_back(scores), -1e+30)
    weights = low(jax.nn.softmax(scores, axis=-1))
    return jnp.einsum('hqk,khd->qhd', weights, value, precision=highest)

def attend_sequence(query, key, value, valid):
    block = min(LEN, 512)
    blocks = query.reshape(LEN // block, block, HEADS, HEAD)
    visit_block = jax.checkpoint(lambda query_block: attend_block(query_block, key, value, valid))
    mixed = lax.map(visit_block, blocks)
    return mixed.reshape(LEN, HEADS * HEAD)

def forward(params, inputs, lengths):
    norm1_gain, norm1_shift, w_query, b_query, w_key, b_key, w_value, b_value, w_out, b_out, norm2_gain, norm2_shift, w_up, b_up, w_down, b_down = params
    group = inputs.shape[0]
    flat_in = inputs.reshape(group * LEN, D)
    normed = low(layer_norm(flat_in, norm1_gain, norm1_shift))

    def project(weight, bias):
        return low(low_back(matmul(normed, weight) + bias)).reshape(group, LEN, HEADS, HEAD)
    query = low(rotate(project(w_query, b_query), 1.0))
    key = low(rotate(project(w_key, b_key), 1.0))
    value = project(w_value, b_value)
    valid = jnp.arange(LEN)[None, :] < lengths[:, None]
    mixed = jax.vmap(attend_sequence)(query, key, value, valid)
    attended = low(low_back(mixed)).reshape(group * LEN, D)
    middle = flat_in + low_back(matmul(attended, w_out)) + b_out
    normed2 = low(layer_norm(middle, norm2_gain, norm2_shift))
    hidden_in = low_back(matmul(normed2, w_up) + b_up)
    hidden = low(gelu(hidden_in))
    result = middle + matmul(hidden, w_down) + b_down
    return result.reshape(group, LEN, D)

def reference(inputs, cotangent, lengths, predicted, norm1_gain, norm1_shift, w_query, b_query, w_key, b_key, w_value, b_value, w_out, b_out, norm2_gain, norm2_shift, w_up, b_up, w_down, b_down):
    params = tuple((item.astype(jnp.float32) for item in (norm1_gain, norm1_shift, w_query, b_query, w_key, b_key, w_value, b_value, w_out, b_out, norm2_gain, norm2_shift, w_up, b_up, w_down, b_down)))
    group = math.gcd(SEQS, max(1, 4096 // LEN))
    turns = SEQS // group
    items = (inputs.reshape(turns, group, LEN, D), cotangent.reshape(turns, group, LEN, D), lengths.reshape(turns, group))
    zeros = jax.tree.map(jnp.zeros_like, params)

    def visit(carry, item):
        span_in, span_cot, span_len = item
        outputs, pullback = jax.vjp(lambda weights, values: forward(weights, values, span_len), params, span_in.astype(jnp.float32))
        grad_params, grad_in = pullback(span_cot.astype(jnp.float32))
        carry = jax.tree.map(jnp.add, carry, grad_params)
        return (carry, (outputs.astype(jnp.bfloat16), grad_in.astype(jnp.bfloat16)))
    grads, (outputs, grad_in) = lax.scan(visit, zeros, items)
    valid = jnp.arange(LEN)[None, :] < lengths[:, None]
    classes = jnp.arange(CLASSES).astype(jnp.int32)
    histogram = lax.optimization_barrier(jnp.sum(jnp.where(valid[:, :, None] & (predicted[:, :, None] == classes), 1, 0), axis=(0, 1))).astype(jnp.int32)
    return (outputs.reshape(SEQS, LEN, D), grad_in.reshape(SEQS, LEN, D), grads[0], grads[1], grads[2], grads[3], grads[4], grads[5], grads[6], grads[7], grads[8], grads[9], grads[10], grads[11], grads[12], grads[13], grads[14], grads[15], histogram)
```

```python
import functools

import jax
import jax.numpy as jnp
from jax import lax
from jax.experimental import pallas as pl
from jax.experimental.pallas import tpu as pltpu
from jax.sharding import PartitionSpec as P

HEAD = 64
CLASSES = 70
PAIR = 2 * HEAD
BLOCK = 256

epsilon = 1e-05
low = jnp.bfloat16
full = jnp.float32


def matmul(left, right):
    return lax.dot_general(
        left, right, (((1,), (0,)), ((), ())), preferred_element_type=full
    )


def matmul_left(left, right):
    return lax.dot_general(
        left, right, (((0,), (0,)), ((), ())), preferred_element_type=full
    )


def matmul_right(left, right):
    return lax.dot_general(
        left, right, (((1,), (1,)), ((), ())), preferred_element_type=full
    )


def whiten(value):
    centre = value - jnp.mean(value, axis=-1, keepdims=True)
    scale = lax.rsqrt(jnp.mean(centre * centre, axis=-1, keepdims=True) + epsilon)
    return centre * scale, scale


def whiten_back(grad, hat, scale):
    mean = jnp.mean(grad, axis=-1, keepdims=True)
    along = jnp.mean(grad * hat, axis=-1, keepdims=True)
    return scale * (grad - mean - hat * along)


def rotate(value, cosine, sine):
    lane = lax.broadcasted_iota(jnp.int32, value.shape, 1)
    ahead = pltpu.roll(value, PAIR - HEAD // 2, 1)
    behind = pltpu.roll(value, HEAD // 2, 1)
    swapped = jnp.where(lane % HEAD < HEAD // 2, ahead, behind)
    return value * cosine + swapped * sine


def call(kernel, grid, scalars, inputs, outputs, scratch=(), flops=0, special=0):
    moved = sum(array.size * array.dtype.itemsize for array, _ in inputs)
    moved += sum(shape.size * shape.dtype.itemsize for shape, _ in outputs)
    return pl.pallas_call(
        kernel,
        grid_spec=pltpu.PrefetchScalarGridSpec(
            num_scalar_prefetch=1,
            grid=grid,
            in_specs=[spec for _, spec in inputs],
            out_specs=[spec for _, spec in outputs],
            scratch_shapes=list(scratch),
        ),
        out_shape=[shape for shape, _ in outputs],
        compiler_params=pltpu.CompilerParams(
            dimension_semantics=("arbitrary",) * len(grid), vmem_limit_bytes=60 << 20
        ),
        cost_estimate=pl.CostEstimate(
            flops=int(flops), transcendentals=int(special), bytes_accessed=int(moved)
        ),
    )(scalars, *[array for array, _ in inputs])


def whole(array):
    rank = len(array.shape)
    return (array, pl.BlockSpec(array.shape, lambda *_: (0,) * rank))


def fresh(shape, kind):
    return jax.ShapeDtypeStruct(shape, kind)


def pack_kernel(order, first, second, to_first, to_second):
    to_first[...] = first[...]
    to_second[...] = second[...]


def pack(array, order):
    seqs, span, width = array.shape
    half = span // 2
    blocks = array.reshape(2 * seqs, half, width)
    shape = fresh((seqs * half, width), array.dtype)
    spot = pl.BlockSpec((half, width), lambda j, order: (j, 0))
    return call(
        pack_kernel,
        (seqs,),
        order,
        [
            (blocks, pl.BlockSpec((None, half, width), lambda j, order: (order[j], 0, 0))),
            (blocks, pl.BlockSpec((None, half, width), lambda j, order: (order[seqs + j], 0, 0))),
        ],
        [(shape, spot), (shape, spot)],
    )


def unpack_kernel(order, first, second, out):
    take = order[pl.program_id(0)] == 0

    @pl.when(take)
    def _():
        out[...] = first[...]

    @pl.when(jnp.logical_not(take))
    def _():
        out[...] = second[...]


def unpack(first, second, order, seqs):
    rows, width = first.shape
    half = rows // seqs
    spot = pl.BlockSpec((half, width), lambda i, order: (order[2 * seqs + i], 0))
    blocks = call(
        unpack_kernel,
        (2 * seqs,),
        order,
        [(first, spot), (second, spot)],
        [
            (
                fresh((2 * seqs, half, width), first.dtype),
                pl.BlockSpec((None, half, width), lambda i, order: (i, 0, 0)),
            )
        ],
    )[0]
    return blocks.reshape(seqs, 2 * half, width)


def join(first, second, span):
    return jnp.concatenate(
        [first[:span], second[:span], first[span:], second[span:]], axis=0
    )


def project_kernel(
    place, first, second, gain, shift, w_query, w_key, w_value, b_query, b_key, b_value,
    cosine, sine, query, both, shared, normed,
):
    width = first.shape[1]
    span = 2 * first.shape[0] // 3
    half = span // 2
    for slot, message in enumerate((first, second)):
        own = slice(slot * span, (slot + 1) * span)
        mixed = slice(2 * span + slot * half, 2 * span + (slot + 1) * half)
        hat, _ = whiten(message[...].astype(full))
        item = (hat * gain[...] + shift[...]).astype(low)
        normed[own, :] = item[:span]
        normed[mixed, :] = item[span:]
        at = pl.ds(pl.multiple_of(place[slot], half), span)
        at_mixed = pl.ds(pl.multiple_of(place[2 + slot], half), half)
        cos = jnp.concatenate([cosine[at, :], cosine[at_mixed, :]], axis=0)
        sin = jnp.concatenate([sine[at, :], sine[at_mixed, :]], axis=0)
        raw = (matmul(item, w_query[...]) + b_query[...]).astype(low).astype(full)
        for column in range(0, width, PAIR):
            spot = slice(column, column + PAIR)
            turned = rotate(raw[:, spot], cos, sin).astype(low) * low(HEAD**-0.5)
            query[own, spot] = turned[:span]
            query[mixed, spot] = turned[span:]
        raw = (matmul(item, w_key[...]) + b_key[...]).astype(low).astype(full)
        for column in range(0, width, PAIR):
            spot = slice(column, column + PAIR)
            turned = rotate(raw[:, spot], cos, sin).astype(low)
            both[0, own, spot] = turned[:span]
            both[0, mixed, spot] = turned[span:]
            shared[0, slot * half : (slot + 1) * half, spot] = turned[span:]
        raw = (matmul(item, w_value[...]) + b_value[...]).astype(low)
        both[1, own, :] = raw[:span]
        both[1, mixed, :] = raw[span:]
        shared[1, slot * half : (slot + 1) * half, :] = raw[span:]


def load_pieces(place, pieces, keys, values):
    for index, piece in enumerate(pieces):
        rows = piece.shape[1] // 2
        for slot in range(2):
            at = pl.ds(pl.multiple_of(place[1 + 2 * index + slot], rows), rows)
            keys[at, :] = piece[0, slot * rows : (slot + 1) * rows, :]
            values[at, :] = piece[1, slot * rows : (slot + 1) * rows, :]


def head_masks(value):
    lane = lax.broadcasted_iota(jnp.int32, value.shape, 1)
    wide = value.astype(full)
    return (
        jnp.where(lane < HEAD, wide, 0.0).astype(low),
        jnp.where(lane < HEAD, 0.0, wide).astype(low),
    )


def attend_kernel(count, place, query, *refs):
    pieces = refs[:count]
    out, logsum, keys, values = refs[count:]
    load_pieces(place, pieces, keys, values)
    length = place[0]
    masked = head_masks(query[...])
    rows = query.shape[0]

    def visit(block, state, left=None):
        at = pl.ds(pl.multiple_of(block * BLOCK, BLOCK), BLOCK)
        key = keys[at, :]
        value = values[at, :].T
        fresh_state = []
        for head in range(2):
            peak, total, mixed = state[3 * head : 3 * head + 3]
            scores = matmul_right(key, masked[head])
            if left is not None:
                index = lax.broadcasted_iota(jnp.int32, scores.shape, 0)
                scores = jnp.where(index < left, scores, -1e30)
            top = jnp.maximum(peak, jnp.max(scores, axis=0, keepdims=True))
            weights = jnp.exp(scores - top)
            fade = jnp.exp(peak - top)
            total = total * fade + jnp.sum(weights, axis=0, keepdims=True)
            mixed = mixed * fade + matmul(
                value[head * HEAD : (head + 1) * HEAD, :], weights.astype(low)
            )
            fresh_state += [top, total, mixed]
        return tuple(fresh_state)

    start = (
        jnp.full((1, rows), -1e30, full),
        jnp.zeros((1, rows), full),
        jnp.zeros((HEAD, rows), full),
    )
    number = length // BLOCK
    state = lax.fori_loop(0, number, visit, start + start)
    state = lax.cond(
        length % BLOCK > 0,
        lambda given: visit(number, given, length % BLOCK),
        lambda given: given,
        state,
    )
    out[...] = (
        jnp.concatenate([state[2] / state[1], state[5] / state[4]], axis=0).T.astype(low)
    )
    logsum[0:1, :] = state[0] + jnp.log(state[1])
    logsum[1:2, :] = state[3] + jnp.log(state[4])


def attend_back_kernel(count, kept, place, query, grad, mixed, logsum, cosine, sine, *refs):
    pieces = refs[:count]
    grad_query, *grad_pieces = refs[count : 1 + 2 * count]
    keys, values, grad_keys, grad_values, grad_turned = refs[1 + 2 * count :]
    load_pieces(place, pieces, keys, values)
    length = place[0]
    grad_low = grad[...]
    masked = head_masks(query[...])
    masked_grad = head_masks(grad_low)
    inner = (grad_low.astype(full) * mixed[...].astype(full)).T
    delta = [
        jnp.sum(inner[head * HEAD : (head + 1) * HEAD, :], axis=0, keepdims=True)
        for head in range(2)
    ]
    grad_turned[...] = jnp.zeros_like(grad_turned)

    def visit(block, left=None):
        at = pl.ds(pl.multiple_of(block * BLOCK, BLOCK), BLOCK)
        key = keys[at, :]
        value = values[at, :]
        turned = key.T
        grad_key = jnp.zeros((BLOCK, PAIR), full)
        grad_value = jnp.zeros((BLOCK, PAIR), full)
        for head in range(2):
            spot = slice(head * HEAD, (head + 1) * HEAD)
            scores = matmul_right(key, masked[head])
            weights = jnp.exp(scores - logsum[head : head + 1, :])
            if left is not None:
                index = lax.broadcasted_iota(jnp.int32, scores.shape, 0)
                weights = jnp.where(index < left, weights, 0.0)
            grad_weights = matmul_right(value, masked_grad[head])
            grad_scores = (weights * (grad_weights - delta[head])).astype(low)
            grad_value += matmul(weights.astype(low), masked_grad[head])
            grad_key += matmul(grad_scores, masked[head])
            grad_turned[spot, :] += matmul(turned[spot, :], grad_scores)
        grad_keys[at, :] = rotate(grad_key, cosine[at, :], -sine[at, :]).astype(low)
        grad_values[at, :] = grad_value.astype(low)

    def visit_whole(block, carry):
        visit(block)
        return carry

    def clear(block, carry):
        at = pl.ds(pl.multiple_of(block * BLOCK, BLOCK), BLOCK)
        grad_keys[at, :] = jnp.zeros((BLOCK, PAIR), low)
        grad_values[at, :] = jnp.zeros((BLOCK, PAIR), low)
        return carry

    number = length // BLOCK
    lax.fori_loop(0, number, visit_whole, 0)

    @pl.when(length % BLOCK > 0)
    def _():
        visit(number, length % BLOCK)

    lax.fori_loop(pl.cdiv(length, BLOCK), keys.shape[0] // BLOCK, clear, 0)
    rows = query.shape[0]
    step = rows // 2
    back = grad_turned[...].T * HEAD**-0.5
    for slot in range(2):
        at = pl.ds(pl.multiple_of(place[1 + 2 * count + slot], step), step)
        part = slice(slot * step, (slot + 1) * step)
        grad_query[part, :] = rotate(back[part], cosine[at, :], -sine[at, :]).astype(low)
    for index, piece in enumerate(grad_pieces):
        rows = piece.shape[1] // 2
        for slot in range(2):
            at = pl.ds(pl.multiple_of(place[1 + 2 * index + slot], rows), rows)
            piece[0, slot * rows : (slot + 1) * rows, :] = grad_keys[at, :]
            piece[1, slot * rows : (slot + 1) * rows, :] = grad_values[at, :]


def hidden_tile(normed, cot, w_up, b_up, w_down, result, grad_normed, hidden, grad_hidden):
    count = normed.shape[0]
    step = min(count, 256)
    total = jnp.zeros((1, w_up.shape[1]), full)
    for row in range(0, count, step):
        spot = slice(row, row + step)
        hidden_in = matmul(normed[spot, :], w_up[...]) + b_up[...]
        back = matmul_right(cot[spot, :], w_down[...])
        share = 0.5 * (1.0 + lax.erf(hidden_in * 0.5**0.5))
        item = (hidden_in * share).astype(low)
        slope = share + hidden_in * jnp.exp(-0.5 * hidden_in * hidden_in) * 0.3989422804014327
        grad_item = (back * slope).astype(low)
        hidden[spot, :] = item
        grad_hidden[spot, :] = grad_item
        total += jnp.sum(grad_item.astype(full), axis=0, keepdims=True)
        result[spot, :] += matmul(item, w_down[...])
        grad_normed[spot, :] += matmul_right(grad_item, w_up[...])
    return total


def forward_kernel(
    tiles, own, mixed, first, second, cot_first, cot_second, w_out, b_out, gain, shift,
    w_up, b_up, w_down, middle, result, grad_normed, normed, cot, sent, grad_b_up,
    hidden, grad_hidden,
):
    span = 2 * first.shape[0] // 3

    @pl.when(pl.program_id(0) == 0)
    def _():
        cot[...] = join(cot_first[...], cot_second[...], span)
        attended = jnp.concatenate([own[...], mixed[...]], axis=0)
        value = join(first[...], second[...], span).astype(full)
        value = value + matmul(attended, w_out[...]) + b_out[...]
        middle[...] = value
        hat, _ = whiten(value)
        normed[...] = (hat * gain[...] + shift[...]).astype(low)
        result[...] = jnp.zeros_like(result)
        grad_normed[...] = jnp.zeros_like(grad_normed)

    grad_b_up[0:1, :] = hidden_tile(
        normed, cot, w_up, b_up, w_down, result, grad_normed, hidden, grad_hidden
    )
    sent[0, ...] = matmul_left(hidden[...], cot[...]).astype(low)
    sent[1, ...] = matmul_left(normed[...], grad_hidden[...]).astype(low)


def backward_kernel(
    tiles, own, mixed, middle, result_in, grad_normed_in, normed, cot, w_out, gain, w_up, b_up,
    w_down, b_down, kept, grad_b_up, to_first, to_second, grad_middle, grad_own, grad_mixed,
    out_kept, out_sent, rows_out, result, grad_normed, hidden, grad_hidden, grad_out,
):
    span = 2 * to_first.shape[0] // 3
    half = span // 2

    @pl.when(pl.program_id(0) == 0)
    def _():
        result[...] = result_in[...]
        grad_normed[...] = grad_normed_in[...]

    grad_b_up[0:1, :] = hidden_tile(
        normed, cot, w_up, b_up, w_down, result, grad_normed, hidden, grad_hidden
    )
    kept[0, ...] = matmul_left(hidden[...], cot[...]).astype(low)
    kept[1, ...] = matmul_left(normed[...], grad_hidden[...]).astype(low)

    @pl.when(pl.program_id(0) == pl.num_programs(0) - 1)
    def _():
        value = middle[...]
        done = (value + result[...] + b_down[...]).astype(low)
        to_first[:span, :] = done[:span]
        to_second[:span, :] = done[span : 2 * span]
        to_first[span:, :] = done[2 * span : 2 * span + half]
        to_second[span:, :] = done[2 * span + half :]
        hat, scale = whiten(value)
        grad = grad_normed[...]
        cot_full = cot[...].astype(full)
        rows_out[0:1, :] = jnp.sum(cot_full, axis=0, keepdims=True)
        rows_out[2:3, :] = jnp.sum(grad * hat, axis=0, keepdims=True)
        rows_out[3:4, :] = jnp.sum(grad, axis=0, keepdims=True)
        total = cot_full + whiten_back(grad * gain[...], hat, scale)
        rows_out[1:2, :] = jnp.sum(total, axis=0, keepdims=True)
        rows_out[4:8, :] = jnp.zeros_like(rows_out[4:8, :])
        grad_middle[...] = total
        branch = total.astype(low)
        back = matmul_right(branch, w_out[...]).astype(low)
        grad_own[...] = back[: 2 * span]
        grad_mixed[...] = back[2 * span :]
        attended = jnp.concatenate([own[...], mixed[...]], axis=0)
        grad_out[...] = matmul_left(attended, branch).astype(low)
        size = out_kept.shape[0]
        core = tiles[2]
        out_kept[...] = grad_out[pl.ds(pl.multiple_of(core * size, size), size), :]
        out_sent[...] = grad_out[pl.ds(pl.multiple_of((1 - core) * size, size), size), :]


def weight_kernel(
    core, normed, query_own, query_mixed, own_kept, own_sent, mixed_kept, mixed_sent,
    kept, sent, both, rows_out, whole_grad,
):
    grad_query = jnp.concatenate([query_own[...], query_mixed[...]], axis=0)
    parts = [grad_query]
    for index in range(2):
        own = own_kept[index].astype(full) + own_sent[index].astype(full)
        mixed = mixed_kept[index].astype(full) + mixed_sent[index].astype(full)
        part = jnp.concatenate([own, mixed], axis=0).astype(low)
        both[index] = part
        parts.append(part)
    size = kept.shape[1]
    for index, part in enumerate(parts):
        rows_out[index : index + 1, :] = jnp.sum(part.astype(full), axis=0, keepdims=True)
        whole_grad[...] = matmul_left(normed[...], part).astype(low)
        kept[index] = whole_grad[pl.ds(pl.multiple_of(core[0] * size, size), size), :]
        sent[index] = whole_grad[pl.ds(pl.multiple_of((1 - core[0]) * size, size), size), :]
    rows_out[3:8, :] = jnp.zeros_like(rows_out[3:8, :])


def input_kernel(
    core, query_own, query_mixed, both, w_query, w_key, w_value, first, second, gain,
    grad_middle, to_first, to_second, rows_out,
):
    span = 2 * first.shape[0] // 3
    half = span // 2
    grad_query = jnp.concatenate([query_own[...], query_mixed[...]], axis=0)
    grad = (
        matmul_right(grad_query, w_query[...])
        + matmul_right(both[0], w_key[...])
        + matmul_right(both[1], w_value[...])
    )
    hat, scale = whiten(join(first[...], second[...], span).astype(full))
    rows_out[0:1, :] = jnp.sum(grad * hat, axis=0, keepdims=True)
    rows_out[1:2, :] = jnp.sum(grad, axis=0, keepdims=True)
    rows_out[2:8, :] = jnp.zeros_like(rows_out[2:8, :])
    done = (grad_middle[...] + whiten_back(grad * gain[...], hat, scale)).astype(low)
    to_first[:span, :] = done[:span]
    to_second[:span, :] = done[span : 2 * span]
    to_first[span:, :] = done[2 * span : 2 * span + half]
    to_second[span:, :] = done[2 * span + half :]


def expand_kernel(halves, order, *refs):
    sources = refs[:4]
    outs = refs[4:]
    index = pl.program_id(0)
    for place, out in enumerate(outs):
        core = index // halves
        half = index % halves if halves > 1 else place
        choice = 2 * (core ^ order[0]) + (half ^ order[1])
        for number, source in enumerate(sources):

            @pl.when(choice == number)
            def _(source=source, out=out):
                out[...] = source[...].astype(full)


def on_device(
    inputs, cotangent, lengths, predicted, norm1_gain, norm1_shift, w_query, b_query, w_key,
    b_key, w_value, b_value, w_out, b_out, norm2_gain, norm2_shift, w_up, b_up, w_down, b_down,
):
    seqs, span, width = inputs.shape
    half = span // 2
    tokens = seqs * span
    hidden_width = w_up.shape[1]
    groups = lax.axis_size("dp")
    assert seqs == 3 and lax.axis_size("seq") == 4 and hidden_width == 4 * width
    bits = [1 << place for place in range(1, groups.bit_length() - 1)]
    group = lax.axis_index("dp")
    depth = lax.axis_index("seq")
    core = group & 1
    side = depth & 1
    pair = depth >> 1
    count = 4 * span

    def flip(value, bit):
        return lax.ppermute(value, "dp", [(i, i ^ bit) for i in range(groups)])

    def flip_depth(value, bit):
        return lax.ppermute(value, "seq", [(i, i ^ bit) for i in range(4)])

    def route(turn):
        moves = []
        for at in range(groups):
            for z in range(4):
                to = (at & ~1) | (z & 1)
                to_z = 2 * (at & 1) + (turn ^ (z >> 1))
                moves.append((at * 4 + z, to * 4 + to_z))
        return moves

    def send(value, turn):
        return lax.ppermute(value, ("dp", "seq"), route(turn))

    def send_back(value, turn):
        return lax.ppermute(value, ("dp", "seq"), [(b, a) for a, b in route(turn)])

    def ranks(sizes):
        longest = jnp.argmax(sizes).astype(jnp.int32)
        return (
            jnp.where(longest == 0, 1, 0),
            jnp.where(longest == 2, 1, 2),
            longest,
        )

    low_own, high_own, mixed_at = ranks(lengths)
    near = jnp.where(pair == 0, low_own, high_own)
    other = jnp.where(pair == 0, high_own, low_own)
    index = jnp.arange(2 * seqs)
    turn = index // seqs
    spot = index % seqs
    chosen = jnp.where(turn == 0, near, other)
    order = jnp.where(spot < 2, 2 * chosen + spot, 2 * mixed_at + (turn ^ pair))
    first, second = pack(inputs, order)
    first, second = send(first, 0), send(second, 1)
    seq_at = index // 2
    part = index % 2
    from_turn = jnp.where(seq_at == mixed_at, part, (seq_at == high_own).astype(jnp.int32)) ^ pair
    from_row = jnp.where(seq_at == mixed_at, 2, part)
    order_back = jnp.concatenate([from_turn, from_row])

    sibling_lengths = flip(lengths, 1)
    sizes = jnp.where(core == pair, lengths, sibling_lengths)
    low_here, high_here, mixed_here = ranks(sizes)
    own_length = sizes[jnp.where(side == 0, low_here, high_here)]
    mixed_length = sizes[mixed_here]

    def starts(at_side, at_core):
        slots = jnp.arange(2)
        quarter = 2 * (slots ^ at_side) + at_core
        return quarter * span, quarter * span + at_side * half

    own_at, mixed_start = starts(side, core)
    own_sibling, mixed_sibling = starts(side, 1 - core)
    _, mixed_far = starts(1 - side, core)
    _, mixed_far_sibling = starts(1 - side, 1 - core)
    own_place = jnp.concatenate([own_length[None], own_at, own_sibling, own_at])
    mixed_place = jnp.concatenate(
        [mixed_length[None], mixed_start, mixed_sibling, mixed_far, mixed_far_sibling, mixed_start]
    )

    frequency = 10000.0 ** (-jnp.arange(HEAD // 2, dtype=full) / (HEAD // 2))
    angle = jnp.arange(count, dtype=full)[:, None] * frequency[None, :]
    cosine = jnp.tile(jnp.cos(angle), (1, 4))
    sine = jnp.sin(angle)
    sine = jnp.tile(jnp.concatenate([-sine, sine], axis=1), (1, 2))

    def row(vector):
        return vector.reshape(1, -1)

    gain1, shift1 = row(norm1_gain), row(norm1_shift)
    gain2, shift2 = row(norm2_gain), row(norm2_shift)

    query, both, shared, normed = call(
        project_kernel,
        (1,),
        jnp.concatenate([own_at, mixed_start]),
        [
            whole(item)
            for item in (
                first, second, gain1, shift1, w_query, w_key, w_value, row(b_query), row(b_key),
                row(b_value), cosine, sine,
            )
        ],
        [
            whole(fresh((tokens, width), low)),
            whole(fresh((2, tokens, width), low)),
            whole(fresh((2, span, width), low)),
            whole(fresh((tokens, width), low)),
        ],
        flops=6 * tokens * width * width,
    )
    both_sibling = flip(both, 1)
    shared_far = flip_depth(shared, 1)
    shared_far_sibling = flip(shared_far, 1)

    cot_in, _, _ = lax.optimization_barrier((cotangent, first, second))
    cot_first, cot_second = pack(cot_in, order)
    cot_first, cot_second = send(cot_first, 0), send(cot_second, 1)

    pairs = width // PAIR

    def columns(array, rows, at):
        if len(array.shape) == 2:
            return (array, pl.BlockSpec((rows, PAIR), lambda h, _: (at, h)))
        return (array, pl.BlockSpec((2, rows, PAIR), lambda h, _: (0, at, h)))

    own_pieces = [columns(both, 2 * span, 0), columns(both_sibling, 2 * span, 0)]
    mixed_pieces = [
        columns(both, span, 2),
        columns(both_sibling, span, 2),
        columns(shared_far, span, 0),
        columns(shared_far_sibling, span, 0),
    ]

    def attend(place, rows, at, pieces):
        return call(
            functools.partial(attend_kernel, len(pieces)),
            (pairs,),
            place,
            [columns(query, rows, at), *pieces],
            [
                columns(fresh((rows, width), low), rows, 0),
                (
                    fresh((pairs, 8, rows), full),
                    pl.BlockSpec((None, 8, rows), lambda h, _: (h, 0, 0)),
                ),
            ],
            [pltpu.VMEM((count, PAIR), low), pltpu.VMEM((count, PAIR), low)],
            flops=4 * rows * count * width,
            special=rows * count * width // HEAD,
        )

    own, own_logsum = attend(own_place, 2 * span, 0, own_pieces)
    mixed, mixed_logsum = attend(mixed_place, span, 2, mixed_pieces)

    tiles_sent = jnp.stack([2 * (1 - core), 2 * (1 - core) + 1, core])
    tiles_kept = jnp.stack([2 * core, 2 * core + 1, core])
    square = (width, width)

    def tiled():
        return [
            (w_up, pl.BlockSpec(square, lambda j, tiles: (0, tiles[j]))),
            (row(b_up), pl.BlockSpec((1, width), lambda j, tiles: (0, tiles[j]))),
            (w_down, pl.BlockSpec(square, lambda j, tiles: (tiles[j], 0))),
        ]

    def tile_outs():
        return [
            (
                fresh((2, 2, width, width), low),
                pl.BlockSpec((2, None, width, width), lambda j, tiles: (0, j, 0, 0)),
            ),
            (
                fresh((2, 8, width), full),
                pl.BlockSpec((None, 8, width), lambda j, tiles: (j, 0, 0)),
            ),
        ]

    tile_scratch = [pltpu.VMEM((tokens, width), low), pltpu.VMEM((tokens, width), low)]
    middle, result, grad_normed2, normed2, cot, up_sent, b_up_sent = call(
        forward_kernel,
        (2,),
        tiles_sent,
        [
            whole(item)
            for item in (
                own, mixed, first, second, cot_first, cot_second, w_out, row(b_out), gain2, shift2,
            )
        ]
        + tiled(),
        [
            whole(fresh((tokens, width), full)),
            whole(fresh((tokens, width), full)),
            whole(fresh((tokens, width), full)),
            whole(fresh((tokens, width), low)),
            whole(fresh((tokens, width), low)),
        ]
        + tile_outs(),
        tile_scratch,
        flops=26 * tokens * width * width,
        special=4 * tokens * width,
    )
    up_received = flip(up_sent, 1)
    (
        up_kept, b_up_kept, result_first, result_second, grad_middle, grad_own, grad_mixed,
        out_kept, out_sent, rows_middle,
    ) = call(
        backward_kernel,
        (2,),
        tiles_kept,
        [
            whole(item)
            for item in (
                own, mixed, middle, result, grad_normed2, normed2, cot, w_out, gain2,
            )
        ]
        + tiled()
        + [whole(row(b_down))],
        tile_outs()
        + [
            whole(fresh((tokens // 2, width), low)),
            whole(fresh((tokens // 2, width), low)),
            whole(fresh((tokens, width), full)),
            whole(fresh((2 * span, width), low)),
            whole(fresh((span, width), low)),
            whole(fresh((width // 2, width), low)),
            whole(fresh((width // 2, width), low)),
            whole(fresh((8, width), full)),
        ],
        [pltpu.VMEM((tokens, width), full), pltpu.VMEM((tokens, width), full)]
        + tile_scratch
        + [pltpu.VMEM(square, low)],
        flops=28 * tokens * width * width,
        special=4 * tokens * width,
    )
    out_received = flip(out_sent, 1)
    result = unpack(send_back(result_first, 0), send_back(result_second, 1), order_back, seqs)

    def bit_of(bit):
        return (group & bit) // bit

    def split(addends, at):
        rows = addends[0].shape[0] // 2

        def part(which):
            items = [
                lax.dynamic_slice_in_dim(item, which * rows, rows, 0).astype(full)
                for item in addends
            ]
            return sum(items[1:], items[0]).astype(low)

        return part(at), part(1 - at)

    def added(addends):
        return (addends[0].astype(full) + addends[1].astype(full)).astype(low)

    def ordered(at, mine, theirs):
        return jnp.where(
            at == 0,
            jnp.concatenate([mine, theirs], axis=0),
            jnp.concatenate([theirs, mine], axis=0),
        )

    def reduce(left, right):
        for near_bit, far_bit in zip(bits, bits[::-1]):
            keep, give = split(left, bit_of(near_bit))
            left = [keep, flip(give, near_bit)]
            keep, give = split(right, bit_of(far_bit))
            right = [keep, flip(give, far_bit)]
        left, right = added(left), added(right)
        keep = jnp.where(side == 0, left, right)
        give = jnp.where(side == 0, right, left)
        keep, give = split([keep, flip_depth(give, 1)], pair)
        return added([keep, flip_depth(give, 2)])

    def gather(piece):
        piece = ordered(pair, piece, flip_depth(piece, 2))
        far = flip_depth(piece, 1)
        left = jnp.where(side == 0, piece, far)
        right = jnp.where(side == 0, far, piece)
        for near_bit, far_bit in list(zip(bits, bits[::-1]))[:0:-1]:
            left = ordered(bit_of(near_bit), left, flip(left, near_bit))
            right = ordered(bit_of(far_bit), right, flip(right, far_bit))
        left = [left, flip(left, bits[0])]
        right = [right, flip(right, bits[-1])]
        left = left + [flip(item, 1) for item in left]
        right = right + [flip(item, 1) for item in right]
        return left, right

    def expand(sources, bit, halves, outs):
        rows, columns_in = sources[0].shape
        return call(
            functools.partial(expand_kernel, halves),
            (2 * halves,),
            jnp.stack([core, bit_of(bit)]),
            [whole(item) for item in sources],
            [
                (
                    fresh(shape, full),
                    pl.BlockSpec(
                        (rows, columns_in),
                        (lambda i, _: (i, 0)) if shape[1] == columns_in else (lambda i, _: (0, i)),
                    ),
                )
                for shape in outs
            ],
        )

    up_pieces = reduce(
        [item[0].reshape(2 * width, width) for item in (up_kept, up_received)],
        [item[1].reshape(2 * width, width) for item in (up_kept, up_received)],
    )
    down_left, up_right = gather(up_pieces)
    grad_w_down = expand(down_left, bits[0], 2, [(hidden_width, width)])[0]
    grad_w_up = expand(up_right, bits[-1], 2, [(width, hidden_width)])[0]

    def attend_back(place, rows, at, pieces, grad, out, logsum):
        return call(
            functools.partial(attend_back_kernel, len(pieces), rows // span),
            (pairs,),
            place,
            [
                columns(query, rows, at),
                columns(grad, rows, 0),
                columns(out, rows, 0),
                (logsum, pl.BlockSpec((None, 8, rows), lambda h, _: (h, 0, 0))),
                whole(cosine),
                whole(sine),
                *pieces,
            ],
            [columns(fresh((rows, width), low), rows, 0)]
            + [columns(fresh((2, rows, width), low), rows, 0) for _ in pieces],
            [
                pltpu.VMEM((count, PAIR), low),
                pltpu.VMEM((count, PAIR), low),
                pltpu.VMEM((count, PAIR), low),
                pltpu.VMEM((count, PAIR), low),
                pltpu.VMEM((PAIR, rows), full),
            ],
            flops=10 * rows * count * width,
            special=rows * count * width // HEAD,
        )

    query_mixed, mixed_here_grad, mixed_sibling_grad, far_grad, far_sibling_grad = attend_back(
        mixed_place, span, 2, mixed_pieces, grad_mixed, mixed, mixed_logsum
    )
    near_sum = added([mixed_here_grad, flip(mixed_sibling_grad, 1)])
    far_sum = added([far_grad, flip(far_sibling_grad, 1)])
    far_received = flip_depth(far_sum, 1)
    query_own, own_kept, own_sent = attend_back(
        own_place, 2 * span, 0, own_pieces, grad_own, own, own_logsum
    )
    own_received = flip(own_sent, 1)

    weight_kept, weight_sent, both_grad, rows_weight = call(
        weight_kernel,
        (1,),
        core[None],
        [
            whole(item)
            for item in (
                normed, query_own, query_mixed, own_kept, own_received, near_sum, far_received,
            )
        ],
        [
            whole(fresh((3, width // 2, width), low)),
            whole(fresh((3, width // 2, width), low)),
            whole(fresh((2, tokens, width), low)),
            whole(fresh((8, width), full)),
        ],
        [pltpu.VMEM(square, low)],
        flops=6 * tokens * width * width,
    )
    weight_received = flip(weight_sent, 1)
    back_first, back_second, rows_input = call(
        input_kernel,
        (1,),
        core[None],
        [
            whole(item)
            for item in (
                query_own, query_mixed, both_grad, w_query, w_key, w_value, first, second, gain1,
                grad_middle,
            )
        ],
        [
            whole(fresh((tokens // 2, width), low)),
            whole(fresh((tokens // 2, width), low)),
            whole(fresh((8, width), full)),
        ],
        flops=6 * tokens * width * width,
    )
    grad_inputs = unpack(send_back(back_first, 0), send_back(back_second, 1), order_back, seqs)

    left, right = gather(
        reduce(
            [item[0:2].reshape(width, width) for item in (weight_kept, weight_received)],
            [
                jnp.concatenate([item[2], extra], axis=0)
                for item, extra in ((weight_kept, out_kept), (weight_received, out_received))
            ],
        )
    )
    grad_w_query, grad_w_key = expand(left, bits[0], 1, [(width, width)] * 2)
    grad_w_value, grad_w_out = expand(right, bits[-1], 1, [(width, width)] * 2)

    live = (depth * span + jnp.arange(span))[None, :] < lengths[:, None]
    counts = jnp.sum(
        jnp.where(live[:, :, None] & (predicted[:, :, None] == jnp.arange(CLASSES)), 1.0, 0.0),
        axis=(0, 1),
    )
    counts = jnp.zeros((1, width), full).at[0, :CLASSES].set(counts)
    b_up_sent, b_up_kept = b_up_sent[:, 0], b_up_kept[:, 0]
    rows_up = jnp.where(
        core == 0,
        jnp.concatenate([b_up_kept, b_up_sent]),
        jnp.concatenate([b_up_sent, b_up_kept]),
    )
    small = jnp.concatenate(
        [rows_middle[:4], rows_up, rows_weight[:3], rows_input[:2], counts], axis=0
    )
    for bit in [1, *bits]:
        small = small + flip(small, bit)
    for bit in (1, 2):
        small = small + flip_depth(small, bit)

    return (
        result,
        grad_inputs,
        small[11],
        small[12],
        grad_w_query,
        small[8],
        grad_w_key,
        small[9],
        grad_w_value,
        small[10],
        grad_w_out,
        small[1],
        small[2],
        small[3],
        grad_w_up,
        small[4:8].reshape(-1),
        grad_w_down,
        small[0],
        small[13, :CLASSES].astype(jnp.int32),
    )


def solution(mesh):
    tokens = P("dp", "seq", None)
    return jax.shard_map(
        on_device,
        mesh=mesh,
        in_specs=(tokens, tokens, P("dp"), P("dp", "seq")) + (P(),) * 16,
        out_specs=(tokens, tokens) + (P(),) * 17,
        check_vma=False,
    )
```

```python
import functools

import jax
import jax.numpy as jnp
from jax import lax
from jax.experimental import pallas as pl
from jax.experimental.pallas import tpu as pltpu
from jax.sharding import PartitionSpec as P

HEAD = 64
CLASSES = 70
PAIR = 2 * HEAD
BLOCK = 256

epsilon = 1e-05
low = jnp.bfloat16
full = jnp.float32


def matmul(left, right):
    return lax.dot_general(
        left, right, (((1,), (0,)), ((), ())), preferred_element_type=full
    )


def matmul_left(left, right):
    return lax.dot_general(
        left, right, (((0,), (0,)), ((), ())), preferred_element_type=full
    )


def matmul_right(left, right):
    return lax.dot_general(
        left, right, (((1,), (1,)), ((), ())), preferred_element_type=full
    )


def whiten(value):
    centre = value - jnp.mean(value, axis=-1, keepdims=True)
    scale = lax.rsqrt(jnp.mean(centre * centre, axis=-1, keepdims=True) + epsilon)
    return centre * scale, scale


def whiten_back(grad, hat, scale):
    mean = jnp.mean(grad, axis=-1, keepdims=True)
    along = jnp.mean(grad * hat, axis=-1, keepdims=True)
    return scale * (grad - mean - hat * along)


def rotate(value, cosine, sine):
    lane = lax.broadcasted_iota(jnp.int32, value.shape, 1)
    ahead = pltpu.roll(value, PAIR - HEAD // 2, 1)
    behind = pltpu.roll(value, HEAD // 2, 1)
    swapped = jnp.where(lane % HEAD < HEAD // 2, ahead, behind)
    return value * cosine + swapped * sine


def call(kernel, grid, scalars, inputs, outputs, scratch=(), flops=0, special=0, room=60, aliases=None):
    moved = sum(array.size * array.dtype.itemsize for array, _ in inputs)
    moved += sum(shape.size * shape.dtype.itemsize for shape, _ in outputs)
    return pl.pallas_call(
        kernel,
        grid_spec=pltpu.PrefetchScalarGridSpec(
            num_scalar_prefetch=1,
            grid=grid,
            in_specs=[spec for _, spec in inputs],
            out_specs=[spec for _, spec in outputs],
            scratch_shapes=list(scratch),
        ),
        out_shape=[shape for shape, _ in outputs],
        input_output_aliases=aliases or {},
        compiler_params=pltpu.CompilerParams(
            dimension_semantics=("arbitrary",) * len(grid), vmem_limit_bytes=room << 20
        ),
        cost_estimate=pl.CostEstimate(
            flops=1, transcendentals=0, bytes_accessed=1
        ),
    )(scalars, *[array for array, _ in inputs])


def whole(array):
    rank = len(array.shape)
    return (array, pl.BlockSpec(array.shape, lambda *_: (0,) * rank))


def fresh(shape, kind):
    return jax.ShapeDtypeStruct(shape, kind)


def pack_kernel(order, blocks, first, second, sems):
    half = blocks.shape[1]
    copies = []
    for number, target in enumerate((first, second)):
        for place in range(target.shape[0] // half):
            at = 4 * number + place
            copies.append(
                pltpu.make_async_copy(
                    blocks.at[order[at]], target.at[pl.ds(place * half, half)], sems.at[at]
                )
            )
    for copy in copies:
        copy.start()
    for copy in copies:
        copy.wait()


def in_place(array):
    return (array, pl.BlockSpec(memory_space=pl.ANY))


def pack(array, order, parts):
    seqs, span, width = array.shape
    half = span // 2
    message = fresh((parts * half, width), array.dtype)
    return call(
        pack_kernel,
        (1,),
        order,
        [in_place(array.reshape(2 * seqs, half, width))],
        [whole(message), whole(message)],
        [pltpu.SemaphoreType.DMA((8,))],
        room=12,
    )


def unpack_kernel(order, first, second, out, sems):
    half = out.shape[1]
    number = out.shape[0]

    def copy(source, index):
        at = pl.ds(pl.multiple_of(order[number + index] * half, half), half)
        return pltpu.make_async_copy(source.at[at], out.at[index], sems.at[index])

    for index in range(number):

        @pl.when(order[index] == 0)
        def _(index=index):
            copy(first, index).start()

        @pl.when(order[index] != 0)
        def _(index=index):
            copy(second, index).start()

    for index in range(number):
        copy(first, index).wait()


def unpack(first, second, order, seqs):
    rows, width = first.shape
    half = rows // seqs
    blocks = call(
        unpack_kernel,
        (1,),
        order,
        [in_place(first), in_place(second)],
        [whole(fresh((2 * seqs, half, width), first.dtype))],
        [pltpu.SemaphoreType.DMA((2 * seqs,))],
        room=12,
    )[0]
    return blocks.reshape(seqs, 2 * half, width)


def join(first, second, span):
    half = span // 2
    return jnp.concatenate(
        [first[:span], second[:span], first[span : span + half], second[span : span + half]],
        axis=0,
    )


def turn_heads(raw, cos, sin):
    columns = range(0, raw.shape[1], PAIR)
    return [rotate(raw[:, at : at + PAIR], cos, sin).astype(low) for at in columns]


def project_kernel(
    place, first, second, gain, shift, w_query, w_key, w_value, b_query, b_key, b_value,
    cosine, sine, query, both, normed,
):
    span = first.shape[0] // 2
    half = span // 2
    for slot, message in enumerate((first, second)):
        rows = [
            slice(slot * span, (slot + 1) * span),
            slice(2 * span + slot * half, 2 * span + (slot + 1) * half),
            slice(3 * span + slot * half, 3 * span + (slot + 1) * half),
        ]
        parts = [slice(0, span), slice(span, span + half), slice(span + half, 2 * span)]
        hat, _ = whiten(message[...].astype(full))
        item = (hat * gain[...] + shift[...]).astype(low)
        starts = [(place[slot], span), (place[2 + slot], half), (place[4 + slot], half)]
        at = [pl.ds(pl.multiple_of(start, half), size) for start, size in starts]
        cos = jnp.concatenate([cosine[index, :] for index in at], axis=0)
        sin = jnp.concatenate([sine[index, :] for index in at], axis=0)
        for row, part in zip(rows, parts):
            normed[row, :] = item[part]
        raw = (matmul(item, w_key[...]) + b_key[...]).astype(low).astype(full)
        for index, turned in enumerate(turn_heads(raw, cos, sin)):
            spot = slice(index * PAIR, (index + 1) * PAIR)
            for row, part in zip(rows, parts):
                both[0, row, spot] = turned[part]
        raw = (matmul(item, w_value[...]) + b_value[...]).astype(low)
        for row, part in zip(rows, parts):
            both[1, row, :] = raw[part]
        near = span + half
        raw = (matmul(item[:near], w_query[...]) + b_query[...]).astype(low).astype(full)
        for index, turned in enumerate(turn_heads(raw, cos[:near], sin[:near])):
            spot = slice(index * PAIR, (index + 1) * PAIR)
            turned = turned * low(HEAD**-0.5)
            for row, part in zip(rows[:2], parts[:2]):
                query[row, spot] = turned[part]


def load_pieces(place, pieces, keys, values):
    for index, piece in enumerate(pieces):
        rows = piece.shape[1] // 2
        for slot in range(2):
            at = pl.ds(pl.multiple_of(place[1 + 2 * index + slot], rows), rows)
            keys[at, :] = piece[0, slot * rows : (slot + 1) * rows, :]
            values[at, :] = piece[1, slot * rows : (slot + 1) * rows, :]


def head_masks(value):
    lane = lax.broadcasted_iota(jnp.int32, value.shape, 1)
    wide = value.astype(full)
    return (
        jnp.where(lane < HEAD, wide, 0.0).astype(low),
        jnp.where(lane < HEAD, 0.0, wide).astype(low),
    )


def by_blocks(length, most, visit):
    number = pl.cdiv(length, BLOCK)
    for blocks in range(1, most + 1):

        @pl.when(number == blocks)
        def _(blocks=blocks):
            visit(blocks, length - (blocks - 1) * BLOCK)


def attend_kernel(count, place, query, *refs):
    pieces = refs[:count]
    out, logsum, keys, values = refs[count:]
    load_pieces(place, pieces, keys, values)
    pairs = [slice(at, at + PAIR) for at in range(0, query.shape[1], PAIR)]

    def visit(blocks, left):
        for pair, columns in enumerate(pairs):
            masked = head_masks(query[:, columns])
            value = values[: blocks * BLOCK, columns].T
            mixed = []
            for head in range(2):
                spot = slice(head * HEAD, (head + 1) * HEAD)
                scores = []
                for block in range(blocks):
                    key = keys[block * BLOCK : (block + 1) * BLOCK, columns]
                    item = matmul_right(key, masked[head])
                    if block == blocks - 1:
                        index = lax.broadcasted_iota(jnp.int32, item.shape, 0)
                        item = jnp.where(index < left, item, -1e30)
                    scores.append(item)
                peaks = [jnp.max(item, axis=0, keepdims=True) for item in scores]
                peak = functools.reduce(jnp.maximum, peaks)
                weights = [jnp.exp(item - peak) for item in scores]
                total = sum(jnp.sum(item, axis=0, keepdims=True) for item in weights)
                product = sum(
                    matmul(value[spot, block * BLOCK : (block + 1) * BLOCK], item.astype(low))
                    for block, item in enumerate(weights)
                )
                mixed.append(product / total)
                logsum[pair, head : head + 1, :] = peak + jnp.log(total)
            out[:, columns] = jnp.concatenate(mixed, axis=0).T.astype(low)

    by_blocks(place[0], keys.shape[0] // BLOCK, visit)


def attend_back_kernel(count, place, query, grad, mixed, logsum, cosine, sine, *refs):
    pieces = refs[:count]
    grad_query, *grad_pieces = refs[count : 1 + 2 * count]
    keys, values, grad_keys, grad_values = refs[1 + 2 * count :]
    load_pieces(place, pieces, keys, values)
    rows = query.shape[0]
    step = rows // 2
    pairs = [slice(at, at + PAIR) for at in range(0, query.shape[1], PAIR)]

    def visit(blocks, left):
        for pair, columns in enumerate(pairs):
            grad_low = grad[:, columns]
            masked = head_masks(query[:, columns])
            masked_grad = head_masks(grad_low)
            inner = (grad_low.astype(full) * mixed[:, columns].astype(full)).T
            delta = [
                jnp.sum(inner[head * HEAD : (head + 1) * HEAD, :], axis=0, keepdims=True)
                for head in range(2)
            ]
            turned = [0.0, 0.0]
            for block in range(blocks):
                at = slice(block * BLOCK, (block + 1) * BLOCK)
                key = keys[at, columns]
                value = values[at, columns]
                flat = key.T
                grad_key = 0.0
                grad_value = 0.0
                for head in range(2):
                    scores = matmul_right(key, masked[head])
                    weights = jnp.exp(scores - logsum[pair, head : head + 1, :])
                    if block == blocks - 1:
                        index = lax.broadcasted_iota(jnp.int32, scores.shape, 0)
                        weights = jnp.where(index < left, weights, 0.0)
                    grad_weights = matmul_right(value, masked_grad[head])
                    grad_scores = (weights * (grad_weights - delta[head])).astype(low)
                    grad_value += matmul(weights.astype(low), masked_grad[head])
                    grad_key += matmul(grad_scores, masked[head])
                    turned[head] += matmul(flat[head * HEAD : (head + 1) * HEAD, :], grad_scores)
                grad_keys[at, columns] = rotate(
                    grad_key, cosine[at, :], -sine[at, :]
                ).astype(low)
                grad_values[at, columns] = grad_value.astype(low)
            back = jnp.concatenate(turned, axis=0).T * HEAD**-0.5
            for slot in range(2):
                at = pl.ds(pl.multiple_of(place[1 + 2 * count + slot], step), step)
                part = slice(slot * step, (slot + 1) * step)
                grad_query[part, columns] = rotate(
                    back[part], cosine[at, :], -sine[at, :]
                ).astype(low)
        for block in range(blocks, keys.shape[0] // BLOCK):
            at = slice(block * BLOCK, (block + 1) * BLOCK)
            grad_keys[at, :] = jnp.zeros_like(grad_keys[at, :])
            grad_values[at, :] = jnp.zeros_like(grad_values[at, :])

    by_blocks(place[0], keys.shape[0] // BLOCK, visit)
    for index, piece in enumerate(grad_pieces):
        rows = piece.shape[1] // 2
        for slot in range(2):
            at = pl.ds(pl.multiple_of(place[1 + 2 * index + slot], rows), rows)
            piece[0, slot * rows : (slot + 1) * rows, :] = grad_keys[at, :]
            piece[1, slot * rows : (slot + 1) * rows, :] = grad_values[at, :]


def put_messages(to_first, to_second, value):
    span = 2 * to_first.shape[0] // 3
    half = span // 2
    to_first[:span, :] = value[:span]
    to_second[:span, :] = value[span : 2 * span]
    to_first[span:, :] = value[2 * span : 2 * span + half]
    to_second[span:, :] = value[2 * span + half :]


def forward_kernel(
    order, own, mixed, first, second, w_out, b_out, gain, shift, w_up, b_up, w_down, b_down,
    middle, normed, hidden, slope, to_first, to_second, result,
):
    span = first.shape[0] // 2
    count = middle.shape[0]

    @pl.when(pl.program_id(0) == 0)
    def _():
        attended = jnp.concatenate([own[...], mixed[...]], axis=0)
        value = join(first[...], second[...], span).astype(full)
        value = value + matmul(attended, w_out[...]) + b_out[...]
        middle[...] = value
        result[...] = value + b_down[...]
        hat, _ = whiten(value)
        normed[...] = (hat * gain[...] + shift[...]).astype(low)

    for row in range(0, count, span):
        spot = slice(row, row + span)
        hidden_in = matmul(normed[spot, :], w_up[...]) + b_up[...]
        share = 0.5 * (1.0 + lax.erf(hidden_in * 0.5**0.5))
        item = (hidden_in * share).astype(low)
        hidden[spot, :] = item
        slope[spot, :] = (
            share + hidden_in * jnp.exp(-0.5 * hidden_in * hidden_in) * 0.3989422804014327
        )
        result[spot, :] += matmul(item, w_down[...])

    @pl.when(pl.program_id(0) == pl.num_programs(0) - 1)
    def _():
        put_messages(to_first, to_second, result[...].astype(low))


def backward_tile(hidden, slope, cot, normed, w_up, w_down, grad_normed, grad_hidden, target):
    count = cot.shape[0]
    step = min(count, 256)
    total = jnp.zeros((1, w_up.shape[1]), full)
    target[0] = matmul_left(hidden[...], cot[...]).astype(low)
    for row in range(0, count, step):
        spot = slice(row, row + step)
        item = (matmul_right(cot[spot, :], w_down[...]) * slope[spot, :]).astype(low)
        grad_hidden[spot, :] = item
        total += jnp.sum(item.astype(full), axis=0, keepdims=True)
        grad_normed[spot, :] += matmul_right(item, w_up[...])
    target[1] = matmul_left(normed[: cot.shape[0], :], grad_hidden[...]).astype(low)
    return total


def backward_first_kernel(
    tiles, hidden, slope, cot_first, cot_second, normed, w_up, w_down,
    sent, grad_b_up, grad_normed, cot, grad_hidden,
):
    @pl.when(pl.program_id(0) == 0)
    def _():
        span = 2 * cot_first.shape[0] // 3
        cot[...] = join(cot_first[...], cot_second[...], span)
        grad_normed[...] = jnp.zeros_like(grad_normed)

    grad_b_up[0:1, :] = backward_tile(
        hidden, slope, cot, normed, w_up, w_down, grad_normed, grad_hidden, sent
    )


def backward_last_kernel(
    tiles, hidden, slope, cot, normed, w_up, w_down, grad_normed_in, own, mixed, middle, w_out,
    gain, kept, grad_b_up, grad_middle, grad_own, grad_mixed, out_kept, out_sent, rows_out,
    grad_normed, grad_hidden, grad_out,
):
    @pl.when(pl.program_id(0) == 0)
    def _():
        grad_normed[...] = grad_normed_in[...]

    grad_b_up[0:1, :] = backward_tile(
        hidden, slope, cot, normed, w_up, w_down, grad_normed, grad_hidden, kept
    )

    @pl.when(pl.program_id(0) == pl.num_programs(0) - 1)
    def _():
        hat, scale = whiten(middle[...])
        grad = grad_normed[...]
        cot_full = cot[...].astype(full)
        rows_out[0:1, :] = jnp.sum(cot_full, axis=0, keepdims=True)
        rows_out[2:3, :] = jnp.sum(grad * hat, axis=0, keepdims=True)
        rows_out[3:4, :] = jnp.sum(grad, axis=0, keepdims=True)
        total = cot_full + whiten_back(grad * gain[...], hat, scale)
        rows_out[1:2, :] = jnp.sum(total, axis=0, keepdims=True)
        rows_out[4:8, :] = jnp.zeros_like(rows_out[4:8, :])
        grad_middle[...] = total
        branch = total.astype(low)
        back = matmul_right(branch, w_out[...]).astype(low)
        grad_own[...] = back[: own.shape[0]]
        grad_mixed[...] = back[own.shape[0] :]
        attended = jnp.concatenate([own[...], mixed[...]], axis=0)
        grad_out[...] = matmul_left(attended, branch).astype(low)
        keep_core_half(tiles[2], grad_out, out_kept, out_sent)


def keep_core_half(core, source, kept, sent):
    size = source.shape[0] // 2
    mine = source[pl.ds(pl.multiple_of(core * size, size), size), :]
    theirs = source[pl.ds(pl.multiple_of((1 - core) * size, size), size), :]
    columns = kept.shape[-1]
    for index in range(kept.shape[0]):
        spot = slice(index * columns, (index + 1) * columns)
        kept[index] = mine[:, spot]
        sent[index] = theirs[:, spot]


def halve_kernel(order, kept, received, keep_left, give_left, keep_right, give_right):
    for index, (keep, give) in enumerate(((keep_left, give_left), (keep_right, give_right))):
        for target, half in ((keep, order[1 + index]), (give, 1 - order[1 + index])):
            total = kept[index, half].astype(full) + received[index, half].astype(full)
            target[0] = total.astype(low)


def quarter_kernel(order, kept, received, out_kept, out_received, *targets):
    rows = targets[0].shape[1]
    for index in range(2):
        for target, half in (
            (targets[2 * index], order[1 + index]),
            (targets[2 * index + 1], 1 - order[1 + index]),
        ):
            at = pl.ds(pl.multiple_of((2 * index + half) * rows, rows), rows)
            for lead in range(3):
                total = kept[lead, at, :].astype(full) + received[lead, at, :].astype(full)
                target[lead] = total.astype(low)
            total = out_kept[0, at, :].astype(full) + out_received[0, at, :].astype(full)
            target[3] = total.astype(low)


def stage_kernel(joined, order, *refs):
    count = len(refs) // 5 if not joined else (len(refs) - 3) // 2
    pairs = refs[: 2 * count]
    if joined:
        outs, totals = refs[-3:-1], refs[-1:]
        at = 0
        for index in range(count):
            rows = pairs[2 * index].shape[1]
            totals[0][:, at : at + rows, :] = (
                pairs[2 * index][...].astype(full) + pairs[2 * index + 1][...].astype(full)
            )
            at += rows
    else:
        outs, totals = refs[2 * count : 4 * count], refs[4 * count :]
        for index in range(count):
            totals[index][...] = (
                pairs[2 * index][...].astype(full) + pairs[2 * index + 1][...].astype(full)
            )
    for index, total in enumerate(totals):
        rows = total.shape[1] // 2
        for target, half in ((outs[2 * index], order[index]), (outs[2 * index + 1], 1 - order[index])):
            at = pl.ds(pl.multiple_of(half * rows, rows), rows)
            target[...] = total[:, at, :].astype(low)


def grad_far_kernel(order, kept, received, w_key, w_value, both, grad_far):
    for index in range(2):
        both[index] = (kept[index].astype(full) + received[index].astype(full)).astype(low)
    grad = matmul_right(both[0], w_key[...]) + matmul_right(both[1], w_value[...])
    half = grad.shape[0] // 2
    grad_far[:half, :] = grad[half:].astype(low)
    grad_far[half:, :] = grad[:half].astype(low)


def weight_kernel(
    core, normed, query_own, query_mixed, own_kept, own_received, mixed_kept,
    mixed_received, far, kept, sent, both, rows_out, grad_weight,
):
    item = jnp.concatenate([query_own[...], query_mixed[...]], axis=0)
    count = item.shape[0]
    rows_out[0:1, :] = jnp.sum(item.astype(full), axis=0, keepdims=True)
    grad_weight[...] = matmul_left(normed[:count, :], item).astype(low)
    keep_core_half(core[0], grad_weight, kept.at[0:1], sent.at[0:1])
    for index in range(2):
        own = own_kept[index].astype(full) + own_received[index].astype(full)
        mixed = mixed_kept[index].astype(full) + mixed_received[index].astype(full)
        item = jnp.concatenate([own.astype(low), mixed.astype(low), far[index]], axis=0)
        both[index] = item[:count]
        rows_out[1 + index : 2 + index, :] = jnp.sum(item.astype(full), axis=0, keepdims=True)
        grad_weight[...] = matmul_left(normed[...], item).astype(low)
        keep_core_half(
            core[0], grad_weight, kept.at[1 + index : 2 + index], sent.at[1 + index : 2 + index]
        )
    rows_out[3:8, :] = jnp.zeros_like(rows_out[3:8, :])


def input_kernel(
    core, query_own, query_mixed, both, far, w_query, w_key, w_value, first,
    second, gain, grad_middle, to_first, to_second, rows_out,
):
    span = first.shape[0] // 2
    grad_query = jnp.concatenate([query_own[...], query_mixed[...]], axis=0)
    grad = matmul_right(grad_query, w_query[...])
    for index, weight in enumerate((w_key, w_value)):
        grad = grad + matmul_right(both[index], weight[...])
    grad = jnp.concatenate(
        [grad[: 2 * span], grad[2 * span :] + far[...].astype(full)], axis=0
    )
    hat, scale = whiten(join(first[...], second[...], span).astype(full))
    rows_out[0:1, :] = jnp.sum(grad * hat, axis=0, keepdims=True)
    rows_out[1:2, :] = jnp.sum(grad, axis=0, keepdims=True)
    rows_out[2:8, :] = jnp.zeros_like(rows_out[2:8, :])
    done = (grad_middle[...] + whiten_back(grad * gain[...], hat, scale)).astype(low)
    put_messages(to_first, to_second, done)


def expand_kernel(place, order, *refs):
    sources = refs[:4]
    out = refs[-1]
    choice = 2 * ((pl.program_id(0) // 2) ^ order[0]) + ((pl.program_id(0) % 2) ^ order[place])
    for number, source in enumerate(sources):

        @pl.when(choice == number)
        def _(source=source):
            out[...] = source[0].astype(full)


def expand_mixed_kernel(order, *refs):
    sources, outs = refs[:8], refs[8:]
    index = pl.program_id(0)
    side = (index // 2) % 2
    bit = jnp.where(side == 0, order[1], order[2])
    choice = 4 * side + 2 * ((index // 4) ^ order[0]) + ((index % 2) ^ bit)
    for number, source in enumerate(sources):

        @pl.when(choice == number)
        def _(source=source):
            for place, out in enumerate(outs):
                out[...] = source[place].astype(full)


def after(value, *others):
    return lax.optimization_barrier((value, *others))[0]


def on_device(
    inputs, cotangent, lengths, predicted, norm1_gain, norm1_shift, w_query, b_query, w_key,
    b_key, w_value, b_value, w_out, b_out, norm2_gain, norm2_shift, w_up, b_up, w_down, b_down,
):
    seqs, span, width = inputs.shape
    half = span // 2
    tokens = seqs * span
    hidden_width = w_up.shape[1]
    groups = lax.axis_size("dp")
    assert seqs == 3 and lax.axis_size("seq") == 4 and hidden_width == 4 * width
    bits = [1 << place for place in range(1, groups.bit_length() - 1)]
    group = lax.axis_index("dp")
    depth = lax.axis_index("seq")
    core = group & 1
    side = depth & 1
    pair = depth >> 1
    count = 4 * span
    pairs = width // PAIR
    square = (width, width)

    def flip(value, bit):
        return lax.ppermute(value, "dp", [(i, i ^ bit) for i in range(groups)])

    def flip_depth(value, bit):
        return lax.ppermute(value, "seq", [(i, i ^ bit) for i in range(4)])

    def route(turn):
        moves = []
        for at in range(groups):
            for z in range(4):
                to = (at & ~1) | (z & 1)
                to_z = 2 * (at & 1) + (turn ^ (z >> 1))
                moves.append((at * 4 + z, to * 4 + to_z))
        return moves

    def send(value, turn):
        return lax.ppermute(value, ("dp", "seq"), route(turn))

    def send_back(value, turn):
        return lax.ppermute(value, ("dp", "seq"), [(b, a) for a, b in route(turn)])

    def ranks(sizes):
        longest = jnp.argmax(sizes).astype(jnp.int32)
        return (
            jnp.where(longest == 0, 1, 0),
            jnp.where(longest == 2, 1, 2),
            longest,
        )

    low_own, high_own, mixed_at = ranks(lengths)
    near = jnp.where(pair == 0, low_own, high_own)
    other = jnp.where(pair == 0, high_own, low_own)
    index = jnp.arange(8)
    turn = index // 4
    spot = index % 4
    chosen = jnp.where(turn == 0, near, other)
    order = jnp.where(
        spot < 2, 2 * chosen + spot, 2 * mixed_at + (turn ^ pair ^ (spot // 3))
    )
    first, second = pack(inputs, order, 4)
    cot_first, cot_second = pack(after(cotangent, first), order, 3)
    first, second = send(first, 0), send(second, 1)
    index = jnp.arange(2 * seqs)
    seq_at = index // 2
    part = index % 2
    from_turn = jnp.where(seq_at == mixed_at, part, (seq_at == high_own).astype(jnp.int32)) ^ pair
    from_row = jnp.where(seq_at == mixed_at, 2, part)
    order_back = jnp.concatenate([from_turn, from_row])

    sibling_lengths = flip(lengths, 1)
    sizes = jnp.where(core == pair, lengths, sibling_lengths)
    low_here, high_here, mixed_here = ranks(sizes)
    own_length = sizes[jnp.where(side == 0, low_here, high_here)]
    mixed_length = sizes[mixed_here]

    def starts(at_side, at_core):
        slots = jnp.arange(2)
        quarter = 2 * (slots ^ at_side) + at_core
        return quarter * span, quarter * span + at_side * half

    own_at, mixed_start = starts(side, core)
    own_sibling, mixed_sibling = starts(side, 1 - core)
    far_start = own_at + (1 - side) * half
    far_sibling = own_sibling + (1 - side) * half
    own_place = jnp.concatenate([own_length[None], own_at, own_sibling, own_at])
    mixed_place = jnp.concatenate(
        [mixed_length[None], mixed_start, mixed_sibling, far_start, far_sibling, mixed_start]
    )
    project_place = jnp.concatenate([own_at, mixed_start, far_start])

    frequency = 10000.0 ** (-jnp.arange(HEAD // 2, dtype=full) / (HEAD // 2))
    angle = jnp.arange(count, dtype=full)[:, None] * frequency[None, :]
    cosine = jnp.tile(jnp.cos(angle), (1, 4))
    sine = jnp.sin(angle)
    sine = jnp.tile(jnp.concatenate([-sine, sine], axis=1), (1, 2))

    def row(vector):
        return vector.reshape(1, -1)

    gain1, shift1 = row(norm1_gain), row(norm1_shift)
    gain2, shift2 = row(norm2_gain), row(norm2_shift)

    def wholes(*items):
        return [whole(item) for item in items]

    extent = tokens + span
    project_place = after(project_place, cot_first, own_place, mixed_place, cosine, sine)
    query, both, normed = call(
        project_kernel,
        (1,),
        project_place,
        wholes(
            first, second, gain1, shift1, w_query, w_key, w_value, row(b_query), row(b_key),
            row(b_value), cosine, sine,
        ),
        wholes(
            fresh((tokens, width), low), fresh((2, extent, width), low), fresh((extent, width), low)
        ),
    )
    both_sibling = flip(both, 1)
    cot_first, cot_second, _ = lax.optimization_barrier((cot_first, cot_second, first))
    cot_first, cot_second = send(cot_first, 0), send(cot_second, 1)

    def columns(array, rows, at, size=PAIR, base=0):
        if len(array.shape) == 2:
            return (array, pl.BlockSpec((rows, size), lambda h, _: (at, base + h)))
        return (array, pl.BlockSpec((2, rows, size), lambda h, _: (0, at, base + h)))

    def own_pieces(*given):
        return [columns(both, 2 * span, 0, *given), columns(both_sibling, 2 * span, 0, *given)]

    def mixed_pieces(*given):
        return [
            columns(both, span, 2, *given),
            columns(both_sibling, span, 2, *given),
            columns(both, span, 3, *given),
            columns(both_sibling, span, 3, *given),
        ]

    def attend(place, rows, at, pieces):
        size = 2 * PAIR
        pieces = pieces(size)
        return call(
            functools.partial(attend_kernel, len(pieces)),
            (width // size,),
            place,
            [columns(query, rows, at, size), *pieces],
            [
                columns(fresh((rows, width), low), rows, 0, size),
                (
                    fresh((pairs, 8, rows), full),
                    pl.BlockSpec((2, 8, rows), lambda h, _: (h, 0, 0)),
                ),
            ],
            [pltpu.VMEM((count, size), low), pltpu.VMEM((count, size), low)],
                )

    own, own_logsum = attend(own_place, 2 * span, 0, own_pieces)
    mixed, mixed_logsum = attend(after(mixed_place, own), span, 2, mixed_pieces)

    def wide(array):
        return (array, pl.BlockSpec(square, lambda j, tiles: (0, tiles[j])))

    def tall(array):
        return (array, pl.BlockSpec(square, lambda j, tiles: (tiles[j], 0)))

    middle, normed2, hidden, slope, result_first, result_second = call(
        forward_kernel,
        (4,),
        jnp.arange(4),
        wholes(own, mixed, first, second, w_out, row(b_out), gain2, shift2)
        + [
            wide(w_up),
            (row(b_up), pl.BlockSpec((1, width), lambda j, tiles: (0, tiles[j]))),
            tall(w_down),
            whole(row(b_down)),
        ],
        wholes(fresh((tokens, width), full), fresh((tokens, width), low))
        + [wide(fresh((tokens, hidden_width), low)), wide(fresh((tokens, hidden_width), full))]
        + wholes(fresh((tokens // 2, width), low), fresh((tokens // 2, width), low)),
        [pltpu.VMEM((tokens, width), full)],
    )
    result = [send_back(result_first, 0), send_back(result_second, 1)]

    rows_fresh = fresh((8, width), full)
    grad_scratch = [pltpu.VMEM((tokens, width), low)]

    def tile_outs():
        return [
            (
                fresh((2, 2, width, width), low),
                pl.BlockSpec((2, None, width, width), lambda j, _: (0, j, 0, 0)),
            ),
            (fresh((2, 8, width), full), pl.BlockSpec((None, 8, width), lambda j, _: (j, 0, 0))),
        ]

    tiles_sent, b_up_sent, grad_normed2, cot = call(
        backward_first_kernel,
        (2,),
        jnp.stack([2 * (1 - core), 2 * (1 - core) + 1]),
        [wide(hidden), wide(slope)]
        + wholes(cot_first, cot_second, normed2)
        + [wide(w_up), tall(w_down)],
        tile_outs() + wholes(fresh((tokens, width), full), fresh((tokens, width), low)),
        grad_scratch,
    )
    tiles_received = flip(tiles_sent, 1)
    (
        tiles_kept, b_up_kept, grad_middle, grad_own, grad_mixed, out_kept, out_sent, rows_middle,
    ) = call(
        backward_last_kernel,
        (2,),
        jnp.stack([2 * core, 2 * core + 1, core]),
        [wide(hidden), wide(slope)]
        + wholes(cot, normed2)
        + [wide(w_up), tall(w_down)]
        + wholes(grad_normed2, own, mixed, middle, w_out, gain2),
        tile_outs()
        + wholes(
            fresh((tokens, width), full), fresh((2 * span, width), low), fresh((span, width), low),
            fresh((1, width // 2, width), low), fresh((1, width // 2, width), low), rows_fresh,
        ),
        [pltpu.VMEM((tokens, width), full), *grad_scratch, pltpu.VMEM(square, low)],
    )
    out_received = flip(out_sent, 1)

    def bit_of(bit):
        return (group & bit) // bit

    def split(addends, at):
        rows = addends[0].shape[1] // 2

        def part(which):
            items = [
                lax.dynamic_slice_in_dim(item, which * rows, rows, 1).astype(full)
                for item in addends
            ]
            return sum(items[1:], items[0]).astype(low)

        return part(at), part(1 - at)

    def added(addends):
        return (addends[0].astype(full) + addends[1].astype(full)).astype(low)

    def ordered(at, mine, theirs):
        return jnp.where(
            at == 0,
            jnp.concatenate([mine, theirs], axis=1),
            jnp.concatenate([theirs, mine], axis=1),
        )

    def stage(values, at, joined=False):
        lead, _, columns_in = values[0][0].shape
        sizes = [item[0].shape[1] for item in values]
        sizes = [sum(sizes)] if joined else sizes
        if any(size % 16 for size in sizes):
            if joined:
                values = [[jnp.concatenate([added(item) for item in values], axis=1)]]
            return [split(item, place) for item, place in zip(values, at)]
        parts = call(
            functools.partial(stage_kernel, joined),
            (1,),
            jnp.stack(at),
            wholes(*[part for item in values for part in item]),
            wholes(
                *[fresh((lead, size // 2, columns_in), low) for size in sizes for _ in range(2)]
            ),
            [pltpu.VMEM((lead, size, columns_in), full) for size in sizes],
            room=32,
        )
        return [tuple(parts[2 * place : 2 * place + 2]) for place in range(len(sizes))]

    def chain(parts, orders):
        for step in range(len(bits)):
            if step > 0:
                parts = stage(values, [bit_of(order[step]) for order in orders])
            values = yield [
                [keep, flip(give, order[step])] for (keep, give), order in zip(parts, orders)
            ]
        sizes = [item[0].shape[1] for item in values]
        ((keep, give),) = stage(values, [side], joined=True)
        values = yield [[keep, flip_depth(give, 1)]]
        ((keep, give),) = stage(values, [pair])
        (value,) = yield [[keep, flip_depth(give, 2)]]
        total = added(value)
        (value,) = yield [[total, flip_depth(total, 2)]]
        joined = ordered(pair, *value)
        (value,) = yield [[joined, flip_depth(joined, 1)]]
        joined = ordered(side, *value)
        ends = [sum(sizes[: place + 1]) for place in range(len(sizes))]
        values = [joined[:, end - size : end] for end, size in zip(ends, sizes)]
        for step in range(len(bits) - 1, 0, -1):
            values = yield [
                [item, flip(item, order[step])] for item, order in zip(values, orders)
            ]
            values = [
                ordered(bit_of(order[step]), *item) for item, order in zip(values, orders)
            ]
        values = yield [[item, flip(item, order[0])] for item, order in zip(values, orders)]
        values = yield [item + [flip(part, 1) for part in item] for item in values]
        yield values

    class Chain:
        def __init__(self, left, right):
            self.steps = chain([left, right], [bits, reverse])
            self.state = next(self.steps)
            self.left = 2 * len(bits) + 5

        def here(self):
            return [item[0] for item in self.state]

    def advance(chains, *gates):
        chains = [item for item in chains if item.left > 0]
        states = lax.optimization_barrier(([item.state for item in chains], gates))[0]
        for item, state in zip(chains, states):
            item.state = item.steps.send(state)
            item.left -= 1

    reverse = bits[::-1]
    orders = jnp.stack([core, bit_of(bits[0]), bit_of(bits[-1])])

    part = fresh((1, width, width), low)
    parts = call(
        halve_kernel,
        (1,),
        orders,
        wholes(tiles_kept, tiles_received),
        wholes(part, part, part, part),
        room=40,
    )
    tile_sum = Chain(tuple(parts[:2]), tuple(parts[2:]))
    result = unpack(after(result[0], grad_middle), result[1], order_back, seqs)

    def attend_back(place, rows, at, pieces, grad, out, logsum, size, base, steps):
        given = pieces(size, base)
        group_pairs = size // PAIR
        return call(
            functools.partial(attend_back_kernel, len(given)),
            (steps,),
            place,
            [
                columns(query, rows, at, size, base),
                columns(grad, rows, 0, size, base),
                columns(out, rows, 0, size, base),
                (logsum, pl.BlockSpec((group_pairs, 8, rows), lambda h, _: (base + h, 0, 0))),
                whole(cosine),
                whole(sine),
                *given,
            ],
            [columns(fresh((rows, size * steps), low), rows, 0, size)]
            + [columns(fresh((2, rows, size * steps), low), rows, 0, size) for _ in given],
            [pltpu.VMEM((count, size), low)] * 4,
                )

    query_mixed, mixed_here_grad, mixed_sibling_grad, far_grad, far_sibling_grad = attend_back(
        after(mixed_place, *tile_sum.here(), result), span, 2, mixed_pieces, grad_mixed, mixed, mixed_logsum,
        2 * PAIR, 0, pairs // 2,
    )
    far_received = flip(far_sibling_grad, 1)
    mixed_received = flip(mixed_sibling_grad, 1)
    advance([tile_sum], query_mixed)
    far_both, grad_far = call(
        grad_far_kernel,
        (1,),
        after(core[None], *tile_sum.here()),
        wholes(far_grad, far_received, w_key, w_value),
        wholes(fresh((2, span, width), low), fresh((span, width), low)),
    )
    grad_far = flip_depth(grad_far, 1)

    query_own, own_kept, own_sent = attend_back(
        after(own_place, far_both), 2 * span, 0, own_pieces, grad_own, own, own_logsum, 2 * PAIR, 0,
        pairs // 2,
    )
    own_received = flip(own_sent, 1)
    advance([tile_sum], query_own)
    weight_kept, weight_sent, both_grad, rows_weight = call(
        weight_kernel,
        (1,),
        after(core[None], *tile_sum.here()),
        wholes(
            normed, query_own, query_mixed, own_kept, own_received, mixed_here_grad,
            mixed_received, far_both,
        ),
        wholes(
            fresh((3, width // 2, width), low), fresh((3, width // 2, width), low),
            fresh((2, tokens, width), low), rows_fresh,
        ),
        [pltpu.VMEM(square, low)],
    )
    weight_received = flip(weight_sent, 1)
    advance([tile_sum], rows_weight)
    back_first, back_second, rows_input = call(
        input_kernel,
        (1,),
        after(core[None], *tile_sum.here()),
        wholes(
            query_own, query_mixed, both_grad, grad_far, w_query, w_key, w_value, first, second,
            gain1, grad_middle,
        ),
        wholes(fresh((tokens // 2, width), low), fresh((tokens // 2, width), low), rows_fresh),
    )

    live = (depth * span + jnp.arange(span))[None, :] < lengths[:, None]
    counts = jnp.sum(
        jnp.where(live[:, :, None] & (predicted[:, :, None] == jnp.arange(CLASSES)), 1.0, 0.0),
        axis=(0, 1),
    )
    counts = jnp.zeros((1, width), full).at[0, :CLASSES].set(counts)
    b_up_kept, b_up_sent = b_up_kept[:, 0], b_up_sent[:, 0]
    rows_up = jnp.where(
        core == 0,
        jnp.concatenate([b_up_kept, b_up_sent]),
        jnp.concatenate([b_up_sent, b_up_kept]),
    )
    small = jnp.concatenate(
        [rows_middle[:4], rows_up, rows_weight[:3], rows_input[:2], counts], axis=0
    )

    class Small:
        def __init__(self):
            self.moves = [(flip, bit) for bit in (1, *bits)] + [(flip_depth, 1), (flip_depth, 2)]
            self.steps = self
            move, bit = self.moves.pop(0)
            self.state = [[small, move(small, bit)]]
            self.left = len(bits) + 3

        def send(self, state):
            total = state[0][0] + state[0][1]
            if not self.moves:
                return [[total]]
            move, bit = self.moves.pop(0)
            return [[total, move(total, bit)]]
    back = [send_back(back_first, 0), send_back(back_second, 1)]
    weight_kept, weight_received, out_kept, out_received, _ = lax.optimization_barrier(
        (weight_kept, weight_received, out_kept, out_received, rows_input)
    )
    part = fresh((4, width // 8, width), low)
    parts = call(
        quarter_kernel,
        (1,),
        orders,
        wholes(weight_kept, weight_received, out_kept, out_received),
        wholes(part, part, part, part),
        room=32,
    )
    weight_sum = Chain(tuple(parts[:2]), tuple(parts[2:]))
    small_sum = Small()
    for _ in range(3):
        advance([weight_sum, small_sum, tile_sum])
    grad_inputs = unpack(after(back[0], *weight_sum.here()), back[1], order_back, seqs)
    advance([weight_sum, small_sum, tile_sum], grad_inputs)
    while tile_sum.left > 0:
        advance([weight_sum, small_sum, tile_sum])
    left, right = tile_sum.state
    gate = weight_sum.here()

    def expand(sources, place, shape, target):
        return call(
            functools.partial(expand_kernel, place),
            (4,),
            after(orders, *gate),
            wholes(*sources),
            [(fresh(shape, full), pl.BlockSpec(square, target))],
            room=32,
        )[0]

    grad_w_down = expand(left, 1, (hidden_width, width), lambda i, _: (i, 0))
    grad_w_up = expand(right, 2, (width, hidden_width), lambda i, _: (0, i))
    advance([weight_sum, small_sum], grad_w_down)
    advance([weight_sum, small_sum], grad_w_up)
    gates = []
    while weight_sum.left > 0 or small_sum.left > 0:
        advance([weight_sum, small_sum], *gates)
        gates = []
    left, right = weight_sum.state
    grad_w_query, grad_w_key, grad_w_value, grad_w_out = call(
        expand_mixed_kernel,
        (8,),
        orders,
        wholes(*left, *right),
        [(fresh(square, full), pl.BlockSpec((width // 8, width), lambda i, _: (i, 0)))] * 4,
        room=32,
    )
    small = small_sum.state[0][0]

    return (
        result,
        grad_inputs,
        small[11],
        small[12],
        grad_w_query,
        small[8],
        grad_w_key,
        small[9],
        grad_w_value,
        small[10],
        grad_w_out,
        small[1],
        small[2],
        small[3],
        grad_w_up,
        small[4:8].reshape(-1),
        grad_w_down,
        small[0],
        small[13, :CLASSES].astype(jnp.int32),
    )


def solution(mesh):
    tokens = P("dp", "seq", None)
    return jax.shard_map(
        on_device,
        mesh=mesh,
        in_specs=(tokens, tokens, P("dp"), P("dp", "seq")) + (P(),) * 16,
        out_specs=(tokens, tokens) + (P(),) * 17,
        check_vma=False,
    )
```

```python
import functools

import jax
import jax.numpy as jnp
from jax import lax
from jax.experimental import pallas as pl
from jax.experimental.pallas import tpu as pltpu
from jax.sharding import PartitionSpec as P

HEAD = 64
CLASSES = 70
PAIR = 2 * HEAD
BLOCK = 256

epsilon = 1e-05
low = jnp.bfloat16
full = jnp.float32


def matmul(left, right):
    return lax.dot_general(
        left, right, (((1,), (0,)), ((), ())), preferred_element_type=full
    )


def matmul_left(left, right):
    return lax.dot_general(
        left, right, (((0,), (0,)), ((), ())), preferred_element_type=full
    )


def matmul_right(left, right):
    return lax.dot_general(
        left, right, (((1,), (1,)), ((), ())), preferred_element_type=full
    )


def whiten(value):
    centre = value - jnp.mean(value, axis=-1, keepdims=True)
    scale = lax.rsqrt(jnp.mean(centre * centre, axis=-1, keepdims=True) + epsilon)
    return centre * scale, scale


def whiten_back(grad, hat, scale):
    mean = jnp.mean(grad, axis=-1, keepdims=True)
    along = jnp.mean(grad * hat, axis=-1, keepdims=True)
    return scale * (grad - mean - hat * along)


def rotate(value, cosine, sine):
    lane = lax.broadcasted_iota(jnp.int32, value.shape, 1)
    ahead = pltpu.roll(value, PAIR - HEAD // 2, 1)
    behind = pltpu.roll(value, HEAD // 2, 1)
    swapped = jnp.where(lane % HEAD < HEAD // 2, ahead, behind)
    return value * cosine + swapped * sine


def call(kernel, grid, scalars, inputs, outputs, scratch=(), cost=20, room=60, aliases=None):
    return pl.pallas_call(
        kernel,
        grid_spec=pltpu.PrefetchScalarGridSpec(
            num_scalar_prefetch=1,
            grid=grid,
            in_specs=[spec for _, spec in inputs],
            out_specs=[spec for _, spec in outputs],
            scratch_shapes=list(scratch),
        ),
        out_shape=[shape for shape, _ in outputs],
        input_output_aliases=aliases or {},
        compiler_params=pltpu.CompilerParams(
            dimension_semantics=("arbitrary",) * len(grid), vmem_limit_bytes=room << 20
        ),
        cost_estimate=pl.CostEstimate(
            flops=int(cost * 1e9), transcendentals=0, bytes_accessed=int(cost * 2e6)
        ),
    )(scalars, *[array for array, _ in inputs])


def whole(array):
    rank = len(array.shape)
    return (array, pl.BlockSpec(array.shape, lambda *_: (0,) * rank))


def fresh(shape, kind):
    return jax.ShapeDtypeStruct(shape, kind)


def ranks(sizes):
    one, two, three = sizes[0], sizes[1], sizes[2]
    longest = jnp.where((one >= two) & (one >= three), 0, jnp.where(two >= three, 1, 2))
    return jnp.where(longest == 0, 1, 0), jnp.where(longest == 2, 1, 2), longest


def pack_kernel(sizes, blocks, first, second, sems):
    half = blocks.shape[1]
    pair = lax.axis_index("seq") // 2
    low_own, high_own, longest = ranks(sizes)
    copies = []
    for number, target in enumerate((first, second)):
        side = pair if number == 0 else 1 - pair
        own = jnp.where(side == 0, low_own, high_own)
        spots = [2 * own, 2 * own + 1, 2 * longest + side, 2 * longest + 1 - side]
        for place in range(target.shape[0] // half):
            copies.append(
                pltpu.make_async_copy(
                    blocks.at[spots[place]],
                    target.at[pl.ds(place * half, half)],
                    sems.at[4 * number + place],
                )
            )
    for copy in copies:
        copy.start()
    for copy in copies:
        copy.wait()


def in_place(array):
    return (array, pl.BlockSpec(memory_space=pl.ANY))


def pack(array, sizes, parts):
    seqs, span, width = array.shape
    half = span // 2
    message = fresh((parts * half, width), array.dtype)
    return call(
        pack_kernel,
        (1,),
        sizes,
        [in_place(array.reshape(2 * seqs, half, width))],
        [whole(message), whole(message)],
        [pltpu.SemaphoreType.DMA((8,))],
        room=12,
    )


def unpack_kernel(order, first, second, out, sems):
    half = out.shape[1]
    number = out.shape[0]

    def copy(source, index):
        at = pl.ds(pl.multiple_of(order[number + index] * half, half), half)
        return pltpu.make_async_copy(source.at[at], out.at[index], sems.at[index])

    for index in range(number):

        @pl.when(order[index] == 0)
        def _(index=index):
            copy(first, index).start()

        @pl.when(order[index] != 0)
        def _(index=index):
            copy(second, index).start()

    for index in range(number):
        copy(first, index).wait()


def unpack(first, second, order, seqs):
    rows, width = first.shape
    half = rows // seqs
    blocks = call(
        unpack_kernel,
        (1,),
        order,
        [in_place(first), in_place(second)],
        [whole(fresh((2 * seqs, half, width), first.dtype))],
        [pltpu.SemaphoreType.DMA((2 * seqs,))],
        room=12,
    )[0]
    return blocks.reshape(seqs, 2 * half, width)


def join(first, second, span):
    half = span // 2
    return jnp.concatenate(
        [first[:span], second[:span], first[span : span + half], second[span : span + half]],
        axis=0,
    )


def turn_heads(raw, cos, sin):
    columns = range(0, raw.shape[1], PAIR)
    return [rotate(raw[:, at : at + PAIR], cos, sin).astype(low) for at in columns]


def project_kernel(
    place, first, second, gain, shift, w_query, w_key, w_value, b_query, b_key, b_value,
    cosine, sine, query, both, normed,
):
    span = first.shape[0] // 2
    half = span // 2
    for slot, message in enumerate((first, second)):
        rows = [
            slice(slot * span, (slot + 1) * span),
            slice(2 * span + slot * half, 2 * span + (slot + 1) * half),
            slice(3 * span + slot * half, 3 * span + (slot + 1) * half),
        ]
        parts = [slice(0, span), slice(span, span + half), slice(span + half, 2 * span)]
        hat, _ = whiten(message[...].astype(full))
        item = (hat * gain[...] + shift[...]).astype(low)
        starts = [(place[slot], span), (place[2 + slot], half), (place[4 + slot], half)]
        at = [pl.ds(pl.multiple_of(start, half), size) for start, size in starts]
        cos = jnp.concatenate([cosine[index, :] for index in at], axis=0)
        sin = jnp.concatenate([sine[index, :] for index in at], axis=0)
        for row, part in zip(rows, parts):
            normed[row, :] = item[part]
        raw = (matmul(item, w_key[...]) + b_key[...]).astype(low).astype(full)
        for index, turned in enumerate(turn_heads(raw, cos, sin)):
            spot = slice(index * PAIR, (index + 1) * PAIR)
            for row, part in zip(rows, parts):
                both[0, row, spot] = turned[part]
        raw = (matmul(item, w_value[...]) + b_value[...]).astype(low)
        for row, part in zip(rows, parts):
            both[1, row, :] = raw[part]
        near = span + half
        raw = (matmul(item[:near], w_query[...]) + b_query[...]).astype(low).astype(full)
        for index, turned in enumerate(turn_heads(raw, cos[:near], sin[:near])):
            spot = slice(index * PAIR, (index + 1) * PAIR)
            turned = turned * low(HEAD**-0.5)
            for row, part in zip(rows[:2], parts[:2]):
                query[row, spot] = turned[part]


def load_pieces(place, pieces, keys, values):
    for index, piece in enumerate(pieces):
        rows = piece.shape[1] // 2
        for slot in range(2):
            at = pl.ds(pl.multiple_of(place[1 + 2 * index + slot], rows), rows)
            keys[at, :] = piece[0, slot * rows : (slot + 1) * rows, :]
            values[at, :] = piece[1, slot * rows : (slot + 1) * rows, :]


def head_masks(value):
    lane = lax.broadcasted_iota(jnp.int32, value.shape, 1)
    wide = value.astype(full)
    return (
        jnp.where(lane < HEAD, wide, 0.0).astype(low),
        jnp.where(lane < HEAD, 0.0, wide).astype(low),
    )


def by_blocks(length, most, visit):
    number = pl.cdiv(length, BLOCK)
    for blocks in range(1, most + 1):

        @pl.when(number == blocks)
        def _(blocks=blocks):
            visit(blocks, length - (blocks - 1) * BLOCK)


def attend_kernel(count, place, query, *refs):
    pieces = refs[:count]
    out, logsum, keys, values = refs[count:]
    load_pieces(place, pieces, keys, values)
    pairs = [slice(at, at + PAIR) for at in range(0, query.shape[1], PAIR)]

    def visit(blocks, left):
        for pair, columns in enumerate(pairs):
            masked = head_masks(query[:, columns])
            value = values[: blocks * BLOCK, columns].T
            mixed = []
            for head in range(2):
                spot = slice(head * HEAD, (head + 1) * HEAD)
                scores = []
                for block in range(blocks):
                    key = keys[block * BLOCK : (block + 1) * BLOCK, columns]
                    item = matmul_right(key, masked[head])
                    if block == blocks - 1:
                        index = lax.broadcasted_iota(jnp.int32, item.shape, 0)
                        item = jnp.where(index < left, item, -1e30)
                    scores.append(item)
                peaks = [jnp.max(item, axis=0, keepdims=True) for item in scores]
                peak = functools.reduce(jnp.maximum, peaks)
                weights = [jnp.exp(item - peak) for item in scores]
                total = sum(jnp.sum(item, axis=0, keepdims=True) for item in weights)
                product = sum(
                    matmul(value[spot, block * BLOCK : (block + 1) * BLOCK], item.astype(low))
                    for block, item in enumerate(weights)
                )
                mixed.append(product / total)
                logsum[pair, head : head + 1, :] = peak + jnp.log(total)
            out[:, columns] = jnp.concatenate(mixed, axis=0).T.astype(low)

    by_blocks(place[0], keys.shape[0] // BLOCK, visit)


def attend_back_kernel(count, place, query, grad, mixed, logsum, cosine, sine, *refs):
    pieces = refs[:count]
    grad_query, *grad_pieces = refs[count : 1 + 2 * count]
    keys, values, grad_keys, grad_values = refs[1 + 2 * count :]
    load_pieces(place, pieces, keys, values)
    rows = query.shape[0]
    step = rows // 2
    pairs = [slice(at, at + PAIR) for at in range(0, query.shape[1], PAIR)]

    def visit(blocks, left):
        for pair, columns in enumerate(pairs):
            grad_low = grad[:, columns]
            masked = head_masks(query[:, columns])
            masked_grad = head_masks(grad_low)
            inner = (grad_low.astype(full) * mixed[:, columns].astype(full)).T
            delta = [
                jnp.sum(inner[head * HEAD : (head + 1) * HEAD, :], axis=0, keepdims=True)
                for head in range(2)
            ]
            turned = [0.0, 0.0]
            for block in range(blocks):
                at = slice(block * BLOCK, (block + 1) * BLOCK)
                key = keys[at, columns]
                value = values[at, columns]
                flat = key.T
                grad_key = 0.0
                grad_value = 0.0
                for head in range(2):
                    scores = matmul_right(key, masked[head])
                    weights = jnp.exp(scores - logsum[pair, head : head + 1, :])
                    if block == blocks - 1:
                        index = lax.broadcasted_iota(jnp.int32, scores.shape, 0)
                        weights = jnp.where(index < left, weights, 0.0)
                    grad_weights = matmul_right(value, masked_grad[head])
                    grad_scores = (weights * (grad_weights - delta[head])).astype(low)
                    grad_value += matmul(weights.astype(low), masked_grad[head])
                    grad_key += matmul(grad_scores, masked[head])
                    turned[head] += matmul(flat[head * HEAD : (head + 1) * HEAD, :], grad_scores)
                grad_keys[at, columns] = rotate(
                    grad_key, cosine[at, :], -sine[at, :]
                ).astype(low)
                grad_values[at, columns] = grad_value.astype(low)
            back = jnp.concatenate(turned, axis=0).T * HEAD**-0.5
            for slot in range(2):
                at = pl.ds(pl.multiple_of(place[1 + 2 * count + slot], step), step)
                part = slice(slot * step, (slot + 1) * step)
                grad_query[part, columns] = rotate(
                    back[part], cosine[at, :], -sine[at, :]
                ).astype(low)
        for block in range(blocks, keys.shape[0] // BLOCK):
            at = slice(block * BLOCK, (block + 1) * BLOCK)
            grad_keys[at, :] = jnp.zeros_like(grad_keys[at, :])
            grad_values[at, :] = jnp.zeros_like(grad_values[at, :])

    by_blocks(place[0], keys.shape[0] // BLOCK, visit)
    for index, piece in enumerate(grad_pieces):
        rows = piece.shape[1] // 2
        for slot in range(2):
            at = pl.ds(pl.multiple_of(place[1 + 2 * index + slot], rows), rows)
            piece[0, slot * rows : (slot + 1) * rows, :] = grad_keys[at, :]
            piece[1, slot * rows : (slot + 1) * rows, :] = grad_values[at, :]


def put_messages(to_first, to_second, value):
    span = 2 * to_first.shape[0] // 3
    half = span // 2
    to_first[:span, :] = value[:span]
    to_second[:span, :] = value[span : 2 * span]
    to_first[span:, :] = value[2 * span : 2 * span + half]
    to_second[span:, :] = value[2 * span + half :]


def hidden_tile(normed, cot, w_up, b_up, w_down, result, grad_normed, hidden, grad_hidden):
    count = normed.shape[0]
    step = min(count, 256)
    total = jnp.zeros((1, w_up.shape[1]), full)
    for row in range(0, count, step):
        spot = slice(row, row + step)
        hidden_in = matmul(normed[spot, :], w_up[...]) + b_up[...]
        back = matmul_right(cot[spot, :], w_down[...])
        share = 0.5 * (1.0 + lax.erf(hidden_in * 0.5**0.5))
        item = (hidden_in * share).astype(low)
        slope = share + hidden_in * jnp.exp(-0.5 * hidden_in * hidden_in) * 0.3989422804014327
        grad_item = (back * slope).astype(low)
        hidden[spot, :] = item
        grad_hidden[spot, :] = grad_item
        total += jnp.sum(grad_item.astype(full), axis=0, keepdims=True)
        result[spot, :] += matmul(item, w_down[...])
        grad_normed[spot, :] += matmul_right(grad_item, w_up[...])
    return total


def first_tiles_kernel(
    tiles, own, mixed, first, second, cot_first, cot_second, w_out, b_out, gain, shift,
    w_up, b_up, w_down, middle, result, grad_normed, normed, cot, sent, grad_b_up,
    hidden, grad_hidden,
):
    span = first.shape[0] // 2

    @pl.when(pl.program_id(0) == 0)
    def _():
        cot[...] = join(cot_first[...], cot_second[...], span)
        attended = jnp.concatenate([own[...], mixed[...]], axis=0)
        value = join(first[...], second[...], span).astype(full)
        value = value + matmul(attended, w_out[...]) + b_out[...]
        middle[...] = value
        hat, _ = whiten(value)
        normed[...] = (hat * gain[...] + shift[...]).astype(low)
        result[...] = jnp.zeros_like(result)
        grad_normed[...] = jnp.zeros_like(grad_normed)

    grad_b_up[0:1, :] = hidden_tile(
        normed, cot, w_up, b_up, w_down, result, grad_normed, hidden, grad_hidden
    )
    sent[0, ...] = matmul_left(hidden[...], cot[...]).astype(low)
    sent[1, ...] = matmul_left(normed[...], grad_hidden[...]).astype(low)


def last_tiles_kernel(
    tiles, own, mixed, middle, result_in, grad_normed_in, normed, cot, w_out, gain, w_up, b_up,
    w_down, b_down, kept, grad_b_up, to_first, to_second, grad_middle, grad_own, grad_mixed,
    out_kept, out_sent, rows_out, result, grad_normed, hidden, grad_hidden, grad_out,
):
    @pl.when(pl.program_id(0) == 0)
    def _():
        result[...] = result_in[...]
        grad_normed[...] = grad_normed_in[...]

    grad_b_up[0:1, :] = hidden_tile(
        normed, cot, w_up, b_up, w_down, result, grad_normed, hidden, grad_hidden
    )
    kept[0, ...] = matmul_left(hidden[...], cot[...]).astype(low)
    kept[1, ...] = matmul_left(normed[...], grad_hidden[...]).astype(low)

    @pl.when(pl.program_id(0) == pl.num_programs(0) - 1)
    def _():
        value = middle[...]
        put_messages(to_first, to_second, (value + result[...] + b_down[...]).astype(low))
        hat, scale = whiten(value)
        grad = grad_normed[...]
        cot_full = cot[...].astype(full)
        rows_out[0:1, :] = jnp.sum(cot_full, axis=0, keepdims=True)
        rows_out[2:3, :] = jnp.sum(grad * hat, axis=0, keepdims=True)
        rows_out[3:4, :] = jnp.sum(grad, axis=0, keepdims=True)
        total = cot_full + whiten_back(grad * gain[...], hat, scale)
        rows_out[1:2, :] = jnp.sum(total, axis=0, keepdims=True)
        rows_out[4:8, :] = jnp.zeros_like(rows_out[4:8, :])
        grad_middle[...] = total
        branch = total.astype(low)
        back = matmul_right(branch, w_out[...]).astype(low)
        grad_own[...] = back[: own.shape[0]]
        grad_mixed[...] = back[own.shape[0] :]
        attended = jnp.concatenate([own[...], mixed[...]], axis=0)
        grad_out[...] = matmul_left(attended, branch).astype(low)
        keep_core_half(tiles[2], grad_out, out_kept, out_sent)


def keep_core_half(core, source, kept, sent):
    size = source.shape[0] // 2
    mine = source[pl.ds(pl.multiple_of(core * size, size), size), :]
    theirs = source[pl.ds(pl.multiple_of((1 - core) * size, size), size), :]
    columns = kept.shape[-1]
    for index in range(kept.shape[0]):
        spot = slice(index * columns, (index + 1) * columns)
        kept[index] = mine[:, spot]
        sent[index] = theirs[:, spot]


def halve_kernel(order, kept, received, keep_left, give_left, keep_right, give_right):
    for index, (keep, give) in enumerate(((keep_left, give_left), (keep_right, give_right))):
        for target, half in ((keep, order[1 + index]), (give, 1 - order[1 + index])):
            total = kept[index, half].astype(full) + received[index, half].astype(full)
            target[0] = total.astype(low)


def quarter_kernel(order, kept, received, out_kept, out_received, *targets):
    rows = targets[0].shape[1]
    for index in range(2):
        for target, half in (
            (targets[2 * index], order[1 + index]),
            (targets[2 * index + 1], 1 - order[1 + index]),
        ):
            at = pl.ds(pl.multiple_of((2 * index + half) * rows, rows), rows)
            for lead in range(3):
                total = kept[lead, at, :].astype(full) + received[lead, at, :].astype(full)
                target[lead] = total.astype(low)
            total = out_kept[0, at, :].astype(full) + out_received[0, at, :].astype(full)
            target[3] = total.astype(low)


def stage_kernel(joined, order, *refs):
    count = len(refs) // 5 if not joined else (len(refs) - 3) // 2
    pairs = refs[: 2 * count]
    if joined:
        outs, totals = refs[-3:-1], refs[-1:]
        at = 0
        for index in range(count):
            rows = pairs[2 * index].shape[1]
            totals[0][:, at : at + rows, :] = (
                pairs[2 * index][...].astype(full) + pairs[2 * index + 1][...].astype(full)
            )
            at += rows
    else:
        outs, totals = refs[2 * count : 4 * count], refs[4 * count :]
        for index in range(count):
            totals[index][...] = (
                pairs[2 * index][...].astype(full) + pairs[2 * index + 1][...].astype(full)
            )
    for index, total in enumerate(totals):
        rows = total.shape[1] // 2
        for target, half in ((outs[2 * index], order[index]), (outs[2 * index + 1], 1 - order[index])):
            at = pl.ds(pl.multiple_of(half * rows, rows), rows)
            target[...] = total[:, at, :].astype(low)


def grad_far_kernel(order, kept, received, w_key, w_value, both, grad_far):
    for index in range(2):
        both[index] = (kept[index].astype(full) + received[index].astype(full)).astype(low)
    grad = matmul_right(both[0], w_key[...]) + matmul_right(both[1], w_value[...])
    half = grad.shape[0] // 2
    grad_far[:half, :] = grad[half:].astype(low)
    grad_far[half:, :] = grad[:half].astype(low)


def weight_kernel(
    core, normed, query_own, query_mixed, own_kept, own_received, mixed_kept,
    mixed_received, far, kept, sent, both, rows_out, grad_weight,
):
    item = jnp.concatenate([query_own[...], query_mixed[...]], axis=0)
    count = item.shape[0]
    rows_out[0:1, :] = jnp.sum(item.astype(full), axis=0, keepdims=True)
    grad_weight[...] = matmul_left(normed[:count, :], item).astype(low)
    keep_core_half(core[0], grad_weight, kept.at[0:1], sent.at[0:1])
    for index in range(2):
        own = own_kept[index].astype(full) + own_received[index].astype(full)
        mixed = mixed_kept[index].astype(full) + mixed_received[index].astype(full)
        item = jnp.concatenate([own.astype(low), mixed.astype(low), far[index]], axis=0)
        both[index] = item[:count]
        rows_out[1 + index : 2 + index, :] = jnp.sum(item.astype(full), axis=0, keepdims=True)
        grad_weight[...] = matmul_left(normed[...], item).astype(low)
        keep_core_half(
            core[0], grad_weight, kept.at[1 + index : 2 + index], sent.at[1 + index : 2 + index]
        )
    rows_out[3:8, :] = jnp.zeros_like(rows_out[3:8, :])


def input_kernel(
    core, query_own, query_mixed, both, far, w_query, w_key, w_value, first,
    second, gain, grad_middle, to_first, to_second, rows_out,
):
    span = first.shape[0] // 2
    grad_query = jnp.concatenate([query_own[...], query_mixed[...]], axis=0)
    grad = matmul_right(grad_query, w_query[...])
    for index, weight in enumerate((w_key, w_value)):
        grad = grad + matmul_right(both[index], weight[...])
    grad = jnp.concatenate(
        [grad[: 2 * span], grad[2 * span :] + far[...].astype(full)], axis=0
    )
    hat, scale = whiten(join(first[...], second[...], span).astype(full))
    rows_out[0:1, :] = jnp.sum(grad * hat, axis=0, keepdims=True)
    rows_out[1:2, :] = jnp.sum(grad, axis=0, keepdims=True)
    rows_out[2:8, :] = jnp.zeros_like(rows_out[2:8, :])
    done = (grad_middle[...] + whiten_back(grad * gain[...], hat, scale)).astype(low)
    put_messages(to_first, to_second, done)


def expand_kernel(place, order, *refs):
    sources = refs[:4]
    out = refs[-1]
    choice = 2 * ((pl.program_id(0) // 2) ^ order[0]) + ((pl.program_id(0) % 2) ^ order[place])
    for number, source in enumerate(sources):

        @pl.when(choice == number)
        def _(source=source):
            out[...] = source[0].astype(full)


def expand_mixed_kernel(order, *refs):
    sources, outs = refs[:8], refs[8:]
    index = pl.program_id(0)
    side = (index // 2) % 2
    bit = jnp.where(side == 0, order[1], order[2])
    choice = 4 * side + 2 * ((index // 4) ^ order[0]) + ((index % 2) ^ bit)
    for number, source in enumerate(sources):

        @pl.when(choice == number)
        def _(source=source):
            for place, out in enumerate(outs):
                out[...] = source[place].astype(full)


def after(value, *others):
    return lax.optimization_barrier((value, *others))[0]


def on_device(
    inputs, cotangent, lengths, predicted, norm1_gain, norm1_shift, w_query, b_query, w_key,
    b_key, w_value, b_value, w_out, b_out, norm2_gain, norm2_shift, w_up, b_up, w_down, b_down,
):
    seqs, span, width = inputs.shape
    half = span // 2
    tokens = seqs * span
    hidden_width = w_up.shape[1]
    groups = lax.axis_size("dp")
    assert seqs == 3 and lax.axis_size("seq") == 4 and hidden_width == 4 * width
    bits = [1 << place for place in range(1, groups.bit_length() - 1)]
    group = lax.axis_index("dp")
    depth = lax.axis_index("seq")
    core = group & 1
    side = depth & 1
    pair = depth >> 1
    count = 4 * span
    pairs = width // PAIR
    square = (width, width)

    def bit_of(bit):
        return (group & bit) // bit

    def flip(value, bit):
        return lax.ppermute(value, "dp", [(i, i ^ bit) for i in range(groups)])

    def flip_depth(value, bit):
        return lax.ppermute(value, "seq", [(i, i ^ bit) for i in range(4)])

    def route(turn):
        moves = []
        for at in range(groups):
            for z in range(4):
                to = (at & ~1) | (z & 1)
                to_z = 2 * (at & 1) + (turn ^ (z >> 1))
                moves.append((at * 4 + z, to * 4 + to_z))
        return moves

    def send(value, turn):
        return lax.ppermute(value, ("dp", "seq"), route(turn))

    def send_back(value, turn):
        return lax.ppermute(value, ("dp", "seq"), [(b, a) for a, b in route(turn)])

    first, second = pack(inputs, lengths, 4)
    cot_first, cot_second = pack(after(cotangent, first), lengths, 3)
    first, second = send(first, 0), send(second, 1)
    low_own, high_own, mixed_at = ranks(lengths)
    index = jnp.arange(2 * seqs)
    seq_at = index // 2
    part = index % 2
    from_turn = jnp.where(seq_at == mixed_at, part, (seq_at == high_own).astype(jnp.int32)) ^ pair
    from_row = jnp.where(seq_at == mixed_at, 2, part)
    order_back = jnp.concatenate([from_turn, from_row])

    sibling_lengths = flip(lengths, 1)
    sizes = jnp.where(core == pair, lengths, sibling_lengths)
    low_here, high_here, mixed_here = ranks(sizes)
    own_length = sizes[jnp.where(side == 0, low_here, high_here)]
    mixed_length = sizes[mixed_here]

    def starts(at_side, at_core):
        slots = jnp.arange(2)
        quarter = 2 * (slots ^ at_side) + at_core
        return quarter * span, quarter * span + at_side * half

    own_at, mixed_start = starts(side, core)
    own_sibling, mixed_sibling = starts(side, 1 - core)
    far_start = own_at + (1 - side) * half
    far_sibling = own_sibling + (1 - side) * half
    own_place = jnp.concatenate([own_length[None], own_at, own_sibling, own_at])
    mixed_place = jnp.concatenate(
        [mixed_length[None], mixed_start, mixed_sibling, far_start, far_sibling, mixed_start]
    )
    project_place = jnp.concatenate([own_at, mixed_start, far_start])

    frequency = 10000.0 ** (-jnp.arange(HEAD // 2, dtype=full) / (HEAD // 2))
    angle = jnp.arange(count, dtype=full)[:, None] * frequency[None, :]
    cosine = jnp.tile(jnp.cos(angle), (1, 4))
    sine = jnp.sin(angle)
    sine = jnp.tile(jnp.concatenate([-sine, sine], axis=1), (1, 2))

    def row(vector):
        return vector.reshape(1, -1)

    gain1, shift1 = row(norm1_gain), row(norm1_shift)
    gain2, shift2 = row(norm2_gain), row(norm2_shift)

    def wholes(*items):
        return [whole(item) for item in items]

    extent = tokens + span
    bias_rows = [row(item) for item in (b_query, b_key, b_value, b_out, b_up, b_down)]
    tiles_first = jnp.stack([2 * (1 - core), 2 * (1 - core) + 1])
    tiles_last = jnp.stack([2 * core, 2 * core + 1, core])
    orders = jnp.stack([core, bit_of(bits[0]), bit_of(bits[-1])])
    core_only = core[None]
    sides = [jnp.stack([bit_of(near), bit_of(far)]) for near, far in zip(bits, bits[::-1])]
    sides += [side[None], pair[None]]
    live = (depth * span + jnp.arange(span))[None, :] < lengths[:, None]
    counts = jnp.sum(
        jnp.where(live[:, :, None] & (predicted[:, :, None] == jnp.arange(CLASSES)), 1.0, 0.0),
        axis=(0, 1),
    )
    counts = jnp.pad(counts[None], ((0, 0), (0, width - CLASSES)))
    early = (
        own_place, mixed_place, cosine, sine, bias_rows, gain1, shift1, gain2, shift2, tiles_first,
        tiles_last, orders, core_only, sides, counts, order_back,
    )
    project_place, early, _ = lax.optimization_barrier((project_place, early, cot_first))
    (
        own_place, mixed_place, cosine, sine, bias_rows, gain1, shift1, gain2, shift2, tiles_first,
        tiles_last, orders, core_only, sides, counts, order_back,
    ) = early
    b_query, b_key, b_value, b_out, b_up, b_down = bias_rows
    query, both, normed = call(
        project_kernel,
        (1,),
        project_place,
        wholes(
            first, second, gain1, shift1, w_query, w_key, w_value, b_query, b_key, b_value,
            cosine, sine,
        ),
        wholes(
            fresh((tokens, width), low), fresh((2, extent, width), low), fresh((extent, width), low)
        ),
    )
    both_sibling = flip(both, 1)
    cot_first, cot_second, _ = lax.optimization_barrier((cot_first, cot_second, first))
    cot_first, cot_second = send(cot_first, 0), send(cot_second, 1)

    def columns(array, rows, at, size=PAIR, base=0):
        if len(array.shape) == 2:
            return (array, pl.BlockSpec((rows, size), lambda h, _: (at, base + h)))
        return (array, pl.BlockSpec((2, rows, size), lambda h, _: (0, at, base + h)))

    def own_pieces(*given):
        return [columns(both, 2 * span, 0, *given), columns(both_sibling, 2 * span, 0, *given)]

    def mixed_pieces(*given):
        return [
            columns(both, span, 2, *given),
            columns(both_sibling, span, 2, *given),
            columns(both, span, 3, *given),
            columns(both_sibling, span, 3, *given),
        ]

    def attend(place, rows, at, pieces):
        size = 2 * PAIR
        pieces = pieces(size)
        return call(
            functools.partial(attend_kernel, len(pieces)),
            (width // size,),
            place,
            [columns(query, rows, at, size), *pieces],
            [
                columns(fresh((rows, width), low), rows, 0, size),
                (
                    fresh((pairs, 8, rows), full),
                    pl.BlockSpec((2, 8, rows), lambda h, _: (h, 0, 0)),
                ),
            ],
            [pltpu.VMEM((count, size), low), pltpu.VMEM((count, size), low)],
                )

    own, own_logsum = attend(own_place, 2 * span, 0, own_pieces)
    mixed, mixed_logsum = attend(after(mixed_place, own), span, 2, mixed_pieces)

    def wide(array):
        return (array, pl.BlockSpec(square, lambda j, tiles: (0, tiles[j])))

    def tall(array):
        return (array, pl.BlockSpec(square, lambda j, tiles: (tiles[j], 0)))

    rows_fresh = fresh((8, width), full)

    def tiles_in():
        return [
            wide(w_up),
            (b_up, pl.BlockSpec((1, width), lambda j, tiles: (0, tiles[j]))),
            tall(w_down),
        ]

    def tile_outs():
        return [
            (
                fresh((2, 2, width, width), low),
                pl.BlockSpec((2, None, width, width), lambda j, _: (0, j, 0, 0)),
            ),
            (fresh((2, 8, width), full), pl.BlockSpec((None, 8, width), lambda j, _: (j, 0, 0))),
        ]

    tokens_full = fresh((tokens, width), full)
    tokens_low = fresh((tokens, width), low)
    tile_scratch = [pltpu.VMEM((tokens, width), low), pltpu.VMEM((tokens, width), low)]
    middle, result, grad_normed2, normed2, cot, tiles_sent, b_up_sent = call(
        first_tiles_kernel,
        (2,),
        tiles_first,
        wholes(
            own, mixed, first, second, cot_first, cot_second, w_out, b_out, gain2, shift2
        )
        + tiles_in(),
        wholes(tokens_full, tokens_full, tokens_full, tokens_low, tokens_low) + tile_outs(),
        tile_scratch,
    )
    tiles_received = flip(tiles_sent, 1)
    (
        tiles_kept, b_up_kept, result_first, result_second, grad_middle, grad_own, grad_mixed,
        out_kept, out_sent, rows_middle,
    ) = call(
        last_tiles_kernel,
        (2,),
        tiles_last,
        wholes(own, mixed, middle, result, grad_normed2, normed2, cot, w_out, gain2)
        + tiles_in()
        + wholes(b_down),
        tile_outs()
        + wholes(
            fresh((tokens // 2, width), low), fresh((tokens // 2, width), low), tokens_full,
            fresh((2 * span, width), low), fresh((span, width), low),
            fresh((1, width // 2, width), low), fresh((1, width // 2, width), low), rows_fresh,
        ),
        [pltpu.VMEM((tokens, width), full), pltpu.VMEM((tokens, width), full)]
        + tile_scratch
        + [pltpu.VMEM(square, low)],
    )
    result = [send_back(result_first, 0), send_back(result_second, 1)]
    out_received = flip(out_sent, 1)

    def split(addends, at):
        rows = addends[0].shape[1] // 2

        def part(which):
            items = [
                lax.dynamic_slice_in_dim(item, which * rows, rows, 1).astype(full)
                for item in addends
            ]
            return sum(items[1:], items[0]).astype(low)

        return part(at), part(1 - at)

    def added(addends):
        return (addends[0].astype(full) + addends[1].astype(full)).astype(low)

    def ordered(at, mine, theirs):
        return jnp.where(
            at == 0,
            jnp.concatenate([mine, theirs], axis=1),
            jnp.concatenate([theirs, mine], axis=1),
        )

    def stage(values, at, number, joined=False):
        lead, _, columns_in = values[0][0].shape
        sizes = [item[0].shape[1] for item in values]
        sizes = [sum(sizes)] if joined else sizes
        if any(size % 16 for size in sizes):
            if joined:
                values = [[jnp.concatenate([added(item) for item in values], axis=1)]]
            return [split(item, place) for item, place in zip(values, at)]
        parts = call(
            functools.partial(stage_kernel, joined),
            (1,),
            sides[number],
            wholes(*[part for item in values for part in item]),
            wholes(
                *[fresh((lead, size // 2, columns_in), low) for size in sizes for _ in range(2)]
            ),
            [pltpu.VMEM((lead, size, columns_in), full) for size in sizes],
            room=32,
        )
        return [tuple(parts[2 * place : 2 * place + 2]) for place in range(len(sizes))]

    def chain(parts, orders):
        for step in range(len(bits)):
            if step > 0:
                parts = stage(values, [bit_of(order[step]) for order in orders], step)
            values = yield [
                [keep, flip(give, order[step])] for (keep, give), order in zip(parts, orders)
            ]
        sizes = [item[0].shape[1] for item in values]
        ((keep, give),) = stage(values, [side], -2, joined=True)
        values = yield [[keep, flip_depth(give, 1)]]
        ((keep, give),) = stage(values, [pair], -1)
        (value,) = yield [[keep, flip_depth(give, 2)]]
        total = added(value)
        (value,) = yield [[total, flip_depth(total, 2)]]
        joined = ordered(pair, *value)
        (value,) = yield [[joined, flip_depth(joined, 1)]]
        joined = ordered(side, *value)
        ends = [sum(sizes[: place + 1]) for place in range(len(sizes))]
        values = [joined[:, end - size : end] for end, size in zip(ends, sizes)]
        for step in range(len(bits) - 1, 0, -1):
            values = yield [
                [item, flip(item, order[step])] for item, order in zip(values, orders)
            ]
            values = [
                ordered(bit_of(order[step]), *item) for item, order in zip(values, orders)
            ]
        values = yield [
            [item, flip(item, order[0]), flip(item, 1)] for item, order in zip(values, orders)
        ]
        values = yield [[*item, flip(item[1], 1)] for item in values]
        yield values

    class Chain:
        def __init__(self, left, right):
            self.steps = chain([left, right], [bits, reverse])
            self.state = next(self.steps)
            self.left = 2 * len(bits) + 5

        def here(self):
            return [item[0] for item in self.state]

    def advance(chains, *gates):
        chains = [item for item in chains if item.left > 0]
        states = lax.optimization_barrier(([item.state for item in chains], gates))[0]
        for item, state in zip(chains, states):
            item.state = item.steps.send(state)
            item.left -= 1

    reverse = bits[::-1]

    part = fresh((1, width, width), low)
    parts = call(
        halve_kernel,
        (1,),
        orders,
        wholes(tiles_kept, tiles_received),
        wholes(part, part, part, part),
        room=40,
    )
    tile_sum = Chain(tuple(parts[:2]), tuple(parts[2:]))

    def attend_back(place, rows, at, pieces, grad, out, logsum, size, base, steps):
        given = pieces(size, base)
        group_pairs = size // PAIR
        return call(
            functools.partial(attend_back_kernel, len(given)),
            (steps,),
            place,
            [
                columns(query, rows, at, size, base),
                columns(grad, rows, 0, size, base),
                columns(out, rows, 0, size, base),
                (logsum, pl.BlockSpec((group_pairs, 8, rows), lambda h, _: (base + h, 0, 0))),
                whole(cosine),
                whole(sine),
                *given,
            ],
            [columns(fresh((rows, size * steps), low), rows, 0, size)]
            + [columns(fresh((2, rows, size * steps), low), rows, 0, size) for _ in given],
            [pltpu.VMEM((count, size), low)] * 4,
                )

    query_mixed, mixed_here_grad, mixed_sibling_grad, far_grad, far_sibling_grad = attend_back(
        after(mixed_place, *tile_sum.here()), span, 2, mixed_pieces, grad_mixed, mixed, mixed_logsum,
        2 * PAIR, 0, pairs // 2,
    )
    far_received = flip(far_sibling_grad, 1)
    mixed_received = flip(mixed_sibling_grad, 1)
    result = unpack(after(result[0], query_mixed), result[1], order_back, seqs)
    advance([tile_sum], query_mixed)
    far_both, grad_far = call(
        grad_far_kernel,
        (1,),
        after(core_only, result, *tile_sum.here()),
        wholes(far_grad, far_received, w_key, w_value),
        wholes(fresh((2, span, width), low), fresh((span, width), low)),
    )
    grad_far = flip_depth(grad_far, 1)

    query_own, own_kept, own_sent = attend_back(
        after(own_place, far_both), 2 * span, 0, own_pieces, grad_own, own, own_logsum, 2 * PAIR, 0,
        pairs // 2,
    )
    own_received = flip(own_sent, 1)
    advance([tile_sum], query_own)
    weight_kept, weight_sent, both_grad, rows_weight = call(
        weight_kernel,
        (1,),
        after(core_only, grad_far, *tile_sum.here()),
        wholes(
            normed, query_own, query_mixed, own_kept, own_received, mixed_here_grad,
            mixed_received, far_both,
        ),
        wholes(
            fresh((3, width // 2, width), low), fresh((3, width // 2, width), low),
            fresh((2, tokens, width), low), rows_fresh,
        ),
        [pltpu.VMEM(square, low)],
    )
    weight_received = flip(weight_sent, 1)
    advance([tile_sum], rows_weight)
    weight_kept, weight_received, out_kept, out_received, _ = lax.optimization_barrier(
        (weight_kept, weight_received, out_kept, out_received, tile_sum.here())
    )
    part = fresh((4, width // 8, width), low)
    parts = call(
        quarter_kernel,
        (1,),
        orders,
        wholes(weight_kept, weight_received, out_kept, out_received),
        wholes(part, part, part, part),
        room=32,
    )
    weight_sum = Chain(tuple(parts[:2]), tuple(parts[2:]))
    back_first, back_second, rows_input = call(
        input_kernel,
        (1,),
        after(core_only, *tile_sum.here(), *weight_sum.here()),
        wholes(
            query_own, query_mixed, both_grad, grad_far, w_query, w_key, w_value, first, second,
            gain1, grad_middle,
        ),
        wholes(fresh((tokens // 2, width), low), fresh((tokens // 2, width), low), rows_fresh),
    )

    b_up_kept, b_up_sent, _ = lax.optimization_barrier((b_up_kept, b_up_sent, rows_input))
    b_up_kept, b_up_sent = b_up_kept[:, 0], b_up_sent[:, 0]
    rows_up = jnp.where(
        core == 0,
        jnp.concatenate([b_up_kept, b_up_sent]),
        jnp.concatenate([b_up_sent, b_up_kept]),
    )
    small = jnp.concatenate(
        [rows_middle[:4], rows_up, rows_weight[:3], rows_input[:2], counts], axis=0
    )

    class Small:
        def __init__(self):
            self.moves = [(flip, bit) for bit in (1, *bits)] + [(flip_depth, 1), (flip_depth, 2)]
            self.steps = self
            move, bit = self.moves.pop(0)
            self.state = [[small, move(small, bit)]]
            self.left = len(bits) + 3

        def send(self, state):
            total = state[0][0] + state[0][1]
            if not self.moves:
                return [[total]]
            move, bit = self.moves.pop(0)
            return [[total, move(total, bit)]]
    advance([tile_sum, weight_sum], rows_input)
    small_sum = Small()
    while tile_sum.left > 2:
        advance([weight_sum, small_sum, tile_sum])
    advance([weight_sum, small_sum])
    back_first, back_second, _ = lax.optimization_barrier(
        (back_first, back_second, weight_sum.here())
    )
    back = [send_back(back_first, 0), send_back(back_second, 1)]
    while tile_sum.left > 0:
        advance([weight_sum, small_sum, tile_sum])
    left, right = tile_sum.state
    gate = weight_sum.here()

    def expand(sources, place, shape, target):
        return call(
            functools.partial(expand_kernel, place),
            (4,),
            after(orders, *gate),
            wholes(*sources),
            [(fresh(shape, full), pl.BlockSpec(square, target))],
            room=32,
        )[0]

    grad_w_down = expand(left, 1, (hidden_width, width), lambda i, _: (i, 0))
    grad_w_up = expand(right, 2, (width, hidden_width), lambda i, _: (0, i))
    gates = [grad_w_down, grad_w_up]
    while weight_sum.left > 0 or small_sum.left > 0:
        advance([weight_sum, small_sum], *gates)
        gates = []
    grad_inputs = unpack(back[0], back[1], order_back, seqs)
    left, right = weight_sum.state
    grad_w_query, grad_w_key, grad_w_value, grad_w_out = call(
        expand_mixed_kernel,
        (8,),
        orders,
        wholes(*left, *right),
        [(fresh(square, full), pl.BlockSpec((width // 8, width), lambda i, _: (i, 0)))] * 4,
        room=32,
    )
    small = small_sum.state[0][0]

    return (
        result,
        grad_inputs,
        small[11],
        small[12],
        grad_w_query,
        small[8],
        grad_w_key,
        small[9],
        grad_w_value,
        small[10],
        grad_w_out,
        small[1],
        small[2],
        small[3],
        grad_w_up,
        small[4:8].reshape(-1),
        grad_w_down,
        small[0],
        small[13, :CLASSES].astype(jnp.int32),
    )


def solution(mesh):
    tokens = P("dp", "seq", None)
    return jax.shard_map(
        on_device,
        mesh=mesh,
        in_specs=(tokens, tokens, P("dp"), P("dp", "seq")) + (P(),) * 16,
        out_specs=(tokens, tokens) + (P(),) * 17,
        check_vma=False,
    )
```

```python
import functools

import jax
import jax.numpy as jnp
from jax import lax
from jax.experimental import pallas as pl
from jax.experimental.pallas import tpu as pltpu
from jax.sharding import PartitionSpec as P

HEAD = 64
CLASSES = 70
PAIR = 2 * HEAD
BLOCK = 256

epsilon = 1e-05
low = jnp.bfloat16
full = jnp.float32


def matmul(left, right):
    return lax.dot_general(
        left, right, (((1,), (0,)), ((), ())), preferred_element_type=full
    )


def matmul_left(left, right):
    return lax.dot_general(
        left, right, (((0,), (0,)), ((), ())), preferred_element_type=full
    )


def matmul_right(left, right):
    return lax.dot_general(
        left, right, (((1,), (1,)), ((), ())), preferred_element_type=full
    )


def whiten(value):
    centre = value - jnp.mean(value, axis=-1, keepdims=True)
    scale = lax.rsqrt(jnp.mean(centre * centre, axis=-1, keepdims=True) + epsilon)
    return centre * scale, scale


def whiten_back(grad, hat, scale):
    mean = jnp.mean(grad, axis=-1, keepdims=True)
    along = jnp.mean(grad * hat, axis=-1, keepdims=True)
    return scale * (grad - mean - hat * along)


def rotate(value, cosine, sine):
    lane = lax.broadcasted_iota(jnp.int32, value.shape, 1)
    ahead = pltpu.roll(value, PAIR - HEAD // 2, 1)
    behind = pltpu.roll(value, HEAD // 2, 1)
    swapped = jnp.where(lane % HEAD < HEAD // 2, ahead, behind)
    return value * cosine + swapped * sine


def call(kernel, grid, scalars, inputs, outputs, scratch=(), cost=20, room=60, aliases=None):
    return pl.pallas_call(
        kernel,
        grid_spec=pltpu.PrefetchScalarGridSpec(
            num_scalar_prefetch=1,
            grid=grid,
            in_specs=[spec for _, spec in inputs],
            out_specs=[spec for _, spec in outputs],
            scratch_shapes=list(scratch),
        ),
        out_shape=[shape for shape, _ in outputs],
        input_output_aliases=aliases or {},
        compiler_params=pltpu.CompilerParams(
            dimension_semantics=("arbitrary",) * len(grid), vmem_limit_bytes=room << 20
        ),
        cost_estimate=pl.CostEstimate(
            flops=int(cost * 1e9), transcendentals=0, bytes_accessed=int(cost * 2e6)
        ),
    )(scalars, *[array for array, _ in inputs])


def whole(array):
    rank = len(array.shape)
    return (array, pl.BlockSpec(array.shape, lambda *_: (0,) * rank))


def fresh(shape, kind):
    return jax.ShapeDtypeStruct(shape, kind)


def ranks(sizes):
    one, two, three = sizes[0], sizes[1], sizes[2]
    longest = jnp.where((one >= two) & (one >= three), 0, jnp.where(two >= three, 1, 2))
    return jnp.where(longest == 0, 1, 0), jnp.where(longest == 2, 1, 2), longest


def pack_kernel(sizes, blocks, *refs):
    *targets, sems = refs
    half = blocks.shape[1]
    pair = lax.axis_index("seq") // 2
    low_own, high_own, longest = ranks(sizes)
    copies = []
    for number in range(2):
        side = pair if number == 0 else 1 - pair
        own = jnp.where(side == 0, low_own, high_own)
        near = (2 * own, 2 * own + 1, 2 * longest + side)
        moves = [(spot, targets[number], place) for place, spot in enumerate(near)]
        moves += [(2 * longest + 1 - side, target, 0) for target in targets[2 + number : 3 + number]]
        for place, (spot, target, at) in enumerate(moves):
            copies.append(
                pltpu.make_async_copy(
                    blocks.at[spot], target.at[pl.ds(at * half, half)], sems.at[4 * number + place]
                )
            )
    for copy in copies:
        copy.start()
    for copy in copies:
        copy.wait()


def in_place(array):
    return (array, pl.BlockSpec(memory_space=pl.ANY))


def pack(array, sizes, far):
    seqs, span, width = array.shape
    half = span // 2
    outs = [fresh((3 * half, width), array.dtype)] * 2
    if far:
        outs += [fresh((half, width), array.dtype)] * 2
    return call(
        pack_kernel,
        (1,),
        sizes,
        [in_place(array.reshape(2 * seqs, half, width))],
        [whole(out) for out in outs],
        [pltpu.SemaphoreType.DMA((8,))],
    )


def unpack_kernel(order, first, second, out, sems):
    half = out.shape[1]
    number = out.shape[0]

    def copy(source, index):
        at = pl.ds(pl.multiple_of(order[number + index] * half, half), half)
        return pltpu.make_async_copy(source.at[at], out.at[index], sems.at[index])

    for index in range(number):

        @pl.when(order[index] == 0)
        def _(index=index):
            copy(first, index).start()

        @pl.when(order[index] != 0)
        def _(index=index):
            copy(second, index).start()

    for index in range(number):
        copy(first, index).wait()


def unpack(first, second, order, seqs):
    rows, width = first.shape
    half = rows // seqs
    blocks = call(
        unpack_kernel,
        (1,),
        order,
        [in_place(first), in_place(second)],
        [whole(fresh((2 * seqs, half, width), first.dtype))],
        [pltpu.SemaphoreType.DMA((2 * seqs,))],
        room=12,
    )[0]
    return blocks.reshape(seqs, 2 * half, width)


def join(first, second, span):
    half = span // 2
    return jnp.concatenate(
        [first[:span], second[:span], first[span : span + half], second[span : span + half]],
        axis=0,
    )


def turn_heads(raw, cos, sin):
    columns = range(0, raw.shape[1], PAIR)
    return [rotate(raw[:, at : at + PAIR], cos, sin).astype(low) for at in columns]


def project_kernel(
    place, first, second, gain, shift, w_query, w_key, w_value, b_query, b_key, b_value,
    cosine, sine, query, both, normed,
):
    span = 2 * first.shape[0] // 3
    half = span // 2
    for slot, message in enumerate((first, second)):
        own = slice(slot * span, (slot + 1) * span)
        mixed = slice(2 * span + slot * half, 2 * span + (slot + 1) * half)
        hat, _ = whiten(message[...].astype(full))
        item = (hat * gain[...] + shift[...]).astype(low)
        normed[own, :] = item[:span]
        normed[mixed, :] = item[span:]
        at = pl.ds(pl.multiple_of(place[slot], half), span)
        at_mixed = pl.ds(pl.multiple_of(place[2 + slot], half), half)
        cos = jnp.concatenate([cosine[at, :], cosine[at_mixed, :]], axis=0)
        sin = jnp.concatenate([sine[at, :], sine[at_mixed, :]], axis=0)
        raw = (matmul(item, w_key[...]) + b_key[...]).astype(low).astype(full)
        for index, turned in enumerate(turn_heads(raw, cos, sin)):
            spot = slice(index * PAIR, (index + 1) * PAIR)
            both[0, own, spot] = turned[:span]
            both[0, mixed, spot] = turned[span:]
        raw = (matmul(item, w_value[...]) + b_value[...]).astype(low)
        both[1, own, :] = raw[:span]
        both[1, mixed, :] = raw[span:]
        raw = (matmul(item, w_query[...]) + b_query[...]).astype(low).astype(full)
        for index, turned in enumerate(turn_heads(raw, cos, sin)):
            spot = slice(index * PAIR, (index + 1) * PAIR)
            turned = turned * low(HEAD**-0.5)
            query[own, spot] = turned[:span]
            query[mixed, spot] = turned[span:]


def project_far_kernel(
    place, first, second, gain, shift, w_key, w_value, b_key, b_value, cosine, sine, both, normed
):
    half = first.shape[0]
    message = jnp.concatenate([first[...], second[...]], axis=0)
    hat, _ = whiten(message.astype(full))
    item = (hat * gain[...] + shift[...]).astype(low)
    normed[...] = item
    at = [pl.ds(pl.multiple_of(place[4 + slot], half), half) for slot in range(2)]
    cos = jnp.concatenate([cosine[at[0], :], cosine[at[1], :]], axis=0)
    sin = jnp.concatenate([sine[at[0], :], sine[at[1], :]], axis=0)
    raw = (matmul(item, w_key[...]) + b_key[...]).astype(low).astype(full)
    for index, turned in enumerate(turn_heads(raw, cos, sin)):
        both[0, :, index * PAIR : (index + 1) * PAIR] = turned
    both[1] = (matmul(item, w_value[...]) + b_value[...]).astype(low)


def load_pieces(place, pieces, keys, values):
    for index, piece in enumerate(pieces):
        rows = piece.shape[1] // 2
        for slot in range(2):
            at = pl.ds(pl.multiple_of(place[1 + 2 * index + slot], rows), rows)
            keys[at, :] = piece[0, slot * rows : (slot + 1) * rows, :]
            values[at, :] = piece[1, slot * rows : (slot + 1) * rows, :]


def head_masks(value):
    lane = lax.broadcasted_iota(jnp.int32, value.shape, 1)
    wide = value.astype(full)
    return (
        jnp.where(lane < HEAD, wide, 0.0).astype(low),
        jnp.where(lane < HEAD, 0.0, wide).astype(low),
    )


def by_blocks(length, most, visit):
    number = pl.cdiv(length, BLOCK)
    for blocks in range(1, most + 1):

        @pl.when(number == blocks)
        def _(blocks=blocks):
            visit(blocks, length - (blocks - 1) * BLOCK)


def attend_kernel(count, place, query, *refs):
    pieces = refs[:count]
    out, logsum, keys, values = refs[count:]
    load_pieces(place, pieces, keys, values)
    pairs = [slice(at, at + PAIR) for at in range(0, query.shape[1], PAIR)]

    def visit(blocks, left):
        for pair, columns in enumerate(pairs):
            masked = head_masks(query[:, columns])
            value = values[: blocks * BLOCK, columns].T
            mixed = []
            for head in range(2):
                spot = slice(head * HEAD, (head + 1) * HEAD)
                scores = []
                for block in range(blocks):
                    key = keys[block * BLOCK : (block + 1) * BLOCK, columns]
                    item = matmul_right(key, masked[head])
                    if block == blocks - 1:
                        index = lax.broadcasted_iota(jnp.int32, item.shape, 0)
                        item = jnp.where(index < left, item, -1e30)
                    scores.append(item)
                peaks = [jnp.max(item, axis=0, keepdims=True) for item in scores]
                peak = functools.reduce(jnp.maximum, peaks)
                weights = [jnp.exp(item - peak) for item in scores]
                total = sum(jnp.sum(item, axis=0, keepdims=True) for item in weights)
                product = sum(
                    matmul(value[spot, block * BLOCK : (block + 1) * BLOCK], item.astype(low))
                    for block, item in enumerate(weights)
                )
                mixed.append(product / total)
                logsum[pair, head : head + 1, :] = peak + jnp.log(total)
            out[:, columns] = jnp.concatenate(mixed, axis=0).T.astype(low)

    by_blocks(place[0], keys.shape[0] // BLOCK, visit)


def attend_back_kernel(count, place, query, grad, mixed, logsum, cosine, sine, *refs):
    pieces = refs[:count]
    grad_query, *grad_pieces = refs[count : 1 + 2 * count]
    keys, values, grad_keys, grad_values = refs[1 + 2 * count :]
    load_pieces(place, pieces, keys, values)
    rows = query.shape[0]
    step = rows // 2
    pairs = [slice(at, at + PAIR) for at in range(0, query.shape[1], PAIR)]

    def visit(blocks, left):
        for pair, columns in enumerate(pairs):
            grad_low = grad[:, columns]
            masked = head_masks(query[:, columns])
            masked_grad = head_masks(grad_low)
            inner = (grad_low.astype(full) * mixed[:, columns].astype(full)).T
            delta = [
                jnp.sum(inner[head * HEAD : (head + 1) * HEAD, :], axis=0, keepdims=True)
                for head in range(2)
            ]
            turned = [0.0, 0.0]
            for block in range(blocks):
                at = slice(block * BLOCK, (block + 1) * BLOCK)
                key = keys[at, columns]
                value = values[at, columns]
                flat = key.T
                grad_key = 0.0
                grad_value = 0.0
                for head in range(2):
                    scores = matmul_right(key, masked[head])
                    weights = jnp.exp(scores - logsum[pair, head : head + 1, :])
                    if block == blocks - 1:
                        index = lax.broadcasted_iota(jnp.int32, scores.shape, 0)
                        weights = jnp.where(index < left, weights, 0.0)
                    grad_weights = matmul_right(value, masked_grad[head])
                    grad_scores = (weights * (grad_weights - delta[head])).astype(low)
                    grad_value += matmul(weights.astype(low), masked_grad[head])
                    grad_key += matmul(grad_scores, masked[head])
                    turned[head] += matmul(flat[head * HEAD : (head + 1) * HEAD, :], grad_scores)
                grad_keys[at, columns] = rotate(
                    grad_key, cosine[at, :], -sine[at, :]
                ).astype(low)
                grad_values[at, columns] = grad_value.astype(low)
            back = jnp.concatenate(turned, axis=0).T * HEAD**-0.5
            for slot in range(2):
                at = pl.ds(pl.multiple_of(place[1 + 2 * count + slot], step), step)
                part = slice(slot * step, (slot + 1) * step)
                grad_query[part, columns] = rotate(
                    back[part], cosine[at, :], -sine[at, :]
                ).astype(low)
        for block in range(blocks, keys.shape[0] // BLOCK):
            at = slice(block * BLOCK, (block + 1) * BLOCK)
            grad_keys[at, :] = jnp.zeros_like(grad_keys[at, :])
            grad_values[at, :] = jnp.zeros_like(grad_values[at, :])

    by_blocks(place[0], keys.shape[0] // BLOCK, visit)
    for index, piece in enumerate(grad_pieces):
        rows = piece.shape[1] // 2
        for slot in range(2):
            at = pl.ds(pl.multiple_of(place[1 + 2 * index + slot], rows), rows)
            piece[0, slot * rows : (slot + 1) * rows, :] = grad_keys[at, :]
            piece[1, slot * rows : (slot + 1) * rows, :] = grad_values[at, :]


def put_messages(to_first, to_second, value):
    span = 2 * to_first.shape[0] // 3
    half = span // 2
    to_first[:span, :] = value[:span]
    to_second[:span, :] = value[span : 2 * span]
    to_first[span:, :] = value[2 * span : 2 * span + half]
    to_second[span:, :] = value[2 * span + half :]


def hidden_tile(normed, cot, w_up, b_up, w_down, result, grad_normed, hidden, grad_hidden):
    count = normed.shape[0]
    step = min(count, 256)
    total = jnp.zeros((1, w_up.shape[1]), full)
    for row in range(0, count, step):
        spot = slice(row, row + step)
        hidden_in = matmul(normed[spot, :], w_up[...]) + b_up[...]
        back = matmul_right(cot[spot, :], w_down[...])
        share = 0.5 * (1.0 + lax.erf(hidden_in * 0.5**0.5))
        item = (hidden_in * share).astype(low)
        slope = share + hidden_in * jnp.exp(-0.5 * hidden_in * hidden_in) * 0.3989422804014327
        grad_item = (back * slope).astype(low)
        hidden[spot, :] = item
        grad_hidden[spot, :] = grad_item
        total += jnp.sum(grad_item.astype(full), axis=0, keepdims=True)
        result[spot, :] += matmul(item, w_down[...])
        grad_normed[spot, :] += matmul_right(grad_item, w_up[...])
    return total


def first_tiles_kernel(
    tiles, own, mixed, first, second, cot_first, cot_second, w_out, b_out, gain, shift,
    w_up, b_up, w_down, middle, result, grad_normed, normed, cot, sent, grad_b_up,
    hidden, grad_hidden,
):
    span = 2 * first.shape[0] // 3

    @pl.when(pl.program_id(0) == 0)
    def _():
        cot[...] = join(cot_first[...], cot_second[...], span)
        attended = jnp.concatenate([own[...], mixed[...]], axis=0)
        value = join(first[...], second[...], span).astype(full)
        value = value + matmul(attended, w_out[...]) + b_out[...]
        middle[...] = value
        hat, _ = whiten(value)
        normed[...] = (hat * gain[...] + shift[...]).astype(low)
        result[...] = jnp.zeros_like(result)
        grad_normed[...] = jnp.zeros_like(grad_normed)

    grad_b_up[0:1, :] = hidden_tile(
        normed, cot, w_up, b_up, w_down, result, grad_normed, hidden, grad_hidden
    )
    sent[0, ...] = matmul_left(hidden[...], cot[...]).astype(low)
    sent[1, ...] = matmul_left(normed[...], grad_hidden[...]).astype(low)


def last_tiles_kernel(
    tiles, own, mixed, middle, result_in, grad_normed_in, normed, cot, w_out, gain, w_up, b_up,
    w_down, b_down, kept, grad_b_up, to_first, to_second, grad_middle, grad_own, grad_mixed,
    out_kept, out_sent, rows_out, result, grad_normed, hidden, grad_hidden, grad_out,
):
    @pl.when(pl.program_id(0) == 0)
    def _():
        result[...] = result_in[...]
        grad_normed[...] = grad_normed_in[...]

    grad_b_up[0:1, :] = hidden_tile(
        normed, cot, w_up, b_up, w_down, result, grad_normed, hidden, grad_hidden
    )
    kept[0, ...] = matmul_left(hidden[...], cot[...]).astype(low)
    kept[1, ...] = matmul_left(normed[...], grad_hidden[...]).astype(low)

    @pl.when(pl.program_id(0) == pl.num_programs(0) - 1)
    def _():
        value = middle[...]
        put_messages(to_first, to_second, (value + result[...] + b_down[...]).astype(low))
        hat, scale = whiten(value)
        grad = grad_normed[...]
        cot_full = cot[...].astype(full)
        rows_out[0:1, :] = jnp.sum(cot_full, axis=0, keepdims=True)
        rows_out[2:3, :] = jnp.sum(grad * hat, axis=0, keepdims=True)
        rows_out[3:4, :] = jnp.sum(grad, axis=0, keepdims=True)
        total = cot_full + whiten_back(grad * gain[...], hat, scale)
        rows_out[1:2, :] = jnp.sum(total, axis=0, keepdims=True)
        rows_out[4:8, :] = jnp.zeros_like(rows_out[4:8, :])
        grad_middle[...] = total
        branch = total.astype(low)
        back = matmul_right(branch, w_out[...]).astype(low)
        grad_own[...] = back[: own.shape[0]]
        grad_mixed[...] = back[own.shape[0] :]
        attended = jnp.concatenate([own[...], mixed[...]], axis=0)
        grad_out[...] = matmul_left(attended, branch).astype(low)
        keep_core_half(tiles[2], grad_out, out_kept, out_sent)


def keep_core_half(core, source, kept, sent):
    size = source.shape[0] // 2
    mine = source[pl.ds(pl.multiple_of(core * size, size), size), :]
    theirs = source[pl.ds(pl.multiple_of((1 - core) * size, size), size), :]
    columns = kept.shape[-1]
    for index in range(kept.shape[0]):
        spot = slice(index * columns, (index + 1) * columns)
        kept[index] = mine[:, spot]
        sent[index] = theirs[:, spot]


def halve_kernel(order, kept, received, keep_left, give_left, keep_right, give_right):
    for index, (keep, give) in enumerate(((keep_left, give_left), (keep_right, give_right))):
        for target, half in ((keep, order[1 + index]), (give, 1 - order[1 + index])):
            total = kept[index, half].astype(full) + received[index, half].astype(full)
            target[0] = total.astype(low)


def quarter_kernel(order, kept, received, out_kept, out_received, *targets):
    rows = targets[0].shape[1]
    for index in range(2):
        for target, half in (
            (targets[2 * index], order[1 + index]),
            (targets[2 * index + 1], 1 - order[1 + index]),
        ):
            at = pl.ds(pl.multiple_of((2 * index + half) * rows, rows), rows)
            for lead in range(3):
                total = kept[lead, at, :].astype(full) + received[lead, at, :].astype(full)
                target[lead] = total.astype(low)
            total = out_kept[0, at, :].astype(full) + out_received[0, at, :].astype(full)
            target[3] = total.astype(low)


def stage_kernel(joined, order, *refs):
    count = len(refs) // 5 if not joined else (len(refs) - 3) // 2
    pairs = refs[: 2 * count]
    if joined:
        outs, totals = refs[-3:-1], refs[-1:]
        at = 0
        for index in range(count):
            rows = pairs[2 * index].shape[1]
            totals[0][:, at : at + rows, :] = (
                pairs[2 * index][...].astype(full) + pairs[2 * index + 1][...].astype(full)
            )
            at += rows
    else:
        outs, totals = refs[2 * count : 4 * count], refs[4 * count :]
        for index in range(count):
            totals[index][...] = (
                pairs[2 * index][...].astype(full) + pairs[2 * index + 1][...].astype(full)
            )
    for index, total in enumerate(totals):
        rows = total.shape[1] // 2
        for target, half in ((outs[2 * index], order[index]), (outs[2 * index + 1], 1 - order[index])):
            at = pl.ds(pl.multiple_of(half * rows, rows), rows)
            target[...] = total[:, at, :].astype(low)


def grad_far_kernel(order, kept, received, w_key, w_value, both, grad_far):
    for index in range(2):
        both[index] = (kept[index].astype(full) + received[index].astype(full)).astype(low)
    grad = matmul_right(both[0], w_key[...]) + matmul_right(both[1], w_value[...])
    half = grad.shape[0] // 2
    grad_far[:half, :] = grad[half:].astype(low)
    grad_far[half:, :] = grad[:half].astype(low)


def weight_kernel(
    core, normed, normed_far, query_own, query_mixed, own_kept, own_received, mixed_kept,
    mixed_received, far, kept, sent, both, rows_out, grad_weight,
):
    item = jnp.concatenate([query_own[...], query_mixed[...]], axis=0)
    count = item.shape[0]
    rows_out[0:1, :] = jnp.sum(item.astype(full), axis=0, keepdims=True)
    grad_weight[...] = matmul_left(normed[...], item).astype(low)
    keep_core_half(core[0], grad_weight, kept.at[0:1], sent.at[0:1])
    rows = jnp.concatenate([normed[...], normed_far[...]], axis=0)
    for index in range(2):
        own = own_kept[index].astype(full) + own_received[index].astype(full)
        mixed = mixed_kept[index].astype(full) + mixed_received[index].astype(full)
        item = jnp.concatenate([own.astype(low), mixed.astype(low), far[index]], axis=0)
        both[index] = item[:count]
        rows_out[1 + index : 2 + index, :] = jnp.sum(item.astype(full), axis=0, keepdims=True)
        grad_weight[...] = matmul_left(rows, item).astype(low)
        keep_core_half(
            core[0], grad_weight, kept.at[1 + index : 2 + index], sent.at[1 + index : 2 + index]
        )
    rows_out[3:8, :] = jnp.zeros_like(rows_out[3:8, :])


def input_kernel(
    core, query_own, query_mixed, both, far, w_query, w_key, w_value, first,
    second, gain, grad_middle, to_first, to_second, rows_out,
):
    span = 2 * first.shape[0] // 3
    grad_query = jnp.concatenate([query_own[...], query_mixed[...]], axis=0)
    grad = matmul_right(grad_query, w_query[...])
    for index, weight in enumerate((w_key, w_value)):
        grad = grad + matmul_right(both[index], weight[...])
    grad = jnp.concatenate(
        [grad[: 2 * span], grad[2 * span :] + far[...].astype(full)], axis=0
    )
    hat, scale = whiten(join(first[...], second[...], span).astype(full))
    rows_out[0:1, :] = jnp.sum(grad * hat, axis=0, keepdims=True)
    rows_out[1:2, :] = jnp.sum(grad, axis=0, keepdims=True)
    rows_out[2:8, :] = jnp.zeros_like(rows_out[2:8, :])
    done = (grad_middle[...] + whiten_back(grad * gain[...], hat, scale)).astype(low)
    put_messages(to_first, to_second, done)


def expand_kernel(place, order, *refs):
    sources = refs[:4]
    out = refs[-1]
    choice = 2 * ((pl.program_id(0) // 2) ^ order[0]) + ((pl.program_id(0) % 2) ^ order[place])
    for number, source in enumerate(sources):

        @pl.when(choice == number)
        def _(source=source):
            out[...] = source[0].astype(full)


def expand_mixed_kernel(order, *refs):
    sources, outs = refs[:8], refs[8:]
    index = pl.program_id(0)
    side = (index // 2) % 2
    bit = jnp.where(side == 0, order[1], order[2])
    choice = 4 * side + 2 * ((index // 4) ^ order[0]) + ((index % 2) ^ bit)
    for number, source in enumerate(sources):

        @pl.when(choice == number)
        def _(source=source):
            for place, out in enumerate(outs):
                out[...] = source[place].astype(full)


def after(value, *others):
    return lax.optimization_barrier((value, *others))[0]


def on_device(
    inputs, cotangent, lengths, predicted, norm1_gain, norm1_shift, w_query, b_query, w_key,
    b_key, w_value, b_value, w_out, b_out, norm2_gain, norm2_shift, w_up, b_up, w_down, b_down,
):
    seqs, span, width = inputs.shape
    half = span // 2
    tokens = seqs * span
    hidden_width = w_up.shape[1]
    groups = lax.axis_size("dp")
    assert seqs == 3 and lax.axis_size("seq") == 4 and hidden_width == 4 * width
    bits = [1 << place for place in range(1, groups.bit_length() - 1)]
    group = lax.axis_index("dp")
    depth = lax.axis_index("seq")
    core = group & 1
    side = depth & 1
    pair = depth >> 1
    count = 4 * span
    pairs = width // PAIR
    square = (width, width)

    def bit_of(bit):
        return (group & bit) // bit

    def flip(value, bit):
        return lax.ppermute(value, "dp", [(i, i ^ bit) for i in range(groups)])

    def flip_depth(value, bit):
        return lax.ppermute(value, "seq", [(i, i ^ bit) for i in range(4)])

    def route(turn):
        moves = []
        for at in range(groups):
            for z in range(4):
                to = (at & ~1) | ((z & 1) ^ 1 ^ turn)
                to_z = 2 * (at & 1) + (turn ^ (z >> 1))
                moves.append((at * 4 + z, to * 4 + to_z))
        return moves

    def cross(value):
        moves = [
            (at * 4 + z, (at ^ 1) * 4 + (z ^ 1)) for at in range(groups) for z in range(4)
        ]
        return lax.ppermute(value, ("dp", "seq"), moves)

    def send(value, turn):
        return lax.ppermute(value, ("dp", "seq"), route(turn))

    def send_back(value, turn):
        return lax.ppermute(value, ("dp", "seq"), [(b, a) for a, b in route(turn)])

    first, second, *far_rows = pack(inputs, lengths, True)
    cot_first, cot_second = pack(after(cotangent, first), lengths, False)
    first, second = send(first, 0), send(second, 1)
    first, second, far_rows = lax.optimization_barrier((first, second, far_rows))
    far_rows = [send(item, turn) for turn, item in enumerate(far_rows)]
    low_own, high_own, mixed_at = ranks(lengths)
    index = jnp.arange(2 * seqs)
    seq_at = index // 2
    part = index % 2
    from_turn = jnp.where(seq_at == mixed_at, part, (seq_at == high_own).astype(jnp.int32)) ^ pair
    from_row = jnp.where(seq_at == mixed_at, 2, part)
    order_back = jnp.concatenate([from_turn, from_row])

    sibling_lengths = flip(lengths, 1)
    sizes = jnp.where(core == pair, lengths, sibling_lengths)
    low_here, high_here, mixed_here = ranks(sizes)
    own_length = sizes[jnp.where(side == 0, low_here, high_here)]
    mixed_length = sizes[mixed_here]

    def starts(at_side, at_core):
        slots = jnp.arange(2)
        quarter = 2 * (slots ^ at_side) + (at_core ^ 1 ^ slots)
        return quarter * span, quarter * span + at_side * half

    own_at, mixed_start = starts(side, core)
    own_sibling, mixed_sibling = starts(side, 1 - core)
    far_start = own_at + (1 - side) * half
    far_sibling_start = own_sibling + (1 - side) * half
    own_place = jnp.concatenate([own_length[None], own_at, own_sibling, own_at])
    mixed_place = jnp.concatenate(
        [mixed_length[None], mixed_start, mixed_sibling, far_start, far_sibling_start, mixed_start]
    )
    project_place = jnp.concatenate([own_at, mixed_start, far_start])

    frequency = 10000.0 ** (-jnp.arange(HEAD // 2, dtype=full) / (HEAD // 2))
    angle = jnp.arange(count, dtype=full)[:, None] * frequency[None, :]
    cosine = jnp.tile(jnp.cos(angle), (1, 4))
    sine = jnp.sin(angle)
    sine = jnp.tile(jnp.concatenate([-sine, sine], axis=1), (1, 2))

    def row(vector):
        return vector.reshape(1, -1)

    gain1, shift1 = row(norm1_gain), row(norm1_shift)
    gain2, shift2 = row(norm2_gain), row(norm2_shift)

    def wholes(*items):
        return [whole(item) for item in items]

    bias_rows = [row(item) for item in (b_query, b_key, b_value, b_out, b_up, b_down)]
    tiles_first = jnp.stack([2 * (1 - core), 2 * (1 - core) + 1])
    tiles_last = jnp.stack([2 * core, 2 * core + 1, core])
    orders = jnp.stack([core, bit_of(bits[0]), bit_of(bits[-1])])
    core_only = core[None]
    sides = [jnp.stack([bit_of(near), bit_of(far)]) for near, far in zip(bits, bits[::-1])]
    sides += [side[None], pair[None]]
    live = (depth * span + jnp.arange(span))[None, :] < lengths[:, None]
    counts = jnp.sum(
        jnp.where(live[:, :, None] & (predicted[:, :, None] == jnp.arange(CLASSES)), 1.0, 0.0),
        axis=(0, 1),
    )
    counts = jnp.pad(counts[None], ((0, 0), (0, width - CLASSES)))
    early = (
        own_place, mixed_place, cosine, sine, bias_rows, gain1, shift1, gain2, shift2, tiles_first,
        tiles_last, orders, core_only, sides, counts, order_back,
    )
    project_place, early, _ = lax.optimization_barrier((project_place, early, cot_first))
    (
        own_place, mixed_place, cosine, sine, bias_rows, gain1, shift1, gain2, shift2, tiles_first,
        tiles_last, orders, core_only, sides, counts, order_back,
    ) = early
    b_query, b_key, b_value, b_out, b_up, b_down = bias_rows
    query, both, normed = call(
        project_kernel,
        (1,),
        project_place,
        wholes(
            first, second, gain1, shift1, w_query, w_key, w_value, b_query, b_key, b_value,
            cosine, sine,
        ),
        wholes(
            fresh((tokens, width), low), fresh((2, tokens, width), low), fresh((tokens, width), low)
        ),
    )
    both, far_rows = lax.optimization_barrier((both, far_rows))
    both_sibling = flip(both, 1)
    far, normed_far = call(
        project_far_kernel,
        (1,),
        after(project_place, query),
        wholes(*far_rows, gain1, shift1, w_key, w_value, b_key, b_value, cosine, sine),
        wholes(fresh((2, span, width), low), fresh((span, width), low)),
    )
    far_sibling = flip(far, 1)
    cot_first, cot_second, _ = lax.optimization_barrier((cot_first, cot_second, far))
    cot_first, cot_second = send(cot_first, 0), send(cot_second, 1)

    def columns(array, rows, at, size=PAIR, base=0):
        if len(array.shape) == 2:
            return (array, pl.BlockSpec((rows, size), lambda h, _: (at, base + h)))
        return (array, pl.BlockSpec((2, rows, size), lambda h, _: (0, at, base + h)))

    def own_pieces(*given):
        return [columns(both, 2 * span, 0, *given), columns(both_sibling, 2 * span, 0, *given)]

    def mixed_pieces(*given):
        return [
            columns(both, span, 2, *given),
            columns(both_sibling, span, 2, *given),
            columns(far, span, 0, *given),
            columns(far_sibling, span, 0, *given),
        ]

    def attend(place, rows, at, pieces):
        size = 2 * PAIR
        pieces = pieces(size)
        return call(
            functools.partial(attend_kernel, len(pieces)),
            (width // size,),
            place,
            [columns(query, rows, at, size), *pieces],
            [
                columns(fresh((rows, width), low), rows, 0, size),
                (
                    fresh((pairs, 8, rows), full),
                    pl.BlockSpec((2, 8, rows), lambda h, _: (h, 0, 0)),
                ),
            ],
            [pltpu.VMEM((count, size), low), pltpu.VMEM((count, size), low)],
                )

    own, own_logsum = attend(after(own_place, far), 2 * span, 0, own_pieces)
    mixed, mixed_logsum = attend(after(mixed_place, own), span, 2, mixed_pieces)

    def wide(array):
        return (array, pl.BlockSpec(square, lambda j, tiles: (0, tiles[j])))

    def tall(array):
        return (array, pl.BlockSpec(square, lambda j, tiles: (tiles[j], 0)))

    rows_fresh = fresh((8, width), full)

    def tiles_in():
        return [
            wide(w_up),
            (b_up, pl.BlockSpec((1, width), lambda j, tiles: (0, tiles[j]))),
            tall(w_down),
        ]

    def tile_outs():
        return [
            (
                fresh((2, 2, width, width), low),
                pl.BlockSpec((2, None, width, width), lambda j, _: (0, j, 0, 0)),
            ),
            (fresh((2, 8, width), full), pl.BlockSpec((None, 8, width), lambda j, _: (j, 0, 0))),
        ]

    tokens_full = fresh((tokens, width), full)
    tokens_low = fresh((tokens, width), low)
    tile_scratch = [pltpu.VMEM((tokens, width), low), pltpu.VMEM((tokens, width), low)]
    middle, result, grad_normed2, normed2, cot, tiles_sent, b_up_sent = call(
        first_tiles_kernel,
        (2,),
        tiles_first,
        wholes(
            own, mixed, first, second, cot_first, cot_second, w_out, b_out, gain2, shift2
        )
        + tiles_in(),
        wholes(tokens_full, tokens_full, tokens_full, tokens_low, tokens_low) + tile_outs(),
        tile_scratch,
    )
    tiles_received = flip(tiles_sent, 1)
    (
        tiles_kept, b_up_kept, result_first, result_second, grad_middle, grad_own, grad_mixed,
        out_kept, out_sent, rows_middle,
    ) = call(
        last_tiles_kernel,
        (2,),
        tiles_last,
        wholes(own, mixed, middle, result, grad_normed2, normed2, cot, w_out, gain2)
        + tiles_in()
        + wholes(b_down),
        tile_outs()
        + wholes(
            fresh((tokens // 2, width), low), fresh((tokens // 2, width), low), tokens_full,
            fresh((2 * span, width), low), fresh((span, width), low),
            fresh((1, width // 2, width), low), fresh((1, width // 2, width), low), rows_fresh,
        ),
        [pltpu.VMEM((tokens, width), full), pltpu.VMEM((tokens, width), full)]
        + tile_scratch
        + [pltpu.VMEM(square, low)],
    )
    result = [send_back(result_first, 0), send_back(result_second, 1)]
    out_received = flip(out_sent, 1)

    def split(addends, at):
        rows = addends[0].shape[1] // 2

        def part(which):
            items = [
                lax.dynamic_slice_in_dim(item, which * rows, rows, 1).astype(full)
                for item in addends
            ]
            return sum(items[1:], items[0]).astype(low)

        return part(at), part(1 - at)

    def added(addends):
        return (addends[0].astype(full) + addends[1].astype(full)).astype(low)

    def ordered(at, mine, theirs):
        return jnp.where(
            at == 0,
            jnp.concatenate([mine, theirs], axis=1),
            jnp.concatenate([theirs, mine], axis=1),
        )

    def stage(values, at, number, joined=False):
        lead, _, columns_in = values[0][0].shape
        sizes = [item[0].shape[1] for item in values]
        sizes = [sum(sizes)] if joined else sizes
        if any(size % 16 for size in sizes):
            if joined:
                values = [[jnp.concatenate([added(item) for item in values], axis=1)]]
            return [split(item, place) for item, place in zip(values, at)]
        parts = call(
            functools.partial(stage_kernel, joined),
            (1,),
            sides[number],
            wholes(*[part for item in values for part in item]),
            wholes(
                *[fresh((lead, size // 2, columns_in), low) for size in sizes for _ in range(2)]
            ),
            [pltpu.VMEM((lead, size, columns_in), full) for size in sizes],
            room=32,
        )
        return [tuple(parts[2 * place : 2 * place + 2]) for place in range(len(sizes))]

    def chain(parts, orders):
        for step in range(len(bits)):
            if step > 0:
                parts = stage(values, [bit_of(order[step]) for order in orders], step)
            values = yield [
                [keep, flip(give, order[step])] for (keep, give), order in zip(parts, orders)
            ]
        sizes = [item[0].shape[1] for item in values]
        ((keep, give),) = stage(values, [side], -2, joined=True)
        values = yield [[keep, flip_depth(give, 1)]]
        ((keep, give),) = stage(values, [pair], -1)
        (value,) = yield [[keep, flip_depth(give, 2)]]
        total = added(value)
        (value,) = yield [[total, flip_depth(total, 2)]]
        joined = ordered(pair, *value)
        (value,) = yield [[joined, flip_depth(joined, 1)]]
        joined = ordered(side, *value)
        ends = [sum(sizes[: place + 1]) for place in range(len(sizes))]
        values = [joined[:, end - size : end] for end, size in zip(ends, sizes)]
        for step in range(len(bits) - 1, 0, -1):
            values = yield [
                [item, flip(item, order[step])] for item, order in zip(values, orders)
            ]
            values = [
                ordered(bit_of(order[step]), *item) for item, order in zip(values, orders)
            ]
        values = yield [
            [item, flip(item, order[0]), flip(item, 1)] for item, order in zip(values, orders)
        ]
        values = yield [[*item, flip(item[1], 1)] for item in values]
        yield values

    class Chain:
        def __init__(self, left, right):
            self.steps = chain([left, right], [bits, reverse])
            self.state = next(self.steps)
            self.left = 2 * len(bits) + 5

        def here(self):
            return [item[0] for item in self.state]

    def advance(chains, *gates):
        chains = [item for item in chains if item.left > 0]
        states = lax.optimization_barrier(([item.state for item in chains], gates))[0]
        for item, state in zip(chains, states):
            item.state = item.steps.send(state)
            item.left -= 1

    reverse = bits[::-1]

    part = fresh((1, width, width), low)
    parts = call(
        halve_kernel,
        (1,),
        orders,
        wholes(tiles_kept, tiles_received),
        wholes(part, part, part, part),
        room=40,
    )
    tile_sum = Chain(tuple(parts[:2]), tuple(parts[2:]))

    def attend_back(place, rows, at, pieces, grad, out, logsum, size, base, steps):
        given = pieces(size, base)
        group_pairs = size // PAIR
        return call(
            functools.partial(attend_back_kernel, len(given)),
            (steps,),
            place,
            [
                columns(query, rows, at, size, base),
                columns(grad, rows, 0, size, base),
                columns(out, rows, 0, size, base),
                (logsum, pl.BlockSpec((group_pairs, 8, rows), lambda h, _: (base + h, 0, 0))),
                whole(cosine),
                whole(sine),
                *given,
            ],
            [columns(fresh((rows, size * steps), low), rows, 0, size)]
            + [columns(fresh((2, rows, size * steps), low), rows, 0, size) for _ in given],
            [pltpu.VMEM((count, size), low)] * 4,
                )

    query_mixed, mixed_here_grad, mixed_sibling_grad, far_grad, far_sibling_grad = attend_back(
        after(mixed_place, *tile_sum.here()), span, 2, mixed_pieces, grad_mixed, mixed, mixed_logsum,
        2 * PAIR, 0, pairs // 2,
    )
    far_received = flip(far_sibling_grad, 1)
    mixed_received = flip(mixed_sibling_grad, 1)
    result = unpack(after(result[0], query_mixed), result[1], order_back, seqs)
    advance([tile_sum], query_mixed)
    far_both, grad_far = call(
        grad_far_kernel,
        (1,),
        after(core_only, result, *tile_sum.here()),
        wholes(far_grad, far_received, w_key, w_value),
        wholes(fresh((2, span, width), low), fresh((span, width), low)),
    )
    grad_far = cross(grad_far)

    query_own, own_kept, own_sent = attend_back(
        after(own_place, far_both), 2 * span, 0, own_pieces, grad_own, own, own_logsum, 2 * PAIR, 0,
        pairs // 2,
    )
    own_received = flip(own_sent, 1)
    advance([tile_sum], query_own)
    weight_kept, weight_sent, both_grad, rows_weight = call(
        weight_kernel,
        (1,),
        after(core_only, grad_far, *tile_sum.here()),
        wholes(
            normed, normed_far, query_own, query_mixed, own_kept, own_received, mixed_here_grad,
            mixed_received, far_both,
        ),
        wholes(
            fresh((3, width // 2, width), low), fresh((3, width // 2, width), low),
            fresh((2, tokens, width), low), rows_fresh,
        ),
        [pltpu.VMEM(square, low)],
    )
    weight_received = flip(weight_sent, 1)
    advance([tile_sum], rows_weight)
    weight_kept, weight_received, out_kept, out_received, _ = lax.optimization_barrier(
        (weight_kept, weight_received, out_kept, out_received, tile_sum.here())
    )
    part = fresh((4, width // 8, width), low)
    parts = call(
        quarter_kernel,
        (1,),
        orders,
        wholes(weight_kept, weight_received, out_kept, out_received),
        wholes(part, part, part, part),
        room=32,
    )
    weight_sum = Chain(tuple(parts[:2]), tuple(parts[2:]))
    back_first, back_second, rows_input = call(
        input_kernel,
        (1,),
        after(core_only, *tile_sum.here(), *weight_sum.here()),
        wholes(
            query_own, query_mixed, both_grad, grad_far, w_query, w_key, w_value, first, second,
            gain1, grad_middle,
        ),
        wholes(fresh((tokens // 2, width), low), fresh((tokens // 2, width), low), rows_fresh),
    )

    b_up_kept, b_up_sent, _ = lax.optimization_barrier((b_up_kept, b_up_sent, rows_input))
    b_up_kept, b_up_sent = b_up_kept[:, 0], b_up_sent[:, 0]
    rows_up = jnp.where(
        core == 0,
        jnp.concatenate([b_up_kept, b_up_sent]),
        jnp.concatenate([b_up_sent, b_up_kept]),
    )
    small = jnp.concatenate(
        [rows_middle[:4], rows_up, rows_weight[:3], rows_input[:2], counts], axis=0
    )

    class Small:
        def __init__(self):
            self.moves = [(flip, bit) for bit in (1, *bits)] + [(flip_depth, 1), (flip_depth, 2)]
            self.steps = self
            move, bit = self.moves.pop(0)
            self.state = [[small, move(small, bit)]]
            self.left = len(bits) + 3

        def send(self, state):
            total = state[0][0] + state[0][1]
            if not self.moves:
                return [[total]]
            move, bit = self.moves.pop(0)
            return [[total, move(total, bit)]]
    advance([tile_sum, weight_sum], rows_input)
    small_sum = Small()
    while tile_sum.left > 2:
        advance([weight_sum, small_sum, tile_sum])
    advance([weight_sum, small_sum])
    back_first, back_second, _ = lax.optimization_barrier(
        (back_first, back_second, weight_sum.here())
    )
    back = [send_back(back_first, 0), send_back(back_second, 1)]
    while tile_sum.left > 0:
        advance([weight_sum, small_sum, tile_sum])
    left, right = tile_sum.state
    gate = weight_sum.here()

    def expand(sources, place, shape, target):
        return call(
            functools.partial(expand_kernel, place),
            (4,),
            after(orders, *gate),
            wholes(*sources),
            [(fresh(shape, full), pl.BlockSpec(square, target))],
            room=32,
        )[0]

    grad_w_down = expand(left, 1, (hidden_width, width), lambda i, _: (i, 0))
    grad_w_up = expand(right, 2, (width, hidden_width), lambda i, _: (0, i))
    gates = [grad_w_down, grad_w_up]
    while weight_sum.left > 0 or small_sum.left > 0:
        advance([weight_sum, small_sum], *gates)
        gates = []
    grad_inputs = unpack(back[0], back[1], order_back, seqs)
    left, right = weight_sum.state
    grad_w_query, grad_w_key, grad_w_value, grad_w_out = call(
        expand_mixed_kernel,
        (8,),
        orders,
        wholes(*left, *right),
        [(fresh(square, full), pl.BlockSpec((width // 8, width), lambda i, _: (i, 0)))] * 4,
        room=32,
    )
    small = small_sum.state[0][0]

    return (
        result,
        grad_inputs,
        small[11],
        small[12],
        grad_w_query,
        small[8],
        grad_w_key,
        small[9],
        grad_w_value,
        small[10],
        grad_w_out,
        small[1],
        small[2],
        small[3],
        grad_w_up,
        small[4:8].reshape(-1),
        grad_w_down,
        small[0],
        small[13, :CLASSES].astype(jnp.int32),
    )


def solution(mesh):
    tokens = P("dp", "seq", None)
    return jax.shard_map(
        on_device,
        mesh=mesh,
        in_specs=(tokens, tokens, P("dp"), P("dp", "seq")) + (P(),) * 16,
        out_specs=(tokens, tokens) + (P(),) * 17,
        check_vma=False,
    )
```

```python
import functools

import jax
import jax.numpy as jnp
from jax import lax
from jax.experimental import pallas as pl
from jax.experimental.pallas import tpu as pltpu
from jax.sharding import PartitionSpec as P

HEAD = 64
CLASSES = 70
PAIR = 2 * HEAD
BLOCK = 256

epsilon = 1e-05
low = jnp.bfloat16
full = jnp.float32


def matmul(left, right):
    return lax.dot_general(
        left, right, (((1,), (0,)), ((), ())), preferred_element_type=full
    )


def matmul_left(left, right):
    return lax.dot_general(
        left, right, (((0,), (0,)), ((), ())), preferred_element_type=full
    )


def matmul_right(left, right):
    return lax.dot_general(
        left, right, (((1,), (1,)), ((), ())), preferred_element_type=full
    )


def whiten(value):
    centre = value - jnp.mean(value, axis=-1, keepdims=True)
    scale = lax.rsqrt(jnp.mean(centre * centre, axis=-1, keepdims=True) + epsilon)
    return centre * scale, scale


def whiten_back(grad, hat, scale):
    mean = jnp.mean(grad, axis=-1, keepdims=True)
    along = jnp.mean(grad * hat, axis=-1, keepdims=True)
    return scale * (grad - mean - hat * along)


def rotate(value, cosine, sine):
    lane = lax.broadcasted_iota(jnp.int32, value.shape, 1)
    ahead = pltpu.roll(value, PAIR - HEAD // 2, 1)
    behind = pltpu.roll(value, HEAD // 2, 1)
    swapped = jnp.where(lane % HEAD < HEAD // 2, ahead, behind)
    return value * cosine + swapped * sine


def call(kernel, grid, scalars, inputs, outputs, scratch=(), cost=20, room=60, aliases=None):
    return pl.pallas_call(
        kernel,
        grid_spec=pltpu.PrefetchScalarGridSpec(
            num_scalar_prefetch=1,
            grid=grid,
            in_specs=[spec for _, spec in inputs],
            out_specs=[spec for _, spec in outputs],
            scratch_shapes=list(scratch),
        ),
        out_shape=[shape for shape, _ in outputs],
        input_output_aliases=aliases or {},
        compiler_params=pltpu.CompilerParams(
            dimension_semantics=("arbitrary",) * len(grid), vmem_limit_bytes=room << 20
        ),
        cost_estimate=pl.CostEstimate(
            flops=int(cost * 1e9), transcendentals=0, bytes_accessed=int(cost * 2e6)
        ),
    )(scalars, *[array for array, _ in inputs])


def whole(array):
    rank = len(array.shape)
    return (array, pl.BlockSpec(array.shape, lambda *_: (0,) * rank))


def fresh(shape, kind):
    return jax.ShapeDtypeStruct(shape, kind)


def ranks(sizes):
    one, two, three = sizes[0], sizes[1], sizes[2]
    longest = jnp.where((one >= two) & (one >= three), 0, jnp.where(two >= three, 1, 2))
    return jnp.where(longest == 0, 1, 0), jnp.where(longest == 2, 1, 2), longest


def pack_kernel(sizes, blocks, *refs):
    *targets, sems = refs
    half = blocks.shape[1]
    pair = lax.axis_index("seq") // 2
    low_own, high_own, longest = ranks(sizes)
    copies = []
    for number in range(2):
        side = pair if number == 0 else 1 - pair
        own = jnp.where(side == 0, low_own, high_own)
        near = (2 * own, 2 * own + 1, 2 * longest + side)
        moves = [(spot, targets[number], place) for place, spot in enumerate(near)]
        moves += [(2 * longest + 1 - side, target, 0) for target in targets[2 + number : 3 + number]]
        for place, (spot, target, at) in enumerate(moves):
            copies.append(
                pltpu.make_async_copy(
                    blocks.at[spot], target.at[pl.ds(at * half, half)], sems.at[4 * number + place]
                )
            )
    for copy in copies:
        copy.start()
    for copy in copies:
        copy.wait()


def in_place(array):
    return (array, pl.BlockSpec(memory_space=pl.ANY))


def pack(array, sizes, far):
    seqs, span, width = array.shape
    half = span // 2
    outs = [fresh((3 * half, width), array.dtype)] * 2
    if far:
        outs += [fresh((half, width), array.dtype)] * 2
    return call(
        pack_kernel,
        (1,),
        sizes,
        [in_place(array.reshape(2 * seqs, half, width))],
        [whole(out) for out in outs],
        [pltpu.SemaphoreType.DMA((8,))],
    )


def unpack_kernel(order, first, second, out, sems):
    half = out.shape[1]
    number = out.shape[0]

    def copy(source, index):
        at = pl.ds(pl.multiple_of(order[number + index] * half, half), half)
        return pltpu.make_async_copy(source.at[at], out.at[index], sems.at[index])

    for index in range(number):

        @pl.when(order[index] == 0)
        def _(index=index):
            copy(first, index).start()

        @pl.when(order[index] != 0)
        def _(index=index):
            copy(second, index).start()

    for index in range(number):
        copy(first, index).wait()


def unpack(first, second, order, seqs):
    rows, width = first.shape
    half = rows // seqs
    blocks = call(
        unpack_kernel,
        (1,),
        order,
        [in_place(first), in_place(second)],
        [whole(fresh((2 * seqs, half, width), first.dtype))],
        [pltpu.SemaphoreType.DMA((2 * seqs,))],
        room=12,
    )[0]
    return blocks.reshape(seqs, 2 * half, width)


def join(first, second, span):
    half = span // 2
    return jnp.concatenate(
        [first[:span], second[:span], first[span : span + half], second[span : span + half]],
        axis=0,
    )


def turn_heads(raw, cos, sin):
    columns = range(0, raw.shape[1], PAIR)
    return [rotate(raw[:, at : at + PAIR], cos, sin).astype(low) for at in columns]


def project_kernel(
    place, first, second, gain, shift, w_query, w_key, w_value, b_query, b_key, b_value,
    cosine, sine, query, both, normed,
):
    span = 2 * first.shape[0] // 3
    half = span // 2
    for slot, message in enumerate((first, second)):
        own = slice(slot * span, (slot + 1) * span)
        mixed = slice(2 * span + slot * half, 2 * span + (slot + 1) * half)
        hat, _ = whiten(message[...].astype(full))
        item = (hat * gain[...] + shift[...]).astype(low)
        normed[own, :] = item[:span]
        normed[mixed, :] = item[span:]
        at = pl.ds(pl.multiple_of(place[slot], half), span)
        at_mixed = pl.ds(pl.multiple_of(place[2 + slot], half), half)
        cos = jnp.concatenate([cosine[at, :], cosine[at_mixed, :]], axis=0)
        sin = jnp.concatenate([sine[at, :], sine[at_mixed, :]], axis=0)
        raw = (matmul(item, w_key[...]) + b_key[...]).astype(low).astype(full)
        for index, turned in enumerate(turn_heads(raw, cos, sin)):
            spot = slice(index * PAIR, (index + 1) * PAIR)
            both[0, own, spot] = turned[:span]
            both[0, mixed, spot] = turned[span:]
        raw = (matmul(item, w_value[...]) + b_value[...]).astype(low)
        both[1, own, :] = raw[:span]
        both[1, mixed, :] = raw[span:]
        raw = (matmul(item, w_query[...]) + b_query[...]).astype(low).astype(full)
        for index, turned in enumerate(turn_heads(raw, cos, sin)):
            spot = slice(index * PAIR, (index + 1) * PAIR)
            turned = turned * low(HEAD**-0.5)
            query[own, spot] = turned[:span]
            query[mixed, spot] = turned[span:]


def project_far_kernel(
    place, first, second, gain, shift, w_key, w_value, b_key, b_value, cosine, sine, both, normed
):
    half = first.shape[0]
    message = jnp.concatenate([first[...], second[...]], axis=0)
    hat, _ = whiten(message.astype(full))
    item = (hat * gain[...] + shift[...]).astype(low)
    normed[...] = item
    at = [pl.ds(pl.multiple_of(place[4 + slot], half), half) for slot in range(2)]
    cos = jnp.concatenate([cosine[at[0], :], cosine[at[1], :]], axis=0)
    sin = jnp.concatenate([sine[at[0], :], sine[at[1], :]], axis=0)
    raw = (matmul(item, w_key[...]) + b_key[...]).astype(low).astype(full)
    for index, turned in enumerate(turn_heads(raw, cos, sin)):
        both[0, :, index * PAIR : (index + 1) * PAIR] = turned
    both[1] = (matmul(item, w_value[...]) + b_value[...]).astype(low)


def load_pieces(place, pieces, keys, values):
    for index, piece in enumerate(pieces):
        rows = piece.shape[1] // 2
        for slot in range(2):
            at = pl.ds(pl.multiple_of(place[1 + 2 * index + slot], rows), rows)
            keys[at, :] = piece[0, slot * rows : (slot + 1) * rows, :]
            values[at, :] = piece[1, slot * rows : (slot + 1) * rows, :]


def head_masks(value):
    lane = lax.broadcasted_iota(jnp.int32, value.shape, 1)
    wide = value.astype(full)
    return (
        jnp.where(lane < HEAD, wide, 0.0).astype(low),
        jnp.where(lane < HEAD, 0.0, wide).astype(low),
    )


def by_blocks(length, most, visit):
    number = pl.cdiv(length, BLOCK)
    for blocks in range(1, most + 1):

        @pl.when(number == blocks)
        def _(blocks=blocks):
            visit(blocks, length - (blocks - 1) * BLOCK)


def attend_kernel(count, place, query, *refs):
    pieces = refs[:count]
    out, logsum, keys, values = refs[count:]
    load_pieces(place, pieces, keys, values)
    pairs = [slice(at, at + PAIR) for at in range(0, query.shape[1], PAIR)]

    def visit(blocks, left):
        for pair, columns in enumerate(pairs):
            masked = head_masks(query[:, columns])
            value = values[: blocks * BLOCK, columns].T
            mixed = []
            for head in range(2):
                spot = slice(head * HEAD, (head + 1) * HEAD)
                scores = []
                for block in range(blocks):
                    key = keys[block * BLOCK : (block + 1) * BLOCK, columns]
                    item = matmul_right(key, masked[head])
                    if block == blocks - 1:
                        index = lax.broadcasted_iota(jnp.int32, item.shape, 0)
                        item = jnp.where(index < left, item, -1e30)
                    scores.append(item)
                peaks = [jnp.max(item, axis=0, keepdims=True) for item in scores]
                peak = functools.reduce(jnp.maximum, peaks)
                weights = [jnp.exp(item - peak) for item in scores]
                total = sum(jnp.sum(item, axis=0, keepdims=True) for item in weights)
                product = sum(
                    matmul(value[spot, block * BLOCK : (block + 1) * BLOCK], item.astype(low))
                    for block, item in enumerate(weights)
                )
                mixed.append(product / total)
                logsum[pair, head : head + 1, :] = peak + jnp.log(total)
            out[:, columns] = jnp.concatenate(mixed, axis=0).T.astype(low)

    by_blocks(place[0], keys.shape[0] // BLOCK, visit)


def attend_back_kernel(count, place, query, grad, mixed, logsum, cosine, sine, *refs):
    pieces = refs[:count]
    grad_query, *grad_pieces = refs[count : 1 + 2 * count]
    keys, values, grad_keys, grad_values = refs[1 + 2 * count :]
    load_pieces(place, pieces, keys, values)
    rows = query.shape[0]
    step = rows // 2
    pairs = [slice(at, at + PAIR) for at in range(0, query.shape[1], PAIR)]

    def visit(blocks, left):
        for pair, columns in enumerate(pairs):
            grad_low = grad[:, columns]
            masked = head_masks(query[:, columns])
            masked_grad = head_masks(grad_low)
            inner = (grad_low.astype(full) * mixed[:, columns].astype(full)).T
            delta = [
                jnp.sum(inner[head * HEAD : (head + 1) * HEAD, :], axis=0, keepdims=True)
                for head in range(2)
            ]
            turned = [0.0, 0.0]
            for block in range(blocks):
                at = slice(block * BLOCK, (block + 1) * BLOCK)
                key = keys[at, columns]
                value = values[at, columns]
                flat = key.T
                grad_key = 0.0
                grad_value = 0.0
                for head in range(2):
                    scores = matmul_right(key, masked[head])
                    weights = jnp.exp(scores - logsum[pair, head : head + 1, :])
                    if block == blocks - 1:
                        index = lax.broadcasted_iota(jnp.int32, scores.shape, 0)
                        weights = jnp.where(index < left, weights, 0.0)
                    grad_weights = matmul_right(value, masked_grad[head])
                    grad_scores = (weights * (grad_weights - delta[head])).astype(low)
                    grad_value += matmul(weights.astype(low), masked_grad[head])
                    grad_key += matmul(grad_scores, masked[head])
                    turned[head] += matmul(flat[head * HEAD : (head + 1) * HEAD, :], grad_scores)
                grad_keys[at, columns] = rotate(
                    grad_key, cosine[at, :], -sine[at, :]
                ).astype(low)
                grad_values[at, columns] = grad_value.astype(low)
            back = jnp.concatenate(turned, axis=0).T * HEAD**-0.5
            for slot in range(2):
                at = pl.ds(pl.multiple_of(place[1 + 2 * count + slot], step), step)
                part = slice(slot * step, (slot + 1) * step)
                grad_query[part, columns] = rotate(
                    back[part], cosine[at, :], -sine[at, :]
                ).astype(low)
        for block in range(blocks, keys.shape[0] // BLOCK):
            at = slice(block * BLOCK, (block + 1) * BLOCK)
            grad_keys[at, :] = jnp.zeros_like(grad_keys[at, :])
            grad_values[at, :] = jnp.zeros_like(grad_values[at, :])

    by_blocks(place[0], keys.shape[0] // BLOCK, visit)
    for index, piece in enumerate(grad_pieces):
        rows = piece.shape[1] // 2
        for slot in range(2):
            at = pl.ds(pl.multiple_of(place[1 + 2 * index + slot], rows), rows)
            piece[0, slot * rows : (slot + 1) * rows, :] = grad_keys[at, :]
            piece[1, slot * rows : (slot + 1) * rows, :] = grad_values[at, :]


def put_messages(to_first, to_second, value):
    span = 2 * to_first.shape[0] // 3
    half = span // 2
    to_first[:span, :] = value[:span]
    to_second[:span, :] = value[span : 2 * span]
    to_first[span:, :] = value[2 * span : 2 * span + half]
    to_second[span:, :] = value[2 * span + half :]


def hidden_tile(normed, cot, w_up, b_up, w_down, result, grad_normed, hidden, grad_hidden):
    count = normed.shape[0]
    step = min(count, 256)
    total = jnp.zeros((1, w_up.shape[1]), full)
    for row in range(0, count, step):
        spot = slice(row, row + step)
        hidden_in = matmul(normed[spot, :], w_up[...]) + b_up[...]
        back = matmul_right(cot[spot, :], w_down[...])
        share = 0.5 * (1.0 + lax.erf(hidden_in * 0.5**0.5))
        item = (hidden_in * share).astype(low)
        slope = share + hidden_in * jnp.exp(-0.5 * hidden_in * hidden_in) * 0.3989422804014327
        grad_item = (back * slope).astype(low)
        hidden[spot, :] = item
        grad_hidden[spot, :] = grad_item
        total += jnp.sum(grad_item.astype(full), axis=0, keepdims=True)
        result[spot, :] += matmul(item, w_down[...])
        grad_normed[spot, :] += matmul_right(grad_item, w_up[...])
    return total


def first_tiles_kernel(
    tiles, own, mixed, first, second, cot_first, cot_second, w_out, b_out, gain, shift,
    w_up, b_up, w_down, middle, result, grad_normed, normed, cot, sent, grad_b_up,
    hidden, grad_hidden,
):
    span = 2 * first.shape[0] // 3

    @pl.when(pl.program_id(0) == 0)
    def _():
        cot[...] = join(cot_first[...], cot_second[...], span)
        attended = jnp.concatenate([own[...], mixed[...]], axis=0)
        value = join(first[...], second[...], span).astype(full)
        value = value + matmul(attended, w_out[...]) + b_out[...]
        middle[...] = value
        hat, _ = whiten(value)
        normed[...] = (hat * gain[...] + shift[...]).astype(low)
        result[...] = jnp.zeros_like(result)
        grad_normed[...] = jnp.zeros_like(grad_normed)

    grad_b_up[0:1, :] = hidden_tile(
        normed, cot, w_up, b_up, w_down, result, grad_normed, hidden, grad_hidden
    )
    sent[0, ...] = matmul_left(hidden[...], cot[...]).astype(low)
    sent[1, ...] = matmul_left(normed[...], grad_hidden[...]).astype(low)


def last_tiles_kernel(
    tiles, own, mixed, middle, result_in, grad_normed_in, normed, cot, w_out, gain, w_up, b_up,
    w_down, b_down, kept, grad_b_up, to_first, to_second, grad_middle, grad_own, grad_mixed,
    out_kept, out_sent, rows_out, result, grad_normed, hidden, grad_hidden, grad_out,
):
    @pl.when(pl.program_id(0) == 0)
    def _():
        result[...] = result_in[...]
        grad_normed[...] = grad_normed_in[...]

    grad_b_up[0:1, :] = hidden_tile(
        normed, cot, w_up, b_up, w_down, result, grad_normed, hidden, grad_hidden
    )
    kept[0, ...] = matmul_left(hidden[...], cot[...]).astype(low)
    kept[1, ...] = matmul_left(normed[...], grad_hidden[...]).astype(low)

    @pl.when(pl.program_id(0) == pl.num_programs(0) - 1)
    def _():
        value = middle[...]
        put_messages(to_first, to_second, (value + result[...] + b_down[...]).astype(low))
        hat, scale = whiten(value)
        grad = grad_normed[...]
        cot_full = cot[...].astype(full)
        rows_out[0:1, :] = jnp.sum(cot_full, axis=0, keepdims=True)
        rows_out[2:3, :] = jnp.sum(grad * hat, axis=0, keepdims=True)
        rows_out[3:4, :] = jnp.sum(grad, axis=0, keepdims=True)
        total = cot_full + whiten_back(grad * gain[...], hat, scale)
        rows_out[1:2, :] = jnp.sum(total, axis=0, keepdims=True)
        rows_out[4:8, :] = jnp.zeros_like(rows_out[4:8, :])
        grad_middle[...] = total
        branch = total.astype(low)
        back = matmul_right(branch, w_out[...]).astype(low)
        grad_own[...] = back[: own.shape[0]]
        grad_mixed[...] = back[own.shape[0] :]
        attended = jnp.concatenate([own[...], mixed[...]], axis=0)
        grad_out[...] = matmul_left(attended, branch).astype(low)
        keep_core_half(tiles[2], grad_out, out_kept, out_sent)


def keep_core_half(core, source, kept, sent):
    size = source.shape[0] // 2
    mine = source[pl.ds(pl.multiple_of(core * size, size), size), :]
    theirs = source[pl.ds(pl.multiple_of((1 - core) * size, size), size), :]
    columns = kept.shape[-1]
    for index in range(kept.shape[0]):
        spot = slice(index * columns, (index + 1) * columns)
        kept[index] = mine[:, spot]
        sent[index] = theirs[:, spot]


def halve_kernel(order, kept, received, keep_left, give_left, keep_right, give_right):
    for index, (keep, give) in enumerate(((keep_left, give_left), (keep_right, give_right))):
        for target, half in ((keep, order[1 + index]), (give, 1 - order[1 + index])):
            total = kept[index, half].astype(full) + received[index, half].astype(full)
            target[0] = total.astype(low)


def quarter_kernel(order, kept, received, out_kept, out_received, *targets):
    rows = targets[0].shape[1]
    for index in range(2):
        for target, half in (
            (targets[2 * index], order[1 + index]),
            (targets[2 * index + 1], 1 - order[1 + index]),
        ):
            at = pl.ds(pl.multiple_of((2 * index + half) * rows, rows), rows)
            for lead in range(3):
                total = kept[lead, at, :].astype(full) + received[lead, at, :].astype(full)
                target[lead] = total.astype(low)
            total = out_kept[0, at, :].astype(full) + out_received[0, at, :].astype(full)
            target[3] = total.astype(low)


def stage_kernel(joined, order, *refs):
    count = len(refs) // 5 if not joined else (len(refs) - 3) // 2
    pairs = refs[: 2 * count]
    if joined:
        outs, totals = refs[-3:-1], refs[-1:]
        at = 0
        for index in range(count):
            rows = pairs[2 * index].shape[1]
            totals[0][:, at : at + rows, :] = (
                pairs[2 * index][...].astype(full) + pairs[2 * index + 1][...].astype(full)
            )
            at += rows
    else:
        outs, totals = refs[2 * count : 4 * count], refs[4 * count :]
        for index in range(count):
            totals[index][...] = (
                pairs[2 * index][...].astype(full) + pairs[2 * index + 1][...].astype(full)
            )
    for index, total in enumerate(totals):
        rows = total.shape[1] // 2
        for target, half in ((outs[2 * index], order[index]), (outs[2 * index + 1], 1 - order[index])):
            at = pl.ds(pl.multiple_of(half * rows, rows), rows)
            target[...] = total[:, at, :].astype(low)


def grad_far_kernel(order, kept, received, w_key, w_value, both, grad_far):
    for index in range(2):
        both[index] = (kept[index].astype(full) + received[index].astype(full)).astype(low)
    grad = matmul_right(both[0], w_key[...]) + matmul_right(both[1], w_value[...])
    half = grad.shape[0] // 2
    grad_far[:half, :] = grad[half:].astype(low)
    grad_far[half:, :] = grad[:half].astype(low)


def weight_kernel(
    core, normed, normed_far, query_own, query_mixed, own_kept, own_received, mixed_kept,
    mixed_received, far, kept, sent, both, rows_out, grad_weight,
):
    item = jnp.concatenate([query_own[...], query_mixed[...]], axis=0)
    count = item.shape[0]
    rows_out[0:1, :] = jnp.sum(item.astype(full), axis=0, keepdims=True)
    grad_weight[...] = matmul_left(normed[...], item).astype(low)
    keep_core_half(core[0], grad_weight, kept.at[0:1], sent.at[0:1])
    rows = jnp.concatenate([normed[...], normed_far[...]], axis=0)
    for index in range(2):
        own = own_kept[index].astype(full) + own_received[index].astype(full)
        mixed = mixed_kept[index].astype(full) + mixed_received[index].astype(full)
        item = jnp.concatenate([own.astype(low), mixed.astype(low), far[index]], axis=0)
        both[index] = item[:count]
        rows_out[1 + index : 2 + index, :] = jnp.sum(item.astype(full), axis=0, keepdims=True)
        grad_weight[...] = matmul_left(rows, item).astype(low)
        keep_core_half(
            core[0], grad_weight, kept.at[1 + index : 2 + index], sent.at[1 + index : 2 + index]
        )
    rows_out[3:8, :] = jnp.zeros_like(rows_out[3:8, :])


def input_kernel(
    core, query_own, query_mixed, both, far, w_query, w_key, w_value, first,
    second, gain, grad_middle, to_first, to_second, rows_out,
):
    span = 2 * first.shape[0] // 3
    grad_query = jnp.concatenate([query_own[...], query_mixed[...]], axis=0)
    grad = matmul_right(grad_query, w_query[...])
    for index, weight in enumerate((w_key, w_value)):
        grad = grad + matmul_right(both[index], weight[...])
    grad = jnp.concatenate(
        [grad[: 2 * span], grad[2 * span :] + far[...].astype(full)], axis=0
    )
    hat, scale = whiten(join(first[...], second[...], span).astype(full))
    rows_out[0:1, :] = jnp.sum(grad * hat, axis=0, keepdims=True)
    rows_out[1:2, :] = jnp.sum(grad, axis=0, keepdims=True)
    rows_out[2:8, :] = jnp.zeros_like(rows_out[2:8, :])
    done = (grad_middle[...] + whiten_back(grad * gain[...], hat, scale)).astype(low)
    put_messages(to_first, to_second, done)


def expand_kernel(place, order, *refs):
    sources = refs[:4]
    out = refs[-1]
    choice = 2 * ((pl.program_id(0) // 2) ^ order[0]) + ((pl.program_id(0) % 2) ^ order[place])
    for number, source in enumerate(sources):

        @pl.when(choice == number)
        def _(source=source):
            out[...] = source[0].astype(full)


def expand_mixed_kernel(order, *refs):
    sources, outs = refs[:8], refs[8:]
    index = pl.program_id(0)
    side = (index // 2) % 2
    bit = jnp.where(side == 0, order[1], order[2])
    choice = 4 * side + 2 * ((index // 4) ^ order[0]) + ((index % 2) ^ bit)
    for number, source in enumerate(sources):

        @pl.when(choice == number)
        def _(source=source):
            for place, out in enumerate(outs):
                out[...] = source[place].astype(full)


def after(value, *others):
    return lax.optimization_barrier((value, *others))[0]


def on_device(
    inputs, cotangent, lengths, predicted, norm1_gain, norm1_shift, w_query, b_query, w_key,
    b_key, w_value, b_value, w_out, b_out, norm2_gain, norm2_shift, w_up, b_up, w_down, b_down,
):
    seqs, span, width = inputs.shape
    half = span // 2
    tokens = seqs * span
    hidden_width = w_up.shape[1]
    groups = lax.axis_size("dp")
    assert seqs == 3 and lax.axis_size("seq") == 4 and hidden_width == 4 * width
    bits = [1 << place for place in range(1, groups.bit_length() - 1)]
    group = lax.axis_index("dp")
    depth = lax.axis_index("seq")
    core = group & 1
    side = depth & 1
    pair = depth >> 1
    count = 4 * span
    pairs = width // PAIR
    square = (width, width)

    def bit_of(bit):
        return (group & bit) // bit

    def flip(value, bit):
        return lax.ppermute(value, "dp", [(i, i ^ bit) for i in range(groups)])

    def flip_depth(value, bit):
        return lax.ppermute(value, "seq", [(i, i ^ bit) for i in range(4)])

    def route(turn):
        moves = []
        for at in range(groups):
            for z in range(4):
                to = (at & ~1) | ((z & 1) ^ 1 ^ turn)
                to_z = 2 * (at & 1) + (turn ^ (z >> 1))
                moves.append((at * 4 + z, to * 4 + to_z))
        return moves

    def cross(value):
        moves = [
            (at * 4 + z, (at ^ 1) * 4 + (z ^ 1)) for at in range(groups) for z in range(4)
        ]
        return lax.ppermute(value, ("dp", "seq"), moves)

    def send(value, turn):
        return lax.ppermute(value, ("dp", "seq"), route(turn))

    def send_back(value, turn):
        return lax.ppermute(value, ("dp", "seq"), [(b, a) for a, b in route(turn)])

    first, second, *far_rows = pack(inputs, lengths, True)
    cot_first, cot_second = pack(after(cotangent, first), lengths, False)
    first, second = send(first, 0), send(second, 1)
    first, second, far_rows = lax.optimization_barrier((first, second, far_rows))
    far_rows = [send(item, turn) for turn, item in enumerate(far_rows)]
    low_own, high_own, mixed_at = ranks(lengths)
    index = jnp.arange(2 * seqs)
    seq_at = index // 2
    part = index % 2
    from_turn = jnp.where(seq_at == mixed_at, part, (seq_at == high_own).astype(jnp.int32)) ^ pair
    from_row = jnp.where(seq_at == mixed_at, 2, part)
    order_back = jnp.concatenate([from_turn, from_row])

    sibling_lengths = flip(lengths, 1)
    sizes = jnp.where(core == pair, lengths, sibling_lengths)
    low_here, high_here, mixed_here = ranks(sizes)
    own_length = sizes[jnp.where(side == 0, low_here, high_here)]
    mixed_length = sizes[mixed_here]

    def starts(at_side, at_core):
        slots = jnp.arange(2)
        quarter = 2 * (slots ^ at_side) + (at_core ^ 1 ^ slots)
        return quarter * span, quarter * span + at_side * half

    own_at, mixed_start = starts(side, core)
    own_sibling, mixed_sibling = starts(side, 1 - core)
    far_start = own_at + (1 - side) * half
    far_sibling_start = own_sibling + (1 - side) * half
    own_place = jnp.concatenate([own_length[None], own_at, own_sibling, own_at])
    mixed_place = jnp.concatenate(
        [mixed_length[None], mixed_start, mixed_sibling, far_start, far_sibling_start, mixed_start]
    )
    project_place = jnp.concatenate([own_at, mixed_start, far_start])

    frequency = 10000.0 ** (-jnp.arange(HEAD // 2, dtype=full) / (HEAD // 2))
    angle = jnp.arange(count, dtype=full)[:, None] * frequency[None, :]
    cosine = jnp.tile(jnp.cos(angle), (1, 4))
    sine = jnp.sin(angle)
    sine = jnp.tile(jnp.concatenate([-sine, sine], axis=1), (1, 2))

    def row(vector):
        return vector.reshape(1, -1)

    gain1, shift1 = row(norm1_gain), row(norm1_shift)
    gain2, shift2 = row(norm2_gain), row(norm2_shift)

    def wholes(*items):
        return [whole(item) for item in items]

    bias_rows = [row(item) for item in (b_query, b_key, b_value, b_out, b_up, b_down)]
    tiles_first = jnp.stack([2 * (1 - core), 2 * (1 - core) + 1])
    tiles_last = jnp.stack([2 * core, 2 * core + 1, core])
    orders = jnp.stack([core, bit_of(bits[0]), bit_of(bits[-1])])
    core_only = core[None]
    sides = [jnp.stack([bit_of(near), bit_of(far)]) for near, far in zip(bits, bits[::-1])]
    sides += [side[None], pair[None]]
    live = (depth * span + jnp.arange(span))[None, :] < lengths[:, None]
    counts = jnp.sum(
        jnp.where(live[:, :, None] & (predicted[:, :, None] == jnp.arange(CLASSES)), 1.0, 0.0),
        axis=(0, 1),
    )
    counts = jnp.pad(counts[None], ((0, 0), (0, width - CLASSES)))
    early = (
        own_place, mixed_place, cosine, sine, bias_rows, gain1, shift1, gain2, shift2, tiles_first,
        tiles_last, orders, core_only, sides, counts, order_back,
    )
    project_place, early, _ = lax.optimization_barrier((project_place, early, cot_first))
    (
        own_place, mixed_place, cosine, sine, bias_rows, gain1, shift1, gain2, shift2, tiles_first,
        tiles_last, orders, core_only, sides, counts, order_back,
    ) = early
    b_query, b_key, b_value, b_out, b_up, b_down = bias_rows
    query, both, normed = call(
        project_kernel,
        (1,),
        project_place,
        wholes(
            first, second, gain1, shift1, w_query, w_key, w_value, b_query, b_key, b_value,
            cosine, sine,
        ),
        wholes(
            fresh((tokens, width), low), fresh((2, tokens, width), low), fresh((tokens, width), low)
        ),
    )
    both, far_rows = lax.optimization_barrier((both, far_rows))
    both_sibling = flip(both, 1)
    far, normed_far = call(
        project_far_kernel,
        (1,),
        after(project_place, query),
        wholes(*far_rows, gain1, shift1, w_key, w_value, b_key, b_value, cosine, sine),
        wholes(fresh((2, span, width), low), fresh((span, width), low)),
    )
    far_sibling = flip(far, 1)
    cot_first, cot_second, _ = lax.optimization_barrier((cot_first, cot_second, far))
    cot_first, cot_second = send(cot_first, 0), send(cot_second, 1)

    def columns(array, rows, at, size=PAIR, base=0):
        if len(array.shape) == 2:
            return (array, pl.BlockSpec((rows, size), lambda h, _: (at, base + h)))
        return (array, pl.BlockSpec((2, rows, size), lambda h, _: (0, at, base + h)))

    def own_pieces(*given):
        return [columns(both, 2 * span, 0, *given), columns(both_sibling, 2 * span, 0, *given)]

    def mixed_pieces(*given):
        return [
            columns(both, span, 2, *given),
            columns(both_sibling, span, 2, *given),
            columns(far, span, 0, *given),
            columns(far_sibling, span, 0, *given),
        ]

    def attend(place, rows, at, pieces):
        size = 2 * PAIR
        pieces = pieces(size)
        return call(
            functools.partial(attend_kernel, len(pieces)),
            (width // size,),
            place,
            [columns(query, rows, at, size), *pieces],
            [
                columns(fresh((rows, width), low), rows, 0, size),
                (
                    fresh((pairs, 8, rows), full),
                    pl.BlockSpec((2, 8, rows), lambda h, _: (h, 0, 0)),
                ),
            ],
            [pltpu.VMEM((count, size), low), pltpu.VMEM((count, size), low)],
                )

    own, own_logsum = attend(after(own_place, far), 2 * span, 0, own_pieces)
    mixed, mixed_logsum = attend(after(mixed_place, own), span, 2, mixed_pieces)

    def wide(array):
        return (array, pl.BlockSpec(square, lambda j, tiles: (0, tiles[j])))

    def tall(array):
        return (array, pl.BlockSpec(square, lambda j, tiles: (tiles[j], 0)))

    rows_fresh = fresh((8, width), full)

    def tiles_in():
        return [
            wide(w_up),
            (b_up, pl.BlockSpec((1, width), lambda j, tiles: (0, tiles[j]))),
            tall(w_down),
        ]

    def tile_outs():
        return [
            (
                fresh((2, 2, width, width), low),
                pl.BlockSpec((2, None, width, width), lambda j, _: (0, j, 0, 0)),
            ),
            (fresh((2, 8, width), full), pl.BlockSpec((None, 8, width), lambda j, _: (j, 0, 0))),
        ]

    tokens_full = fresh((tokens, width), full)
    tokens_low = fresh((tokens, width), low)
    tile_scratch = [pltpu.VMEM((tokens, width), low), pltpu.VMEM((tokens, width), low)]
    middle, result, grad_normed2, normed2, cot, tiles_sent, b_up_sent = call(
        first_tiles_kernel,
        (2,),
        tiles_first,
        wholes(
            own, mixed, first, second, cot_first, cot_second, w_out, b_out, gain2, shift2
        )
        + tiles_in(),
        wholes(tokens_full, tokens_full, tokens_full, tokens_low, tokens_low) + tile_outs(),
        tile_scratch,
    )
    tiles_received = flip(tiles_sent, 1)
    (
        tiles_kept, b_up_kept, result_first, result_second, grad_middle, grad_own, grad_mixed,
        out_kept, out_sent, rows_middle,
    ) = call(
        last_tiles_kernel,
        (2,),
        tiles_last,
        wholes(own, mixed, middle, result, grad_normed2, normed2, cot, w_out, gain2)
        + tiles_in()
        + wholes(b_down),
        tile_outs()
        + wholes(
            fresh((tokens // 2, width), low), fresh((tokens // 2, width), low), tokens_full,
            fresh((2 * span, width), low), fresh((span, width), low),
            fresh((1, width // 2, width), low), fresh((1, width // 2, width), low), rows_fresh,
        ),
        [pltpu.VMEM((tokens, width), full), pltpu.VMEM((tokens, width), full)]
        + tile_scratch
        + [pltpu.VMEM(square, low)],
    )
    result = [send_back(result_first, 0), send_back(result_second, 1)]
    out_received = flip(out_sent, 1)

    def split(addends, at):
        rows = addends[0].shape[1] // 2

        def part(which):
            items = [
                lax.dynamic_slice_in_dim(item, which * rows, rows, 1).astype(full)
                for item in addends
            ]
            return sum(items[1:], items[0]).astype(low)

        return part(at), part(1 - at)

    def added(addends):
        return (addends[0].astype(full) + addends[1].astype(full)).astype(low)

    def ordered(at, mine, theirs):
        return jnp.where(
            at == 0,
            jnp.concatenate([mine, theirs], axis=1),
            jnp.concatenate([theirs, mine], axis=1),
        )

    def stage(values, at, number, joined=False):
        lead, _, columns_in = values[0][0].shape
        sizes = [item[0].shape[1] for item in values]
        sizes = [sum(sizes)] if joined else sizes
        if any(size % 16 for size in sizes):
            if joined:
                values = [[jnp.concatenate([added(item) for item in values], axis=1)]]
            return [split(item, place) for item, place in zip(values, at)]
        parts = call(
            functools.partial(stage_kernel, joined),
            (1,),
            sides[number],
            wholes(*[part for item in values for part in item]),
            wholes(
                *[fresh((lead, size // 2, columns_in), low) for size in sizes for _ in range(2)]
            ),
            [pltpu.VMEM((lead, size, columns_in), full) for size in sizes],
            room=32,
        )
        return [tuple(parts[2 * place : 2 * place + 2]) for place in range(len(sizes))]

    def chain(parts, orders, early):
        for step in range(len(bits)):
            if step > 0:
                parts = stage(values, [bit_of(order[step]) for order in orders], step)
            values = yield [
                [keep, flip(give, order[step])] for (keep, give), order in zip(parts, orders)
            ]
        sizes = [item[0].shape[1] for item in values]
        ((keep, give),) = stage(values, [side], -2, joined=True)
        values = yield [[keep, flip_depth(give, 1)]]
        ((keep, give),) = stage(values, [pair], -1)
        (value,) = yield [[keep, flip_depth(give, 2)]]
        total = added(value)
        (value,) = yield [[total, flip_depth(total, 2)]]
        joined = ordered(pair, *value)
        (value,) = yield [[joined, flip_depth(joined, 1)]]
        joined = ordered(side, *value)
        ends = [sum(sizes[: place + 1]) for place in range(len(sizes))]
        values = [joined[:, end - size : end] for end, size in zip(ends, sizes)]
        for step in range(len(bits) - 1, 0, -1):
            values = yield [
                [item, flip(item, order[step])] for item, order in zip(values, orders)
            ]
            values = [
                ordered(bit_of(order[step]), *item) for item, order in zip(values, orders)
            ]
        values = yield [
            [item, flip(item, order[0])] + ([flip(item, 1)] if early else [])
            for item, order in zip(values, orders)
        ]
        values = yield [
            [*item, flip(item[1], 1)] if early else [*item, flip(item[0], 1), flip(item[1], 1)]
            for item in values
        ]
        yield values

    class Chain:
        def __init__(self, left, right, early):
            self.steps = chain([left, right], [bits, reverse], early)
            self.state = next(self.steps)
            self.left = 2 * len(bits) + 5

        def here(self):
            return [item[0] for item in self.state]

    def advance(chains, *gates):
        chains = [item for item in chains if item.left > 0]
        states = lax.optimization_barrier(([item.state for item in chains], gates))[0]
        for item, state in zip(chains, states):
            item.state = item.steps.send(state)
            item.left -= 1

    reverse = bits[::-1]

    part = fresh((1, width, width), low)
    parts = call(
        halve_kernel,
        (1,),
        orders,
        wholes(tiles_kept, tiles_received),
        wholes(part, part, part, part),
        room=40,
    )
    tile_sum = Chain(tuple(parts[:2]), tuple(parts[2:]), True)

    def attend_back(place, rows, at, pieces, grad, out, logsum, size, base, steps):
        given = pieces(size, base)
        group_pairs = size // PAIR
        return call(
            functools.partial(attend_back_kernel, len(given)),
            (steps,),
            place,
            [
                columns(query, rows, at, size, base),
                columns(grad, rows, 0, size, base),
                columns(out, rows, 0, size, base),
                (logsum, pl.BlockSpec((group_pairs, 8, rows), lambda h, _: (base + h, 0, 0))),
                whole(cosine),
                whole(sine),
                *given,
            ],
            [columns(fresh((rows, size * steps), low), rows, 0, size)]
            + [columns(fresh((2, rows, size * steps), low), rows, 0, size) for _ in given],
            [pltpu.VMEM((count, size), low)] * 4,
                )

    query_mixed, mixed_here_grad, mixed_sibling_grad, far_grad, far_sibling_grad = attend_back(
        after(mixed_place, *tile_sum.here()), span, 2, mixed_pieces, grad_mixed, mixed, mixed_logsum,
        2 * PAIR, 0, pairs // 2,
    )
    far_received = flip(far_sibling_grad, 1)
    mixed_received = flip(mixed_sibling_grad, 1)
    result = unpack(after(result[0], query_mixed), result[1], order_back, seqs)
    advance([tile_sum], query_mixed)
    far_both, grad_far = call(
        grad_far_kernel,
        (1,),
        after(core_only, result, *tile_sum.here()),
        wholes(far_grad, far_received, w_key, w_value),
        wholes(fresh((2, span, width), low), fresh((span, width), low)),
    )
    grad_far = cross(grad_far)

    query_own, own_kept, own_sent = attend_back(
        after(own_place, far_both), 2 * span, 0, own_pieces, grad_own, own, own_logsum, 2 * PAIR, 0,
        pairs // 2,
    )
    own_received = flip(own_sent, 1)
    advance([tile_sum], query_own)
    weight_kept, weight_sent, both_grad, rows_weight = call(
        weight_kernel,
        (1,),
        after(core_only, grad_far, *tile_sum.here()),
        wholes(
            normed, normed_far, query_own, query_mixed, own_kept, own_received, mixed_here_grad,
            mixed_received, far_both,
        ),
        wholes(
            fresh((3, width // 2, width), low), fresh((3, width // 2, width), low),
            fresh((2, tokens, width), low), rows_fresh,
        ),
        [pltpu.VMEM(square, low)],
    )
    weight_received = flip(weight_sent, 1)
    advance([tile_sum], rows_weight)
    weight_kept, weight_received, out_kept, out_received, _ = lax.optimization_barrier(
        (weight_kept, weight_received, out_kept, out_received, tile_sum.here())
    )
    part = fresh((4, width // 8, width), low)
    parts = call(
        quarter_kernel,
        (1,),
        orders,
        wholes(weight_kept, weight_received, out_kept, out_received),
        wholes(part, part, part, part),
        room=32,
    )
    weight_sum = Chain(tuple(parts[:2]), tuple(parts[2:]), False)
    back_first, back_second, rows_input = call(
        input_kernel,
        (1,),
        after(core_only, *tile_sum.here(), *weight_sum.here()),
        wholes(
            query_own, query_mixed, both_grad, grad_far, w_query, w_key, w_value, first, second,
            gain1, grad_middle,
        ),
        wholes(fresh((tokens // 2, width), low), fresh((tokens // 2, width), low), rows_fresh),
    )

    b_up_kept, b_up_sent, _ = lax.optimization_barrier((b_up_kept, b_up_sent, rows_input))
    b_up_kept, b_up_sent = b_up_kept[:, 0], b_up_sent[:, 0]
    rows_up = jnp.where(
        core == 0,
        jnp.concatenate([b_up_kept, b_up_sent]),
        jnp.concatenate([b_up_sent, b_up_kept]),
    )
    small = jnp.concatenate(
        [rows_middle[:4], rows_up, rows_weight[:3], rows_input[:2], counts], axis=0
    )

    class Small:
        def __init__(self):
            self.moves = [(flip, bit) for bit in (1, *bits)] + [(flip_depth, 1), (flip_depth, 2)]
            self.steps = self
            move, bit = self.moves.pop(0)
            self.state = [[small, move(small, bit)]]
            self.left = len(bits) + 3

        def send(self, state):
            total = state[0][0] + state[0][1]
            if not self.moves:
                return [[total]]
            move, bit = self.moves.pop(0)
            return [[total, move(total, bit)]]
    advance([tile_sum, weight_sum], rows_input)
    small_sum = Small()
    while tile_sum.left > 2:
        advance([weight_sum, small_sum, tile_sum])
    advance([weight_sum, small_sum])
    back_first, back_second, _ = lax.optimization_barrier(
        (back_first, back_second, weight_sum.here())
    )
    back = [send_back(back_first, 0), send_back(back_second, 1)]
    while tile_sum.left > 0:
        advance([weight_sum, small_sum, tile_sum])
    left, right = tile_sum.state
    gate = weight_sum.here()

    def expand(sources, place, shape, target):
        return call(
            functools.partial(expand_kernel, place),
            (4,),
            after(orders, *gate),
            wholes(*sources),
            [(fresh(shape, full), pl.BlockSpec(square, target))],
            room=32,
        )[0]

    grad_w_down = expand(left, 1, (hidden_width, width), lambda i, _: (i, 0))
    grad_w_up = expand(right, 2, (width, hidden_width), lambda i, _: (0, i))
    while small_sum.left > 0:
        advance([small_sum])
    total = small_sum.state[0][0]
    small = [total[at] for at in range(4)] + [total[4:8].reshape(-1)]
    small += [total[at] for at in range(8, 13)]
    small.append(total[13, :CLASSES].astype(jnp.int32))
    small = lax.optimization_barrier(small)
    gates = [grad_w_down, grad_w_up, *small]
    while weight_sum.left > 0:
        advance([weight_sum], *gates)
        gates = []
    grad_inputs = unpack(back[0], back[1], order_back, seqs)
    left, right = weight_sum.state
    grad_w_query, grad_w_key, grad_w_value, grad_w_out = call(
        expand_mixed_kernel,
        (8,),
        orders,
        wholes(*left, *right),
        [(fresh(square, full), pl.BlockSpec((width // 8, width), lambda i, _: (i, 0)))] * 4,
        room=32,
    )
    return (
        result,
        grad_inputs,
        small[8],
        small[9],
        grad_w_query,
        small[5],
        grad_w_key,
        small[6],
        grad_w_value,
        small[7],
        grad_w_out,
        small[1],
        small[2],
        small[3],
        grad_w_up,
        small[4],
        grad_w_down,
        small[0],
        small[10],
    )


def solution(mesh):
    tokens = P("dp", "seq", None)
    return jax.shard_map(
        on_device,
        mesh=mesh,
        in_specs=(tokens, tokens, P("dp"), P("dp", "seq")) + (P(),) * 16,
        out_specs=(tokens, tokens) + (P(),) * 17,
        check_vma=False,
    )
```

```python
import functools

import jax
import jax.numpy as jnp
from jax import lax
from jax.experimental import pallas as pl
from jax.experimental.pallas import tpu as pltpu
from jax.sharding import PartitionSpec as P

HEAD = 64
CLASSES = 70
PAIR = 2 * HEAD
BLOCK = 256

epsilon = 1e-05
low = jnp.bfloat16
full = jnp.float32


def matmul(left, right):
    return lax.dot_general(
        left, right, (((1,), (0,)), ((), ())), preferred_element_type=full
    )


def matmul_left(left, right):
    return lax.dot_general(
        left, right, (((0,), (0,)), ((), ())), preferred_element_type=full
    )


def matmul_right(left, right):
    return lax.dot_general(
        left, right, (((1,), (1,)), ((), ())), preferred_element_type=full
    )


def whiten(value):
    centre = value - jnp.mean(value, axis=-1, keepdims=True)
    scale = lax.rsqrt(jnp.mean(centre * centre, axis=-1, keepdims=True) + epsilon)
    return centre * scale, scale


def whiten_back(grad, hat, scale):
    mean = jnp.mean(grad, axis=-1, keepdims=True)
    along = jnp.mean(grad * hat, axis=-1, keepdims=True)
    return scale * (grad - mean - hat * along)


def rotate(value, cosine, sine):
    lane = lax.broadcasted_iota(jnp.int32, value.shape, 1)
    ahead = pltpu.roll(value, PAIR - HEAD // 2, 1)
    behind = pltpu.roll(value, HEAD // 2, 1)
    swapped = jnp.where(lane % HEAD < HEAD // 2, ahead, behind)
    return value * cosine + swapped * sine


def call(kernel, grid, scalars, inputs, outputs, scratch=(), cost=20, room=60, aliases=None):
    return pl.pallas_call(
        kernel,
        grid_spec=pltpu.PrefetchScalarGridSpec(
            num_scalar_prefetch=1,
            grid=grid,
            in_specs=[spec for _, spec in inputs],
            out_specs=[spec for _, spec in outputs],
            scratch_shapes=list(scratch),
        ),
        out_shape=[shape for shape, _ in outputs],
        input_output_aliases=aliases or {},
        compiler_params=pltpu.CompilerParams(
            dimension_semantics=("arbitrary",) * len(grid), vmem_limit_bytes=room << 20
        ),
        cost_estimate=pl.CostEstimate(
            flops=int(cost * 1e9), transcendentals=0, bytes_accessed=int(cost * 2e6)
        ),
    )(scalars, *[array for array, _ in inputs])


def whole(array):
    rank = len(array.shape)
    return (array, pl.BlockSpec(array.shape, lambda *_: (0,) * rank))


def fresh(shape, kind):
    return jax.ShapeDtypeStruct(shape, kind)


def ranks(sizes):
    one, two, three = sizes[0], sizes[1], sizes[2]
    longest = jnp.where((one >= two) & (one >= three), 0, jnp.where(two >= three, 1, 2))
    return jnp.where(longest == 0, 1, 0), jnp.where(longest == 2, 1, 2), longest


def pack_kernel(sizes, blocks, *refs):
    *targets, sems = refs
    half = blocks.shape[1]
    pair = lax.axis_index("seq") // 2
    low_own, high_own, longest = ranks(sizes)
    copies = []
    for number in range(2):
        side = pair if number == 0 else 1 - pair
        own = jnp.where(side == 0, low_own, high_own)
        near = (2 * own, 2 * own + 1, 2 * longest + side)
        moves = [(spot, targets[number], place) for place, spot in enumerate(near)]
        moves += [(2 * longest + 1 - side, target, 0) for target in targets[2 + number : 3 + number]]
        for place, (spot, target, at) in enumerate(moves):
            copies.append(
                pltpu.make_async_copy(
                    blocks.at[spot], target.at[pl.ds(at * half, half)], sems.at[4 * number + place]
                )
            )
    for copy in copies:
        copy.start()
    for copy in copies:
        copy.wait()


def in_place(array):
    return (array, pl.BlockSpec(memory_space=pl.ANY))


def pack(array, sizes, far):
    seqs, span, width = array.shape
    half = span // 2
    outs = [fresh((3 * half, width), array.dtype)] * 2
    if far:
        outs += [fresh((half, width), array.dtype)] * 2
    return call(
        pack_kernel,
        (1,),
        sizes,
        [in_place(array.reshape(2 * seqs, half, width))],
        [whole(out) for out in outs],
        [pltpu.SemaphoreType.DMA((8,))],
    )


def unpack_kernel(order, first, second, out, sems):
    half = out.shape[1]
    number = out.shape[0]

    def copy(source, index):
        at = pl.ds(pl.multiple_of(order[number + index] * half, half), half)
        return pltpu.make_async_copy(source.at[at], out.at[index], sems.at[index])

    for index in range(number):

        @pl.when(order[index] == 0)
        def _(index=index):
            copy(first, index).start()

        @pl.when(order[index] != 0)
        def _(index=index):
            copy(second, index).start()

    for index in range(number):
        copy(first, index).wait()


def unpack(first, second, order, seqs):
    rows, width = first.shape
    half = rows // seqs
    blocks = call(
        unpack_kernel,
        (1,),
        order,
        [in_place(first), in_place(second)],
        [whole(fresh((2 * seqs, half, width), first.dtype))],
        [pltpu.SemaphoreType.DMA((2 * seqs,))],
        room=12,
    )[0]
    return blocks.reshape(seqs, 2 * half, width)


def join(first, second, span):
    half = span // 2
    return jnp.concatenate(
        [first[:span], second[:span], first[span : span + half], second[span : span + half]],
        axis=0,
    )


def turn_heads(raw, cos, sin):
    columns = range(0, raw.shape[1], PAIR)
    return [rotate(raw[:, at : at + PAIR], cos, sin).astype(low) for at in columns]


def project_kernel(
    place, first, second, gain, shift, w_query, w_key, w_value, b_query, b_key, b_value,
    cosine, sine, query, both, normed,
):
    span = 2 * first.shape[0] // 3
    half = span // 2
    for slot, message in enumerate((first, second)):
        own = slice(slot * span, (slot + 1) * span)
        mixed = slice(2 * span + slot * half, 2 * span + (slot + 1) * half)
        hat, _ = whiten(message[...].astype(full))
        item = (hat * gain[...] + shift[...]).astype(low)
        normed[own, :] = item[:span]
        normed[mixed, :] = item[span:]
        at = pl.ds(pl.multiple_of(place[slot], half), span)
        at_mixed = pl.ds(pl.multiple_of(place[2 + slot], half), half)
        cos = jnp.concatenate([cosine[at, :], cosine[at_mixed, :]], axis=0)
        sin = jnp.concatenate([sine[at, :], sine[at_mixed, :]], axis=0)
        raw = (matmul(item, w_key[...]) + b_key[...]).astype(low).astype(full)
        for index, turned in enumerate(turn_heads(raw, cos, sin)):
            spot = slice(index * PAIR, (index + 1) * PAIR)
            both[0, own, spot] = turned[:span]
            both[0, mixed, spot] = turned[span:]
        raw = (matmul(item, w_value[...]) + b_value[...]).astype(low)
        both[1, own, :] = raw[:span]
        both[1, mixed, :] = raw[span:]
        raw = (matmul(item, w_query[...]) + b_query[...]).astype(low).astype(full)
        for index, turned in enumerate(turn_heads(raw, cos, sin)):
            spot = slice(index * PAIR, (index + 1) * PAIR)
            turned = turned * low(HEAD**-0.5)
            query[own, spot] = turned[:span]
            query[mixed, spot] = turned[span:]


def project_far_kernel(
    place, first, second, gain, shift, w_key, w_value, b_key, b_value, cosine, sine, both, normed
):
    half = first.shape[0]
    message = jnp.concatenate([first[...], second[...]], axis=0)
    hat, _ = whiten(message.astype(full))
    item = (hat * gain[...] + shift[...]).astype(low)
    normed[...] = item
    at = [pl.ds(pl.multiple_of(place[4 + slot], half), half) for slot in range(2)]
    cos = jnp.concatenate([cosine[at[0], :], cosine[at[1], :]], axis=0)
    sin = jnp.concatenate([sine[at[0], :], sine[at[1], :]], axis=0)
    raw = (matmul(item, w_key[...]) + b_key[...]).astype(low).astype(full)
    for index, turned in enumerate(turn_heads(raw, cos, sin)):
        both[0, :, index * PAIR : (index + 1) * PAIR] = turned
    both[1] = (matmul(item, w_value[...]) + b_value[...]).astype(low)


def load_pieces(place, pieces, keys, values):
    for index, piece in enumerate(pieces):
        rows = piece.shape[1] // 2
        for slot in range(2):
            at = pl.ds(pl.multiple_of(place[1 + 2 * index + slot], rows), rows)
            keys[at, :] = piece[0, slot * rows : (slot + 1) * rows, :]
            values[at, :] = piece[1, slot * rows : (slot + 1) * rows, :]


def head_masks(value):
    lane = lax.broadcasted_iota(jnp.int32, value.shape, 1)
    wide = value.astype(full)
    return (
        jnp.where(lane < HEAD, wide, 0.0).astype(low),
        jnp.where(lane < HEAD, 0.0, wide).astype(low),
    )


def by_blocks(length, most, visit):
    number = pl.cdiv(length, BLOCK)
    for blocks in range(1, most + 1):

        @pl.when(number == blocks)
        def _(blocks=blocks):
            visit(blocks, length - (blocks - 1) * BLOCK)


def attend_kernel(count, place, query, *refs):
    pieces = refs[:count]
    out, logsum, keys, values = refs[count:]
    load_pieces(place, pieces, keys, values)
    pairs = [slice(at, at + PAIR) for at in range(0, query.shape[1], PAIR)]

    def visit(blocks, left):
        for pair, columns in enumerate(pairs):
            masked = head_masks(query[:, columns])
            value = values[: blocks * BLOCK, columns].T
            mixed = []
            for head in range(2):
                spot = slice(head * HEAD, (head + 1) * HEAD)
                scores = []
                for block in range(blocks):
                    key = keys[block * BLOCK : (block + 1) * BLOCK, columns]
                    item = matmul_right(key, masked[head])
                    if block == blocks - 1:
                        index = lax.broadcasted_iota(jnp.int32, item.shape, 0)
                        item = jnp.where(index < left, item, -1e30)
                    scores.append(item)
                peaks = [jnp.max(item, axis=0, keepdims=True) for item in scores]
                peak = functools.reduce(jnp.maximum, peaks)
                weights = [jnp.exp(item - peak) for item in scores]
                total = sum(jnp.sum(item, axis=0, keepdims=True) for item in weights)
                product = sum(
                    matmul(value[spot, block * BLOCK : (block + 1) * BLOCK], item.astype(low))
                    for block, item in enumerate(weights)
                )
                mixed.append(product / total)
                logsum[pair, head : head + 1, :] = peak + jnp.log(total)
            out[:, columns] = jnp.concatenate(mixed, axis=0).T.astype(low)

    by_blocks(place[0], keys.shape[0] // BLOCK, visit)


def attend_back_kernel(count, place, query, grad, mixed, logsum, cosine, sine, *refs):
    pieces = refs[:count]
    grad_query, *grad_pieces = refs[count : 1 + 2 * count]
    keys, values, grad_keys, grad_values = refs[1 + 2 * count :]
    load_pieces(place, pieces, keys, values)
    rows = query.shape[0]
    step = rows // 2
    pairs = [slice(at, at + PAIR) for at in range(0, query.shape[1], PAIR)]

    def visit(blocks, left):
        for pair, columns in enumerate(pairs):
            grad_low = grad[:, columns]
            masked = head_masks(query[:, columns])
            masked_grad = head_masks(grad_low)
            inner = (grad_low.astype(full) * mixed[:, columns].astype(full)).T
            delta = [
                jnp.sum(inner[head * HEAD : (head + 1) * HEAD, :], axis=0, keepdims=True)
                for head in range(2)
            ]
            turned = [0.0, 0.0]
            for block in range(blocks):
                at = slice(block * BLOCK, (block + 1) * BLOCK)
                key = keys[at, columns]
                value = values[at, columns]
                flat = key.T
                grad_key = 0.0
                grad_value = 0.0
                for head in range(2):
                    scores = matmul_right(key, masked[head])
                    weights = jnp.exp(scores - logsum[pair, head : head + 1, :])
                    if block == blocks - 1:
                        index = lax.broadcasted_iota(jnp.int32, scores.shape, 0)
                        weights = jnp.where(index < left, weights, 0.0)
                    grad_weights = matmul_right(value, masked_grad[head])
                    grad_scores = (weights * (grad_weights - delta[head])).astype(low)
                    grad_value += matmul(weights.astype(low), masked_grad[head])
                    grad_key += matmul(grad_scores, masked[head])
                    turned[head] += matmul(flat[head * HEAD : (head + 1) * HEAD, :], grad_scores)
                grad_keys[at, columns] = rotate(
                    grad_key, cosine[at, :], -sine[at, :]
                ).astype(low)
                grad_values[at, columns] = grad_value.astype(low)
            back = jnp.concatenate(turned, axis=0).T * HEAD**-0.5
            for slot in range(2):
                at = pl.ds(pl.multiple_of(place[1 + 2 * count + slot], step), step)
                part = slice(slot * step, (slot + 1) * step)
                grad_query[part, columns] = rotate(
                    back[part], cosine[at, :], -sine[at, :]
                ).astype(low)
        for block in range(blocks, keys.shape[0] // BLOCK):
            at = slice(block * BLOCK, (block + 1) * BLOCK)
            grad_keys[at, :] = jnp.zeros_like(grad_keys[at, :])
            grad_values[at, :] = jnp.zeros_like(grad_values[at, :])

    by_blocks(place[0], keys.shape[0] // BLOCK, visit)
    for index, piece in enumerate(grad_pieces):
        rows = piece.shape[1] // 2
        for slot in range(2):
            at = pl.ds(pl.multiple_of(place[1 + 2 * index + slot], rows), rows)
            piece[0, slot * rows : (slot + 1) * rows, :] = grad_keys[at, :]
            piece[1, slot * rows : (slot + 1) * rows, :] = grad_values[at, :]


def put_messages(to_first, to_second, value):
    span = 2 * to_first.shape[0] // 3
    half = span // 2
    to_first[:span, :] = value[:span]
    to_second[:span, :] = value[span : 2 * span]
    to_first[span:, :] = value[2 * span : 2 * span + half]
    to_second[span:, :] = value[2 * span + half :]


def hidden_tile(normed, cot, w_up, b_up, w_down, result, grad_normed, hidden, grad_hidden):
    count = normed.shape[0]
    step = min(count, 256)
    total = jnp.zeros((1, w_up.shape[1]), full)
    for row in range(0, count, step):
        spot = slice(row, row + step)
        hidden_in = matmul(normed[spot, :], w_up[...]) + b_up[...]
        back = matmul_right(cot[spot, :], w_down[...])
        share = 0.5 * (1.0 + lax.erf(hidden_in * 0.5**0.5))
        item = (hidden_in * share).astype(low)
        slope = share + hidden_in * jnp.exp(-0.5 * hidden_in * hidden_in) * 0.3989422804014327
        grad_item = (back * slope).astype(low)
        hidden[spot, :] = item
        grad_hidden[spot, :] = grad_item
        total += jnp.sum(grad_item.astype(full), axis=0, keepdims=True)
        result[spot, :] += matmul(item, w_down[...])
        grad_normed[spot, :] += matmul_right(grad_item, w_up[...])
    return total


def first_tiles_kernel(
    tiles, own, mixed, first, second, cot_first, cot_second, w_out, b_out, gain, shift,
    w_up, b_up, w_down, middle, result, grad_normed, normed, cot, sent, grad_b_up,
    hidden, grad_hidden,
):
    span = 2 * first.shape[0] // 3

    @pl.when(pl.program_id(0) == 0)
    def _():
        cot[...] = join(cot_first[...], cot_second[...], span)
        attended = jnp.concatenate([own[...], mixed[...]], axis=0)
        value = join(first[...], second[...], span).astype(full)
        value = value + matmul(attended, w_out[...]) + b_out[...]
        middle[...] = value
        hat, _ = whiten(value)
        normed[...] = (hat * gain[...] + shift[...]).astype(low)
        result[...] = jnp.zeros_like(result)
        grad_normed[...] = jnp.zeros_like(grad_normed)

    grad_b_up[0:1, :] = hidden_tile(
        normed, cot, w_up, b_up, w_down, result, grad_normed, hidden, grad_hidden
    )
    sent[0, ...] = matmul_left(hidden[...], cot[...]).astype(low)
    sent[1, ...] = matmul_left(normed[...], grad_hidden[...]).astype(low)


def last_tiles_kernel(
    tiles, own, mixed, middle, result_in, grad_normed_in, normed, cot, w_out, gain, w_up, b_up,
    w_down, b_down, kept, grad_b_up, to_first, to_second, grad_middle, grad_own, grad_mixed,
    out_kept, out_sent, rows_out, result, grad_normed, hidden, grad_hidden, grad_out,
):
    @pl.when(pl.program_id(0) == 0)
    def _():
        result[...] = result_in[...]
        grad_normed[...] = grad_normed_in[...]

    grad_b_up[0:1, :] = hidden_tile(
        normed, cot, w_up, b_up, w_down, result, grad_normed, hidden, grad_hidden
    )
    kept[0, ...] = matmul_left(hidden[...], cot[...]).astype(low)
    kept[1, ...] = matmul_left(normed[...], grad_hidden[...]).astype(low)

    @pl.when(pl.program_id(0) == pl.num_programs(0) - 1)
    def _():
        value = middle[...]
        put_messages(to_first, to_second, (value + result[...] + b_down[...]).astype(low))
        hat, scale = whiten(value)
        grad = grad_normed[...]
        cot_full = cot[...].astype(full)
        rows_out[0:1, :] = jnp.sum(cot_full, axis=0, keepdims=True)
        rows_out[2:3, :] = jnp.sum(grad * hat, axis=0, keepdims=True)
        rows_out[3:4, :] = jnp.sum(grad, axis=0, keepdims=True)
        total = cot_full + whiten_back(grad * gain[...], hat, scale)
        rows_out[1:2, :] = jnp.sum(total, axis=0, keepdims=True)
        rows_out[4:8, :] = jnp.zeros_like(rows_out[4:8, :])
        grad_middle[...] = total
        branch = total.astype(low)
        back = matmul_right(branch, w_out[...]).astype(low)
        grad_own[...] = back[: own.shape[0]]
        grad_mixed[...] = back[own.shape[0] :]
        attended = jnp.concatenate([own[...], mixed[...]], axis=0)
        grad_out[...] = matmul_left(attended, branch).astype(low)
        keep_core_half(tiles[2], grad_out, out_kept, out_sent)


def keep_core_half(core, source, kept, sent):
    size = source.shape[0] // 2
    mine = source[pl.ds(pl.multiple_of(core * size, size), size), :]
    theirs = source[pl.ds(pl.multiple_of((1 - core) * size, size), size), :]
    columns = kept.shape[-1]
    for index in range(kept.shape[0]):
        spot = slice(index * columns, (index + 1) * columns)
        kept[index] = mine[:, spot]
        sent[index] = theirs[:, spot]


def halve_kernel(order, kept, received, keep_left, give_left, keep_right, give_right):
    for index, (keep, give) in enumerate(((keep_left, give_left), (keep_right, give_right))):
        for target, half in ((keep, order[1 + index]), (give, 1 - order[1 + index])):
            total = kept[index, half].astype(full) + received[index, half].astype(full)
            target[0] = total.astype(low)


def quarter_kernel(order, kept, received, out_kept, out_received, *targets):
    rows = targets[0].shape[1]
    for index in range(2):
        for target, half in (
            (targets[2 * index], order[1 + index]),
            (targets[2 * index + 1], 1 - order[1 + index]),
        ):
            at = pl.ds(pl.multiple_of((2 * index + half) * rows, rows), rows)
            for lead in range(3):
                total = kept[lead, at, :].astype(full) + received[lead, at, :].astype(full)
                target[lead] = total.astype(low)
            total = out_kept[0, at, :].astype(full) + out_received[0, at, :].astype(full)
            target[3] = total.astype(low)


def stage_kernel(joined, order, *refs):
    count = len(refs) // 5 if not joined else (len(refs) - 3) // 2
    pairs = refs[: 2 * count]
    if joined:
        outs, totals = refs[-3:-1], refs[-1:]
        at = 0
        for index in range(count):
            rows = pairs[2 * index].shape[1]
            totals[0][:, at : at + rows, :] = (
                pairs[2 * index][...].astype(full) + pairs[2 * index + 1][...].astype(full)
            )
            at += rows
    else:
        outs, totals = refs[2 * count : 4 * count], refs[4 * count :]
        for index in range(count):
            totals[index][...] = (
                pairs[2 * index][...].astype(full) + pairs[2 * index + 1][...].astype(full)
            )
    for index, total in enumerate(totals):
        rows = total.shape[1] // 2
        for target, half in ((outs[2 * index], order[index]), (outs[2 * index + 1], 1 - order[index])):
            at = pl.ds(pl.multiple_of(half * rows, rows), rows)
            target[...] = total[:, at, :].astype(low)


def grad_far_kernel(order, kept, received, w_key, w_value, both, grad_far):
    for index in range(2):
        both[index] = (kept[index].astype(full) + received[index].astype(full)).astype(low)
    grad = matmul_right(both[0], w_key[...]) + matmul_right(both[1], w_value[...])
    half = grad.shape[0] // 2
    grad_far[:half, :] = grad[half:].astype(low)
    grad_far[half:, :] = grad[:half].astype(low)


def weight_kernel(
    core, normed, normed_far, query_own, query_mixed, own_kept, own_received, mixed_kept,
    mixed_received, far, kept, sent, both, rows_out, grad_weight,
):
    item = jnp.concatenate([query_own[...], query_mixed[...]], axis=0)
    count = item.shape[0]
    rows_out[0:1, :] = jnp.sum(item.astype(full), axis=0, keepdims=True)
    grad_weight[...] = matmul_left(normed[...], item).astype(low)
    keep_core_half(core[0], grad_weight, kept.at[0:1], sent.at[0:1])
    rows = jnp.concatenate([normed[...], normed_far[...]], axis=0)
    for index in range(2):
        own = own_kept[index].astype(full) + own_received[index].astype(full)
        mixed = mixed_kept[index].astype(full) + mixed_received[index].astype(full)
        item = jnp.concatenate([own.astype(low), mixed.astype(low), far[index]], axis=0)
        both[index] = item[:count]
        rows_out[1 + index : 2 + index, :] = jnp.sum(item.astype(full), axis=0, keepdims=True)
        grad_weight[...] = matmul_left(rows, item).astype(low)
        keep_core_half(
            core[0], grad_weight, kept.at[1 + index : 2 + index], sent.at[1 + index : 2 + index]
        )
    rows_out[3:8, :] = jnp.zeros_like(rows_out[3:8, :])


def input_kernel(
    core, query_own, query_mixed, both, far, w_query, w_key, w_value, first,
    second, gain, grad_middle, to_first, to_second, rows_out,
):
    span = 2 * first.shape[0] // 3
    grad_query = jnp.concatenate([query_own[...], query_mixed[...]], axis=0)
    grad = matmul_right(grad_query, w_query[...])
    for index, weight in enumerate((w_key, w_value)):
        grad = grad + matmul_right(both[index], weight[...])
    grad = jnp.concatenate(
        [grad[: 2 * span], grad[2 * span :] + far[...].astype(full)], axis=0
    )
    hat, scale = whiten(join(first[...], second[...], span).astype(full))
    rows_out[0:1, :] = jnp.sum(grad * hat, axis=0, keepdims=True)
    rows_out[1:2, :] = jnp.sum(grad, axis=0, keepdims=True)
    rows_out[2:8, :] = jnp.zeros_like(rows_out[2:8, :])
    done = (grad_middle[...] + whiten_back(grad * gain[...], hat, scale)).astype(low)
    put_messages(to_first, to_second, done)


def expand_kernel(place, order, *refs):
    sources = refs[:4]
    out = refs[-1]
    choice = 2 * ((pl.program_id(0) // 2) ^ order[0]) + ((pl.program_id(0) % 2) ^ order[place])
    for number, source in enumerate(sources):

        @pl.when(choice == number)
        def _(source=source):
            out[...] = source[0].astype(full)


def expand_mixed_kernel(order, *refs):
    sources, outs = refs[:8], refs[8:]
    index = pl.program_id(0)
    side = (index // 2) % 2
    bit = jnp.where(side == 0, order[1], order[2])
    choice = 4 * side + 2 * ((index // 4) ^ order[0]) + ((index % 2) ^ bit)
    for number, source in enumerate(sources):

        @pl.when(choice == number)
        def _(source=source):
            for place, out in enumerate(outs):
                out[...] = source[place].astype(full)


def after(value, *others):
    return lax.optimization_barrier((value, *others))[0]


def on_device(
    inputs, cotangent, lengths, predicted, norm1_gain, norm1_shift, w_query, b_query, w_key,
    b_key, w_value, b_value, w_out, b_out, norm2_gain, norm2_shift, w_up, b_up, w_down, b_down,
):
    seqs, span, width = inputs.shape
    half = span // 2
    tokens = seqs * span
    hidden_width = w_up.shape[1]
    groups = lax.axis_size("dp")
    assert seqs == 3 and lax.axis_size("seq") == 4 and hidden_width == 4 * width
    bits = [1 << place for place in range(1, groups.bit_length() - 1)]
    group = lax.axis_index("dp")
    depth = lax.axis_index("seq")
    core = group & 1
    side = depth & 1
    pair = depth >> 1
    count = 4 * span
    pairs = width // PAIR
    square = (width, width)

    def bit_of(bit):
        return (group & bit) // bit

    def flip(value, bit):
        return lax.ppermute(value, "dp", [(i, i ^ bit) for i in range(groups)])

    def flip_depth(value, bit):
        return lax.ppermute(value, "seq", [(i, i ^ bit) for i in range(4)])

    def route(turn):
        moves = []
        for at in range(groups):
            for z in range(4):
                to = (at & ~1) | ((z & 1) ^ 1 ^ turn)
                to_z = 2 * (at & 1) + (turn ^ (z >> 1))
                moves.append((at * 4 + z, to * 4 + to_z))
        return moves

    def cross(value):
        moves = [
            (at * 4 + z, (at ^ 1) * 4 + (z ^ 1)) for at in range(groups) for z in range(4)
        ]
        return lax.ppermute(value, ("dp", "seq"), moves)

    def send(value, turn):
        return lax.ppermute(value, ("dp", "seq"), route(turn))

    def send_back(value, turn):
        return lax.ppermute(value, ("dp", "seq"), [(b, a) for a, b in route(turn)])

    first, second, *far_rows = pack(inputs, lengths, True)
    cot_first, cot_second = pack(after(cotangent, first), lengths, False)
    first, second = send(first, 0), send(second, 1)
    first, second, far_rows = lax.optimization_barrier((first, second, far_rows))
    far_rows = [send(item, turn) for turn, item in enumerate(far_rows)]
    low_own, high_own, mixed_at = ranks(lengths)
    index = jnp.arange(2 * seqs)
    seq_at = index // 2
    part = index % 2
    from_turn = jnp.where(seq_at == mixed_at, part, (seq_at == high_own).astype(jnp.int32)) ^ pair
    from_row = jnp.where(seq_at == mixed_at, 2, part)
    order_back = jnp.concatenate([from_turn, from_row])

    sibling_lengths = flip(lengths, 1)
    sizes = jnp.where(core == pair, lengths, sibling_lengths)
    low_here, high_here, mixed_here = ranks(sizes)
    own_length = sizes[jnp.where(side == 0, low_here, high_here)]
    mixed_length = sizes[mixed_here]

    def starts(at_side, at_core):
        slots = jnp.arange(2)
        quarter = 2 * (slots ^ at_side) + (at_core ^ 1 ^ slots)
        return quarter * span, quarter * span + at_side * half

    own_at, mixed_start = starts(side, core)
    own_sibling, mixed_sibling = starts(side, 1 - core)
    far_start = own_at + (1 - side) * half
    far_sibling_start = own_sibling + (1 - side) * half
    own_place = jnp.concatenate([own_length[None], own_at, own_sibling, own_at])
    mixed_place = jnp.concatenate(
        [mixed_length[None], mixed_start, mixed_sibling, far_start, far_sibling_start, mixed_start]
    )
    project_place = jnp.concatenate([own_at, mixed_start, far_start])

    frequency = 10000.0 ** (-jnp.arange(HEAD // 2, dtype=full) / (HEAD // 2))
    angle = jnp.arange(count, dtype=full)[:, None] * frequency[None, :]
    cosine = jnp.tile(jnp.cos(angle), (1, 4))
    sine = jnp.sin(angle)
    sine = jnp.tile(jnp.concatenate([-sine, sine], axis=1), (1, 2))

    def row(vector):
        return vector.reshape(1, -1)

    gain1, shift1 = row(norm1_gain), row(norm1_shift)
    gain2, shift2 = row(norm2_gain), row(norm2_shift)

    def wholes(*items):
        return [whole(item) for item in items]

    bias_rows = [row(item) for item in (b_query, b_key, b_value, b_out, b_up, b_down)]
    tiles_first = jnp.stack([2 * (1 - core), 2 * (1 - core) + 1])
    tiles_last = jnp.stack([2 * core, 2 * core + 1, core])
    orders = jnp.stack([core, bit_of(bits[0]), bit_of(bits[-1])])
    core_only = core[None]
    sides = [jnp.stack([bit_of(near), bit_of(far)]) for near, far in zip(bits, bits[::-1])]
    sides += [side[None], pair[None]]
    live = (depth * span + jnp.arange(span))[None, :] < lengths[:, None]
    counts = jnp.sum(
        jnp.where(live[:, :, None] & (predicted[:, :, None] == jnp.arange(CLASSES)), 1.0, 0.0),
        axis=(0, 1),
    )
    counts = jnp.pad(counts[None], ((0, 0), (0, width - CLASSES)))
    early = (
        own_place, mixed_place, cosine, sine, bias_rows, gain1, shift1, gain2, shift2, tiles_first,
        tiles_last, orders, core_only, sides, counts, order_back,
    )
    project_place, early, _ = lax.optimization_barrier((project_place, early, cot_first))
    (
        own_place, mixed_place, cosine, sine, bias_rows, gain1, shift1, gain2, shift2, tiles_first,
        tiles_last, orders, core_only, sides, counts, order_back,
    ) = early
    b_query, b_key, b_value, b_out, b_up, b_down = bias_rows
    query, both, normed = call(
        project_kernel,
        (1,),
        project_place,
        wholes(
            first, second, gain1, shift1, w_query, w_key, w_value, b_query, b_key, b_value,
            cosine, sine,
        ),
        wholes(
            fresh((tokens, width), low), fresh((2, tokens, width), low), fresh((tokens, width), low)
        ),
    )
    both, far_rows = lax.optimization_barrier((both, far_rows))
    both_sibling = flip(both, 1)
    far, normed_far = call(
        project_far_kernel,
        (1,),
        after(project_place, query),
        wholes(*far_rows, gain1, shift1, w_key, w_value, b_key, b_value, cosine, sine),
        wholes(fresh((2, span, width), low), fresh((span, width), low)),
    )
    far_sibling = flip(far, 1)
    cot_first, cot_second, _ = lax.optimization_barrier((cot_first, cot_second, far))
    cot_first, cot_second = send(cot_first, 0), send(cot_second, 1)

    def columns(array, rows, at, size=PAIR, base=0):
        if len(array.shape) == 2:
            return (array, pl.BlockSpec((rows, size), lambda h, _: (at, base + h)))
        return (array, pl.BlockSpec((2, rows, size), lambda h, _: (0, at, base + h)))

    def own_pieces(*given):
        return [columns(both, 2 * span, 0, *given), columns(both_sibling, 2 * span, 0, *given)]

    def mixed_pieces(*given):
        return [
            columns(both, span, 2, *given),
            columns(both_sibling, span, 2, *given),
            columns(far, span, 0, *given),
            columns(far_sibling, span, 0, *given),
        ]

    def attend(place, rows, at, pieces):
        size = 2 * PAIR
        pieces = pieces(size)
        return call(
            functools.partial(attend_kernel, len(pieces)),
            (width // size,),
            place,
            [columns(query, rows, at, size), *pieces],
            [
                columns(fresh((rows, width), low), rows, 0, size),
                (
                    fresh((pairs, 8, rows), full),
                    pl.BlockSpec((2, 8, rows), lambda h, _: (h, 0, 0)),
                ),
            ],
            [pltpu.VMEM((count, size), low), pltpu.VMEM((count, size), low)],
                )

    own, own_logsum = attend(after(own_place, far), 2 * span, 0, own_pieces)
    mixed, mixed_logsum = attend(after(mixed_place, own), span, 2, mixed_pieces)

    def wide(array):
        return (array, pl.BlockSpec(square, lambda j, tiles: (0, tiles[j])))

    def tall(array):
        return (array, pl.BlockSpec(square, lambda j, tiles: (tiles[j], 0)))

    rows_fresh = fresh((8, width), full)

    def tiles_in():
        return [
            wide(w_up),
            (b_up, pl.BlockSpec((1, width), lambda j, tiles: (0, tiles[j]))),
            tall(w_down),
        ]

    def tile_outs():
        return [
            (
                fresh((2, 2, width, width), low),
                pl.BlockSpec((2, None, width, width), lambda j, _: (0, j, 0, 0)),
            ),
            (fresh((2, 8, width), full), pl.BlockSpec((None, 8, width), lambda j, _: (j, 0, 0))),
        ]

    tokens_full = fresh((tokens, width), full)
    tokens_low = fresh((tokens, width), low)
    tile_scratch = [pltpu.VMEM((tokens, width), low), pltpu.VMEM((tokens, width), low)]
    middle, result, grad_normed2, normed2, cot, tiles_sent, b_up_sent = call(
        first_tiles_kernel,
        (2,),
        tiles_first,
        wholes(
            own, mixed, first, second, cot_first, cot_second, w_out, b_out, gain2, shift2
        )
        + tiles_in(),
        wholes(tokens_full, tokens_full, tokens_full, tokens_low, tokens_low) + tile_outs(),
        tile_scratch,
    )
    tiles_received = flip(tiles_sent, 1)
    (
        tiles_kept, b_up_kept, result_first, result_second, grad_middle, grad_own, grad_mixed,
        out_kept, out_sent, rows_middle,
    ) = call(
        last_tiles_kernel,
        (2,),
        tiles_last,
        wholes(own, mixed, middle, result, grad_normed2, normed2, cot, w_out, gain2)
        + tiles_in()
        + wholes(b_down),
        tile_outs()
        + wholes(
            fresh((tokens // 2, width), low), fresh((tokens // 2, width), low), tokens_full,
            fresh((2 * span, width), low), fresh((span, width), low),
            fresh((1, width // 2, width), low), fresh((1, width // 2, width), low), rows_fresh,
        ),
        [pltpu.VMEM((tokens, width), full), pltpu.VMEM((tokens, width), full)]
        + tile_scratch
        + [pltpu.VMEM(square, low)],
    )
    result = [send_back(result_first, 0), send_back(result_second, 1)]
    out_received = flip(out_sent, 1)

    def split(addends, at):
        rows = addends[0].shape[1] // 2

        def part(which):
            items = [
                lax.dynamic_slice_in_dim(item, which * rows, rows, 1).astype(full)
                for item in addends
            ]
            return sum(items[1:], items[0]).astype(low)

        return part(at), part(1 - at)

    def added(addends):
        return (addends[0].astype(full) + addends[1].astype(full)).astype(low)

    def ordered(at, mine, theirs):
        return jnp.where(
            at == 0,
            jnp.concatenate([mine, theirs], axis=1),
            jnp.concatenate([theirs, mine], axis=1),
        )

    def stage(values, at, number, joined=False):
        lead, _, columns_in = values[0][0].shape
        sizes = [item[0].shape[1] for item in values]
        sizes = [sum(sizes)] if joined else sizes
        if any(size % 16 for size in sizes):
            if joined:
                values = [[jnp.concatenate([added(item) for item in values], axis=1)]]
            return [split(item, place) for item, place in zip(values, at)]
        parts = call(
            functools.partial(stage_kernel, joined),
            (1,),
            sides[number],
            wholes(*[part for item in values for part in item]),
            wholes(
                *[fresh((lead, size // 2, columns_in), low) for size in sizes for _ in range(2)]
            ),
            [pltpu.VMEM((lead, size, columns_in), full) for size in sizes],
            room=32,
        )
        return [tuple(parts[2 * place : 2 * place + 2]) for place in range(len(sizes))]

    def chain(parts, orders, early):
        for step in range(len(bits)):
            if step > 0:
                parts = stage(values, [bit_of(order[step]) for order in orders], step)
            values = yield [
                [keep, flip(give, order[step])] for (keep, give), order in zip(parts, orders)
            ]
        sizes = [item[0].shape[1] for item in values]
        ((keep, give),) = stage(values, [side], -2, joined=True)
        values = yield [[keep, flip_depth(give, 1)]]
        ((keep, give),) = stage(values, [pair], -1)
        (value,) = yield [[keep, flip_depth(give, 2)]]
        total = added(value)
        (value,) = yield [[total, flip_depth(total, 2)]]
        joined = ordered(pair, *value)
        (value,) = yield [[joined, flip_depth(joined, 1)]]
        joined = ordered(side, *value)
        ends = [sum(sizes[: place + 1]) for place in range(len(sizes))]
        values = [joined[:, end - size : end] for end, size in zip(ends, sizes)]
        for step in range(len(bits) - 1, 0, -1):
            values = yield [
                [item, flip(item, order[step])] for item, order in zip(values, orders)
            ]
            values = [
                ordered(bit_of(order[step]), *item) for item, order in zip(values, orders)
            ]
        values = yield [
            [item, flip(item, order[0])] + ([flip(item, 1)] if early else [])
            for item, order in zip(values, orders)
        ]
        values = yield [
            [*item, flip(item[1], 1)] if early else [*item, flip(item[0], 1), flip(item[1], 1)]
            for item in values
        ]
        yield values

    class Chain:
        def __init__(self, left, right, early):
            self.steps = chain([left, right], [bits, reverse], early)
            self.state = next(self.steps)
            self.left = 2 * len(bits) + 5

        def here(self):
            return [item[0] for item in self.state]

    def advance(chains, *gates):
        chains = [item for item in chains if item.left > 0]
        states = lax.optimization_barrier(([item.state for item in chains], gates))[0]
        for item, state in zip(chains, states):
            item.state = item.steps.send(state)
            item.left -= 1

    reverse = bits[::-1]

    part = fresh((1, width, width), low)
    parts = call(
        halve_kernel,
        (1,),
        orders,
        wholes(tiles_kept, tiles_received),
        wholes(part, part, part, part),
        room=40,
    )
    tile_sum = Chain(tuple(parts[:2]), tuple(parts[2:]), True)

    def attend_back(place, rows, at, pieces, grad, out, logsum, size, base, steps):
        given = pieces(size, base)
        group_pairs = size // PAIR
        return call(
            functools.partial(attend_back_kernel, len(given)),
            (steps,),
            place,
            [
                columns(query, rows, at, size, base),
                columns(grad, rows, 0, size, base),
                columns(out, rows, 0, size, base),
                (logsum, pl.BlockSpec((group_pairs, 8, rows), lambda h, _: (base + h, 0, 0))),
                whole(cosine),
                whole(sine),
                *given,
            ],
            [columns(fresh((rows, size * steps), low), rows, 0, size)]
            + [columns(fresh((2, rows, size * steps), low), rows, 0, size) for _ in given],
            [pltpu.VMEM((count, size), low)] * 4,
                )

    query_mixed, mixed_here_grad, mixed_sibling_grad, far_grad, far_sibling_grad = attend_back(
        after(mixed_place, *tile_sum.here()), span, 2, mixed_pieces, grad_mixed, mixed, mixed_logsum,
        2 * PAIR, 0, pairs // 2,
    )
    far_received = flip(far_sibling_grad, 1)
    mixed_received = flip(mixed_sibling_grad, 1)
    result = unpack(after(result[0], query_mixed), result[1], order_back, seqs)
    advance([tile_sum], query_mixed)
    far_both, grad_far = call(
        grad_far_kernel,
        (1,),
        after(core_only, result, *tile_sum.here()),
        wholes(far_grad, far_received, w_key, w_value),
        wholes(fresh((2, span, width), low), fresh((span, width), low)),
    )
    grad_far = cross(grad_far)

    query_own, own_kept, own_sent = attend_back(
        after(own_place, far_both), 2 * span, 0, own_pieces, grad_own, own, own_logsum, 2 * PAIR, 0,
        pairs // 2,
    )
    own_received = flip(own_sent, 1)
    advance([tile_sum], query_own)
    weight_kept, weight_sent, both_grad, rows_weight = call(
        weight_kernel,
        (1,),
        after(core_only, grad_far, *tile_sum.here()),
        wholes(
            normed, normed_far, query_own, query_mixed, own_kept, own_received, mixed_here_grad,
            mixed_received, far_both,
        ),
        wholes(
            fresh((3, width // 2, width), low), fresh((3, width // 2, width), low),
            fresh((2, tokens, width), low), rows_fresh,
        ),
        [pltpu.VMEM(square, low)],
    )
    weight_received = flip(weight_sent, 1)
    advance([tile_sum], rows_weight)
    weight_kept, weight_received, out_kept, out_received, _ = lax.optimization_barrier(
        (weight_kept, weight_received, out_kept, out_received, tile_sum.here())
    )
    part = fresh((4, width // 8, width), low)
    parts = call(
        quarter_kernel,
        (1,),
        orders,
        wholes(weight_kept, weight_received, out_kept, out_received),
        wholes(part, part, part, part),
        room=32,
    )
    weight_sum = Chain(tuple(parts[:2]), tuple(parts[2:]), False)
    back_first, back_second, rows_input = call(
        input_kernel,
        (1,),
        after(core_only, *tile_sum.here(), *weight_sum.here()),
        wholes(
            query_own, query_mixed, both_grad, grad_far, w_query, w_key, w_value, first, second,
            gain1, grad_middle,
        ),
        wholes(fresh((tokens // 2, width), low), fresh((tokens // 2, width), low), rows_fresh),
    )

    b_up_kept, b_up_sent, _ = lax.optimization_barrier((b_up_kept, b_up_sent, rows_input))
    b_up_kept, b_up_sent = b_up_kept[:, 0], b_up_sent[:, 0]
    rows_up = jnp.where(
        core == 0,
        jnp.concatenate([b_up_kept, b_up_sent]),
        jnp.concatenate([b_up_sent, b_up_kept]),
    )
    small = jnp.concatenate([rows_middle, rows_weight, rows_input, rows_up, counts], axis=0)

    class Small:
        def __init__(self):
            self.moves = [(flip, bit) for bit in (1, *bits)] + [(flip_depth, 1), (flip_depth, 2)]
            self.steps = self
            move, bit = self.moves.pop(0)
            self.state = [[small, move(small, bit)]]
            self.left = len(bits) + 3

        def send(self, state):
            total = state[0][0] + state[0][1]
            if not self.moves:
                return [[total]]
            move, bit = self.moves.pop(0)
            return [[total, move(total, bit)]]
    advance([tile_sum, weight_sum], rows_input)
    small_sum = Small()
    while tile_sum.left > 2:
        advance([weight_sum, small_sum, tile_sum])
    advance([weight_sum, small_sum])
    back_first, back_second, _ = lax.optimization_barrier(
        (back_first, back_second, weight_sum.here())
    )
    back = [send_back(back_first, 0), send_back(back_second, 1)]
    while tile_sum.left > 0:
        advance([weight_sum, small_sum, tile_sum])
    left, right = tile_sum.state
    gate = weight_sum.here()

    def expand(sources, place, shape, target):
        return call(
            functools.partial(expand_kernel, place),
            (4,),
            after(orders, *gate),
            wholes(*sources),
            [(fresh(shape, full), pl.BlockSpec(square, target))],
            room=32,
        )[0]

    grad_w_down = expand(left, 1, (hidden_width, width), lambda i, _: (i, 0))
    grad_w_up = expand(right, 2, (width, hidden_width), lambda i, _: (0, i))
    while small_sum.left > 0:
        advance([small_sum])
    total = small_sum.state[0][0]
    small = [total[at] for at in range(4)] + [total[24:28].reshape(-1)]
    small += [total[at] for at in (8, 9, 10, 16, 17)]
    small.append(total[28, :CLASSES].astype(jnp.int32))
    small = lax.optimization_barrier(small)
    gates = [grad_w_down, grad_w_up, *small]
    while weight_sum.left > 0:
        advance([weight_sum], *gates)
        gates = []
    grad_inputs = unpack(back[0], back[1], order_back, seqs)
    left, right = weight_sum.state
    grad_w_query, grad_w_key, grad_w_value, grad_w_out = call(
        expand_mixed_kernel,
        (8,),
        orders,
        wholes(*left, *right),
        [(fresh(square, full), pl.BlockSpec((width // 8, width), lambda i, _: (i, 0)))] * 4,
        room=32,
    )
    return (
        result,
        grad_inputs,
        small[8],
        small[9],
        grad_w_query,
        small[5],
        grad_w_key,
        small[6],
        grad_w_value,
        small[7],
        grad_w_out,
        small[1],
        small[2],
        small[3],
        grad_w_up,
        small[4],
        grad_w_down,
        small[0],
        small[10],
    )


def solution(mesh):
    tokens = P("dp", "seq", None)
    return jax.shard_map(
        on_device,
        mesh=mesh,
        in_specs=(tokens, tokens, P("dp"), P("dp", "seq")) + (P(),) * 16,
        out_specs=(tokens, tokens) + (P(),) * 17,
        check_vma=False,
    )
```
